32 devices in a mesh: tm: 4 (over y, x), region: 8 (over z, core).
Axes of the slice: x: 2, y: 2, z: 4, core: 2. Of those that a mesh axis runs over, the one named last changes fastest.
Arguments:
- gen: float32 [8, 128, 4, 128], P('region', None, 'tm'), may hold values from 0 to 1
- flow: float32 [32, 128, 4, 128], P('region', None, 'tm'), may hold values from -4 to 4
- price: float32 [32, 128, 4, 128], P('region', None, 'tm'), may hold values from -6 to 6
- ramp_dual: float32 [8, 128, 4, 128], P('region', None, 'tm'), may hold values from -3 to 3
- demand: float32 [32, 128, 4, 128], P('region', None, 'tm'), may hold values from -6 to 6
- incid_tiles: bfloat16 [256, 128, 128], P('region'), may hold values from -0.1875 to 0.1875
- tile_bus: int32 [256], P('region'), may hold values from 0 to 3
- tile_line: int32 [256], P('region'), may hold values from 0 to 31, as said below
- gen_tiles: bfloat16 [8, 128, 128], P('region'), may hold values from -0.5 to 0.5
- gen_bus: int32 [8], P('region'), may hold values from 0 to 3
- gen_cost: float32 [8, 128], P('region'), may hold values from 0.1 to 1
- gen_cap: float32 [8, 128], P('region'), may hold values from 0.5 to 2
- ramp_cap: float32 [8, 128], P('region'), may hold values from 0.05 to 0.5
- flow_cap: float32 [32, 128], P('region'), may hold values from 0.3 to 1.5
- weight: float32 [], replicated, may hold values from 0.5 to 2
Outputs:
- gen_next: float32 [8, 128, 4, 128], P('region', None, 'tm')
- flow_next: float32 [32, 128, 4, 128], P('region', None, 'tm')
- price_next: float32 [32, 128, 4, 128], P('region', None, 'tm')
- ramp_next: float32 [8, 128, 4, 128], P('region', None, 'tm')
The draws below stay inside these ranges and needn't reach their ends.
Inputs may be any that keep to these rules, and one draw needn't show every extreme that they name: Tile t belongs to region r = t // 32; its line block lies in region r - 1, r or r + 1 (those that exist), where region q holds line blocks q * 4 to (q + 1) * 4 - 1. No two tiles have the same pair (tile_bus, tile_line) within a region.
All inputs are finite; a program needn't handle non-finite values.
Results may differ from the reference program's by a relative error of at most 0.0006.
The reference program's roundings to bfloat16 on the way (of `price_low`) count: a program that leaves them out, or rounds other values in their place, can miss the bound.
Values may be sent and summed in bfloat16 or wider, within the bound.
A program may use at most 64 MiB of HBM per device.

```python
import math
import jax
import jax.numpy as jnp
from jax import lax

BLK = 128
S = 128
BUS_BLK_DEV = 4
LINE_BLK_DEV = 4
GEN_BLK_DEV = 1
TILE_DEV = 32
HOURS = 4
BUS_BLKS = 32
LINE_BLKS = 32
GEN_BLKS = 8
TILES = 256


def tile_positions(key):
    regions = LINE_BLKS // LINE_BLK_DEV
    slots = BUS_BLK_DEV * 3 * LINE_BLK_DEV
    base = jax.random.fold_in(key, 7)
    region_keys = jax.random.split(base, regions)
    perms = jax.vmap(lambda one: jax.random.permutation(one, slots))(region_keys).astype(jnp.int32)
    window = perms // BUS_BLK_DEV
    buses = perms % BUS_BLK_DEV
    region = jnp.arange(regions, dtype=jnp.int32)[:, None]
    lines = (region - 1) * LINE_BLK_DEV + window
    valid = (lines >= 0) & (lines < LINE_BLKS)
    order_key = jnp.where(valid, 0, slots).astype(jnp.int32) + jnp.arange(slots, dtype=jnp.int32)[None, :]
    order = jnp.argsort(order_key, axis=1)[:, :TILE_DEV]
    chosen_lines = jnp.take_along_axis(lines, order, axis=1)
    chosen_buses = jnp.take_along_axis(buses, order, axis=1)
    return (chosen_buses.reshape(-1).astype(jnp.int32), chosen_lines.reshape(-1).astype(jnp.int32))


def draw_tile_bus(key, part):
    buses, lines = tile_positions(key)
    return buses


def draw_tile_line(key, part):
    buses, lines = tile_positions(key)
    return lines


def set_ends(result, stream_key, low, high):
    spot = [jax.random.randint(jax.random.fold_in(stream_key, axis), (), 0, length) for axis, length in enumerate(result.shape)]
    main_axis = result.shape.index(max(result.shape))
    next_to = spot[:main_axis] + [(spot[main_axis] + 1) % result.shape[main_axis]] + spot[main_axis + 1:]
    return result.at[tuple(spot)].set(low).at[tuple(next_to)].set(high)


def steps_of(stream_key, dims, pieces, smallest, top_value):
    level, own = 1.0, jax.random.fold_in(stream_key, 6)
    for axis_at, blocks in pieces:
        steps = jnp.exp(jax.random.uniform(jax.random.fold_in(own, axis_at), (blocks,), jnp.float32, smallest / len(pieces), top_value / len(pieces)))
        level = level * jnp.repeat(steps, dims[axis_at] // blocks).reshape([-1 if axis == axis_at else 1 for axis in range(len(dims))])
    return level


def noise(rng, extent, scale, most, pieces=(), held_as=jnp.bfloat16):
    values = jax.random.normal(rng, extent, jnp.float32) * scale
    if len(pieces) > 0:
        values = steps_of(rng, extent, pieces, -0.22, 0.18) * values
    return jnp.clip(values, min=-most, max=most).astype(held_as)


def setup_inputs(seed: int = 0) -> dict:
    key_list = jax.random.split(jax.random.key(seed), 16)
    return {
        "gen": jnp.clip(1.0 * jax.random.uniform(key_list[0], (GEN_BLKS, BLK, HOURS, S), jnp.float32) ** steps_of(key_list[0], (GEN_BLKS, BLK, HOURS, S), ((0, 8), (2, 4)), -0.2, 0.2), 0.0, 1.0),
        "flow": noise(key_list[1], (LINE_BLKS, BLK, HOURS, S), 0.5, 4.0, ((0, 8), (2, 4)), jnp.float32),
        "price": noise(key_list[2], (BUS_BLKS, BLK, HOURS, S), 1.0, 6.0, ((0, 8), (2, 4)), jnp.float32),
        "ramp_dual": noise(key_list[3], (GEN_BLKS, BLK, HOURS, S), 0.3, 3.0, ((0, 8), (2, 4)), jnp.float32),
        "demand": noise(key_list[4], (BUS_BLKS, BLK, HOURS, S), 1.0, 6.0, ((0, 8), (2, 4)), jnp.float32),
        "incid_tiles": noise(key_list[5], (TILES, BLK, BLK), (TILE_DEV // BUS_BLK_DEV * BLK + BLK) ** -0.5, 0.1875, ((0, 8),)),
        "tile_bus": draw_tile_bus(jax.random.fold_in(key_list[15], 71), 0),
        "tile_line": draw_tile_line(jax.random.fold_in(key_list[15], 71), 0),
        "gen_tiles": noise(key_list[8], (GEN_BLKS, BLK, BLK), BLK ** -0.5, 0.5, ((0, 8),)),
        "gen_bus": set_ends(jax.random.randint(key_list[9], (GEN_BLKS,), 0, BUS_BLK_DEV), jax.random.fold_in(key_list[9], 1), 0, BUS_BLK_DEV - 1).astype(jnp.int32),
        "gen_cost": jnp.clip(jnp.exp(math.log(1.0) - 2.3025851 * jax.random.uniform(key_list[10], (GEN_BLKS, BLK), jnp.float32) ** steps_of(key_list[10], (GEN_BLKS, BLK), ((0, 8),), -0.2, 0.2)), 0.1, 1.0),
        "gen_cap": jnp.clip(0.5 + 1.5 * jax.random.uniform(key_list[11], (GEN_BLKS, BLK), jnp.float32) ** steps_of(key_list[11], (GEN_BLKS, BLK), ((0, 8),), -0.2, 0.2), 0.5, 2.0),
        "ramp_cap": jnp.clip(jnp.exp(math.log(0.5) - 2.3025851 * jax.random.uniform(key_list[12], (GEN_BLKS, BLK), jnp.float32) ** steps_of(key_list[12], (GEN_BLKS, BLK), ((0, 8),), -0.2, 0.2)), 0.05, 0.5),
        "flow_cap": jnp.clip(0.3 + 1.2 * jax.random.uniform(key_list[13], (LINE_BLKS, BLK), jnp.float32) ** steps_of(key_list[13], (LINE_BLKS, BLK), ((0, 8),), -0.2, 0.2), 0.3, 1.5),
        "weight": jnp.clip(jnp.exp(jax.random.uniform(key_list[14], (), jnp.float32, math.log(0.5), math.log(2.0))), 0.5, 2.0),
    }


step_scale = 0.4
tiny = 1e-06

def push_buses(flow_low, gen_low, incid_tiles, tile_bus, tile_line, gen_tiles, gen_bus):
    regions = LINE_BLKS // LINE_BLK_DEV
    columns = HOURS * S
    flow_cols = flow_low.reshape(LINE_BLKS, BLK, columns)
    tiles_by = incid_tiles.reshape(regions, TILE_DEV, BLK, BLK)
    lines_by = tile_line.reshape(regions, TILE_DEV)
    buses_by = tile_bus.reshape(regions, TILE_DEV)

    def per_region(packed):
        tiles_here, lines_here, buses_here = packed
        picked = flow_cols[lines_here].astype(jnp.float32)
        contrib = jnp.einsum('tij,tjc->tic', tiles_here.astype(jnp.float32), picked)
        return jax.ops.segment_sum(contrib, buses_here, num_segments=BUS_BLK_DEV)
    bus_sum = lax.map(per_region, (tiles_by, lines_by, buses_by)).reshape(BUS_BLKS, BLK, columns)
    gen_cols = gen_low.reshape(GEN_BLKS, BLK, columns).astype(jnp.float32)
    gen_contrib = jnp.einsum('gij,gjc->gic', gen_tiles.astype(jnp.float32), gen_cols)
    target = jnp.arange(GEN_BLKS, dtype=jnp.int32) // GEN_BLK_DEV * BUS_BLK_DEV + gen_bus
    bus_sum = bus_sum.at[target].add(gen_contrib)
    return bus_sum.reshape(BUS_BLKS, BLK, HOURS, S)

def pull_lines(price_low, incid_tiles, tile_bus, tile_line, gen_tiles, gen_bus):
    regions = LINE_BLKS // LINE_BLK_DEV
    columns = HOURS * S
    price_cols = price_low.reshape(BUS_BLKS, BLK, columns)
    tiles_by = incid_tiles.reshape(regions, TILE_DEV, BLK, BLK)
    lines_by = tile_line.reshape(regions, TILE_DEV)
    buses_by = tile_bus.reshape(regions, TILE_DEV)

    def per_region(total, packed):
        tiles_here, lines_here, buses_here, region = packed
        picked = price_cols[region * BUS_BLK_DEV + buses_here].astype(jnp.float32)
        contrib = jnp.einsum('tji,tjc->tic', tiles_here.astype(jnp.float32), picked)
        return (total.at[lines_here].add(contrib), None)
    start = jnp.zeros((LINE_BLKS, BLK, columns), jnp.float32)
    region_ids = jnp.arange(regions, dtype=jnp.int32)
    total, unused = lax.scan(per_region, start, (tiles_by, lines_by, buses_by, region_ids))
    target = jnp.arange(GEN_BLKS, dtype=jnp.int32) // GEN_BLK_DEV * BUS_BLK_DEV + gen_bus
    gen_picked = price_cols[target].astype(jnp.float32)
    gen_pull = jnp.einsum('gji,gjc->gic', gen_tiles.astype(jnp.float32), gen_picked)
    return (total.reshape(LINE_BLKS, BLK, HOURS, S), gen_pull.reshape(GEN_BLKS, BLK, HOURS, S))

def iterate(state, primal_weight, fixed):
    gen, flow, price, ramp_dual = state
    demand, incid_tiles, tile_bus, tile_line, gen_tiles, gen_bus, gen_cost, gen_cap, ramp_cap, flow_cap = fixed
    step_primal = step_scale / primal_weight
    step_dual = step_scale * primal_weight
    price_low = price.astype(jnp.bfloat16)
    pull_f, pull_g = pull_lines(price_low, incid_tiles, tile_bus, tile_line, gen_tiles, gen_bus)
    back = ramp_dual - jnp.roll(ramp_dual, -1, axis=2)
    grad_gen = gen_cost[:, :, None, None] - pull_g + back
    gen_new = jnp.clip(gen - step_primal * grad_gen, 0.0, gen_cap[:, :, None, None])
    limit = flow_cap[:, :, None, None]
    flow_new = jnp.clip(flow + step_primal * pull_f, -limit, limit)
    gen_bar = 2.0 * gen_new - gen
    flow_bar = 2.0 * flow_new - flow
    pushed = push_buses(flow_bar.astype(jnp.bfloat16), gen_bar.astype(jnp.bfloat16), incid_tiles, tile_bus, tile_line, gen_tiles, gen_bus)
    price_new = price + step_dual * (demand - pushed)
    ramping = gen_bar - jnp.roll(gen_bar, 1, axis=2)
    lifted = ramp_dual + step_dual * ramping
    bound = ramp_cap[:, :, None, None]
    ramp_new = lifted - step_dual * jnp.clip(lifted / step_dual, -bound, bound)
    return (gen_new, flow_new, price_new, ramp_new)

def reference(gen, flow, price, ramp_dual, demand, incid_tiles, tile_bus, tile_line, gen_tiles, gen_bus, gen_cost, gen_cap, ramp_cap, flow_cap, weight):
    fixed = (demand, incid_tiles, tile_bus, tile_line, gen_tiles, gen_bus, gen_cost, gen_cap, ramp_cap, flow_cap)
    first = iterate((gen, flow, price, ramp_dual), weight, fixed)
    primal_sq = jnp.sum((first[0] - gen) ** 2) + jnp.sum((first[1] - flow) ** 2)
    dual_sq = jnp.sum((first[2] - price) ** 2) + jnp.sum((first[3] - ramp_dual) ** 2)
    primal_mean = primal_sq / (gen.size + flow.size)
    dual_mean = dual_sq / (price.size + ramp_dual.size)
    weight_two = jnp.sqrt(weight * jnp.sqrt((dual_mean + tiny) / (primal_mean + tiny)))
    second = iterate(first, weight_two, fixed)
    return (second[0], second[1], second[2], second[3])
```

```python
import functools

import jax
import jax.numpy as jnp
from jax import lax
from jax.experimental import pallas as pl
from jax.experimental.pallas import tpu as pltpu
from jax.sharding import PartitionSpec as P

MESH = pl.DeviceIdType.MESH
step_scale = 0.4
tiny = 1e-06
f32 = jnp.float32
bf16 = jnp.bfloat16


def remote(src, dst, send_sem, recv_sem, axis, peer):
    return pltpu.make_async_remote_copy(
        src_ref=src,
        dst_ref=dst,
        send_sem=send_sem,
        recv_sem=recv_sem,
        device_id={axis: peer},
        device_id_type=MESH,
    )


def fold(x):
    rows, columns = x.shape
    y = jnp.sum(x.reshape(rows // 8, 8, columns), axis=0)
    out = y[:, :128]
    for at in range(128, columns, 128):
        out = out + y[:, at : at + 128]
    return out


def both_halves(x):
    row = jnp.sum(x, axis=0, keepdims=True)
    return row + pltpu.roll(row, 64, 1)


def writer(*refs):
    n = (len(refs) - 1) // 2
    copies = [pltpu.make_async_copy(refs[i], refs[n + i], refs[-1].at[i]) for i in range(n)]
    for c in copies:
        c.start()
    for c in copies:
        c.wait()


def flip(x, mask):
    bit = 1
    out = x
    while bit <= mask:
        if mask & bit:
            out = out + bit * (1 - 2 * lax.rem(x // bit, 2))
        bit *= 2
    return out


def partners(x, n):
    if n & (n - 1) == 0:
        return [(m, flip(x, m)) for m in range(n - 1, 0, -1)]
    return [(m, lax.rem(x + m, n)) for m in range(1, n)]


FAR, NEAR = 0, 1


def kernel(
    dims,
    gen_bus, weight, tile_bus, tile_line, tiles, gtiles, price, flow, gen, ramp, demand, cost, gcap, rcap, fcap,
    o_gen, o_flow, o_price, o_ramp,
    tiles_v, a_v, price_v, ramp_v, late_v, caps_v, fcap_v,
    pt_v, own_v, price1_v, flow_s, gen_s, dual_s, genlow_v,
    part_send, part_recv, fw_own, fw_in, d_send, d_recv, v_send, v_recv, prev_v,
    ar_s, ar_r, acc_v, change_v, idx_v, table_v, table_s,
    in_sem, ps_sem, pr_sem, fs_sem, fr_sem, tm_sem, ar_sem, ready, table_sem,
):
    nt, nr, scen, count_p, count_d = dims
    t = lax.axis_index("tm")
    r = lax.axis_index("region")
    n_tiles, blk, _ = tiles.shape
    n_gens = gtiles.shape[0]
    lines, cols = flow.shape
    buses = price.shape[0]
    lb, bb = lines // blk, buses // blk
    width = 3 * lb + n_gens
    gens = gen.shape[0]
    nch = part_send.shape[2]
    cw = lines // nch
    n_stages = ready.shape[0]

    odd = lax.rem(r, 2)
    place = (r - 1 + 2 * odd, r + 1 - 2 * odd)
    has = tuple((p >= 0) & (p < nr) for p in place)
    peer = tuple(jnp.clip(p, 0, nr - 1) for p in place)
    count = tuple(jnp.where(h, 1, 0) for h in has)
    first_window = (2 * lb * odd, 2 * lb * (1 - odd), lb)

    barrier = pltpu.get_barrier_semaphore()
    for side in (FAR, NEAR):
        @pl.when(has[side])
        def _():
            pl.semaphore_signal(
                barrier, inc=1, device_id={"region": peer[side]}, device_id_type=MESH
            )
    for k in range(1, nt):
        pl.semaphore_signal(
            barrier, inc=1, device_id={"tm": lax.rem(t + k, nt)}, device_id_type=MESH
        )

    def stage_signal(stage):
        step = 2**stage
        for to in (r - step, r + step):
            @pl.when((to >= 0) & (to < nr))
            def _():
                pl.semaphore_signal(
                    ready.at[stage], inc=1, device_id={"region": jnp.clip(to, 0, nr - 1)},
                    device_id_type=MESH,
                )

    def stage_wait(stage):
        step = 2**stage
        pl.semaphore_wait(
            ready.at[stage], jnp.where(r >= step, 1, 0) + jnp.where(r + step < nr, 1, 0)
        )

    def pass_on(stage):
        if stage < n_stages - 1:
            stage_wait(stage)
            stage_signal(stage + 1)

    def load(i, *pairs):
        copies = [pltpu.make_async_copy(src, dst, in_sem.at[i]) for src, dst in pairs]
        for c in copies:
            c.start()

    def arrived(i, ref):
        pltpu.make_async_copy(ref, ref, in_sem.at[i]).wait()

    load(0, (tile_bus, idx_v.at[0]), (tile_line, idx_v.at[1]))
    all_tiles = tiles_v.at[pl.ds(0, n_tiles + n_gens)]
    load(1, (price, price_v))
    load(2, (ramp, ramp_v))
    load(3, (tiles, tiles_v.at[pl.ds(0, n_tiles)]), (gtiles, tiles_v.at[pl.ds(n_tiles, n_gens)]))
    flow_v = late_v.at[pl.ds(0, lines)]
    demand_v = late_v.at[pl.ds(lines, buses)]
    gen_v = late_v.at[pl.ds(lines + buses, gens)]

    def late_loads():
        load(4, (flow, flow_v), (demand, demand_v), (gen, gen_v))
        load(5, (cost, caps_v.at[0]), (gcap, caps_v.at[1]), (rcap, caps_v.at[2]))
        load(6, (fcap, fcap_v))

    tiles_v[n_tiles + n_gens] = jnp.zeros((blk, blk), bf16)

    for side in (FAR, NEAR):
        @pl.when(jnp.logical_not(has[side]))
        def _():
            part_recv[:, side] = jnp.zeros_like(part_recv[:, side])
            fw_in[:, side] = jnp.zeros_like(fw_in[:, side])

    t_next, t_prev = lax.rem(t + 1, nt), lax.rem(t + nt - 1, nt)

    def far_part(it, ch):
        return remote(
            part_send.at[it, FAR, ch], part_recv.at[it, FAR, ch],
            ps_sem.at[FAR], pr_sem.at[ch], "region", peer[FAR],
        )

    def near_part(it):
        return remote(
            part_send.at[it, NEAR], part_recv.at[it, NEAR],
            ps_sem.at[NEAR], pr_sem.at[nch], "region", peer[NEAR],
        )

    def far_flow(it, ch):
        return remote(
            fw_own.at[it, ch], fw_in.at[it, FAR, ch],
            fs_sem.at[FAR], fr_sem.at[ch], "region", peer[FAR],
        )

    def near_flow(it):
        return remote(
            fw_own.at[it], fw_in.at[it, NEAR],
            fs_sem.at[NEAR], fr_sem.at[nch], "region", peer[NEAR],
        )

    def dual_copy(it):
        return remote(d_send.at[it], d_recv.at[it], tm_sem.at[0], tm_sem.at[2 + it], "tm", t_prev)

    def prev_copy(it):
        parts = pl.ds(0, 2 - it)
        return remote(
            v_send.at[it, parts], v_recv.at[it, parts], tm_sem.at[1], tm_sem.at[4 + it], "tm", t_next
        )

    def sent(it):
        for side in (FAR, NEAR):
            @pl.when(has[side])
            def _():
                ref = part_send.at[it, side]
                pltpu.make_async_copy(ref, ref, ps_sem.at[side]).wait()
                ref = fw_own.at[it]
                pltpu.make_async_copy(ref, ref, fs_sem.at[side]).wait()

    at_near, at_own, at_gens = lines, 2 * lines, 3 * lines

    def build(group):
        n = n_gens if group == 3 else lb
        for i in range(n):
            window = 3 * lb + i if group == 3 else first_window[group] + i
            lo = group * lines + i * blk
            for b in range(bb):
                a_v[b * blk : (b + 1) * blk, lo : lo + blk] = tiles_v[table_s[0, b * width + window]]

    per_dot = 2 if nch % 2 == 0 else 1

    def far_sums(it, ch):
        sums = jnp.dot(
            pt_v[...], a_v[:, ch * cw : (ch + per_dot) * cw], preferred_element_type=f32
        )
        for i in range(per_dot):
            part_send[it, FAR, ch + i] = sums[:, i * cw : (i + 1) * cw]

    def send_far(it, ch):
        @pl.when(has[FAR])
        def _():
            for i in range(per_dot):
                far_part(it, ch + i).start()

    def pull_near(it):
        for ch in range(0, nch, per_dot):
            at = at_near + ch * cw
            sums = jnp.dot(
                pt_v[...], a_v[:, at : at + per_dot * cw], preferred_element_type=f32
            )
            for i in range(per_dot):
                part_send[it, NEAR, ch + i] = sums[:, i * cw : (i + 1) * cw]

        @pl.when(has[NEAR])
        def _():
            near_part(it).start()

    def pull_gens():
        own_v[:, lines:] = jnp.dot(pt_v[...], a_v[:, at_gens:], preferred_element_type=f32)

    def pull_own():
        own_v[:, :lines] = jnp.dot(
            pt_v[...], a_v[:, at_own:at_gens], preferred_element_type=f32
        )

    def set_pt(ref):
        for b in range(bb):
            pt_v[:, b * blk : (b + 1) * blk] = ref[b * blk : (b + 1) * blk, :].astype(bf16).T

    def row(ref, n):
        return jnp.concatenate([ref[i : i + 1, :] for i in range(n)], axis=1) if n > 1 else ref[...]

    def gen_pull(it):
        grad = row(caps_v.at[0], n_gens) - own_v[:, lines:] + dual_s[it]
        own_v[:, lines:] = grad
        v_send[it, 0] = grad[cols - scen :]
        if it == 0:
            v_send[it, 1] = gen_s[it][cols - scen :]
        prev_copy(it).start()

    def clipped(now, sp, grad):
        return jnp.minimum(jnp.maximum(now - sp * grad, 0.0), row(caps_v.at[1], n_gens))

    def gen_step(it, sp):
        dual_copy(it).wait_recv()
        nxt = d_recv[it]
        later = nxt if cols == scen else jnp.concatenate([dual_s[it][scen:], nxt], axis=0)
        gnow = gen_s[it]
        gnew = clipped(gnow, sp, own_v[:, lines:] - later)
        gbar = 2.0 * gnew - gnow
        gen_s[it + 1] = gnew
        genlow_v[...] = gbar.astype(bf16)
        return (gnew - gnow) ** 2, gbar

    def prev_bar(it, sp):
        now = v_recv[it, 1] if it == 0 else prev_v[...]
        new = clipped(now, sp, v_recv[it, 0] - dual_s[it][:scen])
        prev_v[...] = new
        return 2.0 * new - now

    def near_arrived(it):
        @pl.when(has[NEAR])
        def _():
            near_part(it).wait_recv()

    def total_at(it, ch):
        @pl.when(has[FAR])
        def _():
            far_part(it, ch).wait_recv()

        lo = ch * cw
        return own_v[:, lo : lo + cw] + part_recv[it, NEAR, ch] + part_recv[it, FAR, ch]

    per = cw // blk

    def flow_step(it, ch, sp, total):
        lo = ch * cw
        cap = jnp.concatenate(
            [fcap_v[ch * per + i : ch * per + i + 1, :] for i in range(per)], axis=1
        )
        now = flow_s[it, :, lo : lo + cw]
        new = jnp.minimum(jnp.maximum(now + sp * total, -cap), cap)
        fw_own[it, ch] = (2.0 * new - now).astype(bf16)

        @pl.when(has[FAR])
        def _():
            far_flow(it, ch).start()

        flow_s[it + 1, :, lo : lo + cw] = new
        return (new - now) ** 2

    def send_near(it):
        @pl.when(has[NEAR])
        def _():
            near_flow(it).start()

    nt_dims = (((1,), (1,)), ((), ()))

    def joined(get, n):
        return jnp.concatenate([get(ch) for ch in range(n)], axis=1) if n > 1 else get(0)

    def push_own(it):
        mine = jnp.concatenate([fw_own[it, ch] for ch in range(nch)] + [genlow_v[...]], axis=1)
        acc_v[...] = lax.dot_general(a_v[:, at_own:], mine, nt_dims, preferred_element_type=f32)

    def push_near(it):
        @pl.when(has[NEAR])
        def _():
            near_flow(it).wait_recv()

        other = joined(lambda ch: fw_in[it, NEAR, ch], nch)
        acc_v[...] += lax.dot_general(
            a_v[:, at_near:at_own], other, nt_dims, preferred_element_type=f32
        )

    half = nch // 2

    def push_far(it, first, count):
        for ch in range(first, first + count):
            far_flow(it, ch).wait_recv()
        other = joined(lambda ch: fw_in[it, FAR, first + ch], count)
        return lax.dot_general(
            a_v[:, first * cw : (first + count) * cw], other, nt_dims, preferred_element_type=f32
        )

    def push(it, meanwhile, finish):
        push_own(it)
        if half > 0:
            @pl.when(has[FAR])
            def _():
                acc_v[...] += push_far(it, 0, half)

        push_near(it)
        meanwhile()

        @pl.when(has[FAR])
        def _():
            finish(acc_v[...] + push_far(it, half, nch - half))

        @pl.when(jnp.logical_not(has[FAR]))
        def _():
            finish(acc_v[...])

    def ramp_step(it, gbar, prev, sd):
        earlier = prev if cols == scen else jnp.concatenate([prev, gbar[: cols - scen]], axis=0)
        dual = dual_s[it]
        lifted = dual + sd * (gbar - earlier)
        bound = row(caps_v.at[2], n_gens)
        return lifted - sd * jnp.minimum(jnp.maximum(lifted / sd, -bound), bound)

    zero_at = n_tiles + n_gens
    arrived(0, idx_v)
    slot = idx_v[0] * width + (idx_v[1] - (r - 1) * lb)
    down = lax.broadcasted_iota(jnp.int32, (n_tiles, n_tiles), 0)
    across = lax.broadcasted_iota(jnp.int32, (n_tiles, n_tiles), 1)
    upright = jnp.sum(jnp.where(down == across, slot, 0), axis=1, keepdims=True)
    places = lax.broadcasted_iota(jnp.int32, (n_tiles, 128), 1)
    ids = lax.broadcasted_iota(jnp.int32, (n_tiles, 128), 0)
    found = jnp.sum(jnp.where(upright == places, ids - zero_at, 0), axis=0, keepdims=True)
    lane = lax.broadcasted_iota(jnp.int32, (1, 128), 1)
    for g in range(n_gens):
        found = jnp.where(lane == gen_bus[g] * width + 3 * lb + g, n_tiles + g - zero_at, found)
    table_v[...] = jnp.clip(zero_at + found, 0, zero_at)
    to_scalar = pltpu.make_async_copy(table_v, table_s, table_sem.at[0])
    to_scalar.start()

    w1 = jnp.full((1, 1), weight[...], f32)
    arrived(1, price_v)
    set_pt(price_v)
    arrived(2, ramp_v)
    dual_s[0] = ramp_v[...].T
    d_send[0] = dual_s[0][:scen]
    arrived(3, all_tiles)
    to_scalar.wait()
    build(FAR)
    pl.semaphore_wait(barrier, nt - 1 + count[FAR] + count[NEAR])
    if n_stages > 0:
        stage_signal(0)
    dual_copy(0).start()
    for ch in range(0, nch, per_dot):
        far_sums(0, ch)
        send_far(0, ch)
    late_loads()
    build(NEAR)
    pull_near(0)
    build(3)
    pull_gens()
    arrived(4, late_v)
    arrived(5, caps_v)
    gen_s[0] = gen_v[...].T
    gen_pull(0)
    pass_on(0)
    build(2)
    pull_own()
    sd1 = step_scale * w1
    sp1 = step_scale / w1
    for b in range(lb):
        flow_s[0, :, b * blk : (b + 1) * blk] = flow_v[b * blk : (b + 1) * blk, :].T
    arrived(6, fcap_v)
    near_arrived(0)
    primal_acc = jnp.zeros((8, 128), f32)
    for ch in range(nch):
        primal_acc = primal_acc + fold(flow_step(0, ch, sp1, total_at(0, ch)))
        if ch == 0:
            pass_on(1)
    send_near(0)
    for stage in range(2, n_stages - 1):
        pass_on(stage)
    changed, gbar1 = gen_step(0, sp1)
    primal_acc = primal_acc + fold(changed)
    low = lax.broadcasted_iota(jnp.int32, (1, 128), 1) < 64
    primal_row = both_halves(primal_acc)

    def ramp_now():
        prev_copy(0).wait_recv()
        dual_one = ramp_step(0, gbar1, prev_bar(0, sp1), sd1)
        dual_s[1] = dual_one
        change_v[...] = fold((dual_one - dual_s[0]) ** 2)
        dual_copy(0).wait_send()
        d_send[1] = dual_one[:scen]
        dual_copy(1).start()

    def price_now(pushed):
        new = price_v[...] + sd1 * (demand_v[...] - pushed)
        price1_v[...] = new
        dual_row = both_halves(change_v[...] + fold((new - price_v[...]) ** 2))
        ar_s[...] = jnp.where(low, primal_row, dual_row)
        new_low = new.astype(bf16)
        for b in range(bb):
            pt_v[:, b * blk : (b + 1) * blk] = new_low[b * blk : (b + 1) * blk, :].T
        far_sums(1, 0)

    push(0, ramp_now, price_now)

    if n_stages > 0:
        stage_wait(n_stages - 1)
    sent(0)
    others_t = partners(t, nt) + [(0, t)]
    others_r = partners(r, nr) + [(0, r)]
    for k, to_r in others_r:
        for j, to_t in others_t:
            if j or k:
                pltpu.make_async_remote_copy(
                    src_ref=ar_s,
                    dst_ref=ar_r.at[j * nr + k],
                    send_sem=ar_sem.at[0],
                    recv_sem=ar_sem.at[1],
                    device_id={"tm": to_t, "region": to_r},
                    device_id_type=MESH,
                ).start()
    others = ar_r.at[pl.ds(1, nt * nr - 1)]
    send_far(1, 0)
    for ch in range(per_dot, nch, per_dot):
        far_sums(1, ch)
        send_far(1, ch)
    pull_near(1)
    pull_gens()
    prev_copy(0).wait_send()
    gen_pull(1)
    pull_own()
    near_arrived(1)
    pltpu.make_async_copy(others, others, ar_sem.at[1]).wait()
    summed = ar_s[...]
    for at in range(1, nt * nr):
        summed = summed + ar_r[at]
    primal_mean = jnp.sum(jnp.where(low, summed, 0.0), axis=1, keepdims=True) / count_p
    dual_mean = jnp.sum(jnp.where(low, 0.0, summed), axis=1, keepdims=True) / count_d
    w2 = jnp.sqrt(w1 * jnp.sqrt((dual_mean + tiny) / (primal_mean + tiny)))

    sd2 = step_scale * w2
    sp2 = step_scale / w2
    for ch in range(nch):
        flow_step(1, ch, sp2, total_at(1, ch))
    send_near(1)
    _, gbar2 = gen_step(1, sp2)

    def results():
        prev_copy(1).wait_recv()
        o_ramp[...] = ramp_step(1, gbar2, prev_bar(1, sp2), sd2).T
        for b in range(lb):
            o_flow[b * blk : (b + 1) * blk, :] = flow_s[2, :, b * blk : (b + 1) * blk].T
        o_gen[...] = gen_s[2].T

    def price_out(pushed):
        o_price[...] = price1_v[...] + sd2 * (demand_v[...] - pushed)

    push(1, results, price_out)

    dual_copy(1).wait_send()
    prev_copy(1).wait_send()
    sent(1)
    pltpu.make_async_copy(others, others, ar_sem.at[0]).wait()


def shards(
    gen, flow, price, ramp_dual, demand, incid_tiles, tile_bus, tile_line, gen_tiles, gen_bus,
    gen_cost, gen_cap, ramp_cap, flow_cap, weight,
):
    gb, blk, hours, scen = gen.shape
    lb, bb = flow.shape[0], price.shape[0]
    n_tiles = incid_tiles.shape[0]
    cols = hours * scen
    nt, nr = lax.axis_size("tm"), lax.axis_size("region")
    lines, buses, gens = lb * blk, bb * blk, gb * blk
    width = 3 * lb + gb
    nch = lb
    cw = lines // nch
    n_stages, reach = 0, 0
    while reach < nr - 1:
        reach += 2**n_stages
        n_stages += 1

    dims = (
        nt, nr, scen,
        float((gen.size + flow.size) * nt * nr), float((price.size + ramp_dual.size) * nt * nr),
    )
    any_spec = pl.BlockSpec(memory_space=pl.ANY)
    smem_spec = pl.BlockSpec(memory_space=pltpu.SMEM)
    dma = pltpu.SemaphoreType.DMA
    V = pltpu.VMEM
    scratch = [
        V((n_tiles + gb + 1, blk, blk), bf16),
        V((buses, width * blk), bf16),
        V((buses, cols), f32),
        V((gens, cols), f32),
        V((lines + buses + gens, cols), f32),
        V((3, gb, blk), f32),
        V((lb, blk), f32),
        V((cols, buses), bf16),
        V((cols, lines + gens), f32),
        V((buses, cols), f32),
        V((3, cols, lines), f32),
        V((3, cols, gens), f32),
        V((2, cols, gens), f32),
        V((cols, gens), bf16),
        V((2, 2, nch, cols, cw), f32),
        V((2, 2, nch, cols, cw), f32),
        V((2, nch, cols, cw), bf16),
        V((2, 2, nch, cols, cw), bf16),
        V((2, scen, gens), f32),
        V((2, scen, gens), f32),
        V((2, 2, scen, gens), f32),
        V((2, 2, scen, gens), f32),
        V((scen, gens), f32),
        V((1, 128), f32),
        V((nt * nr, 1, 128), f32),
        V((buses, cols), f32),
        V((8, 128), f32),
        V((2, 1, n_tiles), jnp.int32),
        V((1, 128), jnp.int32),
        pltpu.SMEM((1, 128), jnp.int32),
        dma((7,)),
        dma((2,)),
        dma((nch + 1,)),
        dma((2,)),
        dma((nch + 1,)),
        dma((6,)),
        dma((2,)),
        pltpu.SemaphoreType.REGULAR((n_stages,)),
        dma((1,)),
    ]
    vmem_spec = pl.BlockSpec(memory_space=pltpu.VMEM)
    shapes = ((gens, cols), (lines, cols), (buses, cols), (gens, cols))
    outs = pl.pallas_call(
        functools.partial(kernel, dims),
        out_shape=tuple(V(shape, f32) for shape in shapes),
        in_specs=[smem_spec, smem_spec] + [any_spec] * 13,
        out_specs=(vmem_spec,) * 4,
        scratch_shapes=scratch,
        compiler_params=pltpu.CompilerParams(collective_id=0, has_side_effects=True),
    )(
        gen_bus, weight, tile_bus.reshape(1, n_tiles), tile_line.reshape(1, n_tiles), incid_tiles, gen_tiles,
        price.reshape(buses, cols), flow.reshape(lines, cols), gen.reshape(gens, cols),
        ramp_dual.reshape(gens, cols), demand.reshape(buses, cols),
        gen_cost, gen_cap, ramp_cap, flow_cap,
    )
    outs = pl.pallas_call(
        writer,
        out_shape=tuple(jax.ShapeDtypeStruct(shape, f32) for shape in shapes),
        in_specs=[any_spec] * 4,
        out_specs=(any_spec,) * 4,
        scratch_shapes=[dma((4,))],
    )(*(pltpu.with_memory_space_constraint(out, pltpu.VMEM) for out in outs))
    return tuple(
        out.reshape(like.shape) for out, like in zip(outs, (gen, flow, price, ramp_dual))
    )


def solution(mesh):
    field = P("region", None, "tm", None)
    placed = (
        field, field, field, field, field,
        P("region", None, None), P("region"), P("region"), P("region", None, None), P("region"),
        P("region", None), P("region", None), P("region", None), P("region", None), P(),
    )
    return jax.shard_map(
        shards, mesh=mesh, in_specs=placed, out_specs=(field,) * 4, check_vma=False
    )
```

```python
import functools

import jax
import jax.numpy as jnp
from jax import lax
from jax.experimental import pallas as pl
from jax.experimental.pallas import tpu as pltpu
from jax.sharding import PartitionSpec as P

MESH = pl.DeviceIdType.MESH
step_scale = 0.4
tiny = 1e-06
f32 = jnp.float32
bf16 = jnp.bfloat16


def remote(src, dst, send_sem, recv_sem, axis, peer):
    return pltpu.make_async_remote_copy(
        src_ref=src,
        dst_ref=dst,
        send_sem=send_sem,
        recv_sem=recv_sem,
        device_id={axis: peer},
        device_id_type=MESH,
    )


def fold(x):
    rows, columns = x.shape
    y = jnp.sum(x.reshape(rows // 8, 8, columns), axis=0)
    out = y[:, :128]
    for at in range(128, columns, 128):
        out = out + y[:, at : at + 128]
    return out


def both_halves(x):
    row = jnp.sum(x, axis=0, keepdims=True)
    return row + pltpu.roll(row, 64, 1)


def writer(*refs):
    n = (len(refs) - 1) // 2
    copies = [pltpu.make_async_copy(refs[i], refs[n + i], refs[-1].at[i]) for i in range(n)]
    for c in copies:
        c.start()
    for c in copies:
        c.wait()


def flip(x, mask):
    bit = 1
    out = x
    while bit <= mask:
        if mask & bit:
            out = out + bit * (1 - 2 * lax.rem(x // bit, 2))
        bit *= 2
    return out


def partners(x, n):
    if n & (n - 1) == 0:
        return [(m, flip(x, m)) for m in range(n - 1, 0, -1)]
    return [(m, lax.rem(x + m, n)) for m in range(1, n)]


FAR, NEAR = 0, 1


def kernel(
    dims,
    gen_bus, weight, tile_bus, tile_line, tiles, gtiles, price, flow, gen, ramp, demand, cost, gcap, rcap, fcap,
    o_gen, o_flow, o_price, o_ramp,
    tiles_v, a_v, price_v, ramp_v, late_v, caps_v, fcap_v,
    pt_v, own_v, price1_v, flow_s, gen_s, dual_s, genlow_v,
    part_send, part_recv, fw_own, fw_in, d_send, d_recv, v_send, v_recv, prev_v,
    now_send, now_recv, tot_send, tot_recv,
    ar_s, ar_r, acc_v, change_v, idx_v, table_v, table_s,
    in_sem, ps_sem, pr_sem, fs_sem, fr_sem, tm_sem, ar_sem, ahead_sem, ready, table_sem,
):
    nt, nr, scen, count_p, count_d = dims
    t = lax.axis_index("tm")
    r = lax.axis_index("region")
    n_tiles, blk, _ = tiles.shape
    n_gens = gtiles.shape[0]
    lines, cols = flow.shape
    buses = price.shape[0]
    lb, bb = lines // blk, buses // blk
    width = 3 * lb + n_gens
    gens = gen.shape[0]
    nch = part_send.shape[2]
    cw = lines // nch
    n_stages = ready.shape[0]
    early = tot_send.shape[0]

    odd = lax.rem(r, 2)
    place = (r - 1 + 2 * odd, r + 1 - 2 * odd)
    has = tuple((p >= 0) & (p < nr) for p in place)
    peer = tuple(jnp.clip(p, 0, nr - 1) for p in place)
    count = tuple(jnp.where(h, 1, 0) for h in has)
    first_window = (2 * lb * odd, 2 * lb * (1 - odd), lb)

    barrier = pltpu.get_barrier_semaphore()
    for side in (FAR, NEAR):
        @pl.when(has[side])
        def _():
            pl.semaphore_signal(
                barrier, inc=1, device_id={"region": peer[side]}, device_id_type=MESH
            )
    for k in range(1, nt):
        pl.semaphore_signal(
            barrier, inc=1, device_id={"tm": lax.rem(t + k, nt)}, device_id_type=MESH
        )

    def stage_signal(stage):
        step = 2**stage
        for to in (r - step, r + step):
            @pl.when((to >= 0) & (to < nr))
            def _():
                pl.semaphore_signal(
                    ready.at[stage], inc=1, device_id={"region": jnp.clip(to, 0, nr - 1)},
                    device_id_type=MESH,
                )

    def stage_wait(stage):
        step = 2**stage
        pl.semaphore_wait(
            ready.at[stage], jnp.where(r >= step, 1, 0) + jnp.where(r + step < nr, 1, 0)
        )

    def pass_on(stage):
        if stage < n_stages - 1:
            stage_wait(stage)
            stage_signal(stage + 1)

    def load(i, *pairs):
        copies = [pltpu.make_async_copy(src, dst, in_sem.at[i]) for src, dst in pairs]
        for c in copies:
            c.start()

    def arrived(i, ref):
        pltpu.make_async_copy(ref, ref, in_sem.at[i]).wait()

    load(0, (tile_bus, idx_v.at[0]), (tile_line, idx_v.at[1]))
    all_tiles = tiles_v.at[pl.ds(0, n_tiles + n_gens)]
    load(1, (price, price_v))
    load(2, (ramp, ramp_v))
    load(3, (tiles, tiles_v.at[pl.ds(0, n_tiles)]), (gtiles, tiles_v.at[pl.ds(n_tiles, n_gens)]))
    flow_v = late_v.at[pl.ds(0, lines)]
    demand_v = late_v.at[pl.ds(lines, buses)]
    gen_v = late_v.at[pl.ds(lines + buses, gens)]

    def late_loads():
        load(4, (flow, flow_v), (demand, demand_v), (gen, gen_v))
        load(5, (cost, caps_v.at[0]), (gcap, caps_v.at[1]), (rcap, caps_v.at[2]))
        load(6, (fcap, fcap_v))

    tiles_v[n_tiles + n_gens] = jnp.zeros((blk, blk), bf16)

    for side in (FAR, NEAR):
        @pl.when(jnp.logical_not(has[side]))
        def _():
            part_recv[:, side] = jnp.zeros_like(part_recv[:, side])
            fw_in[:, side] = jnp.zeros_like(fw_in[:, side])

    t_next, t_prev = lax.rem(t + 1, nt), lax.rem(t + nt - 1, nt)

    def far_part(it, ch):
        return remote(
            part_send.at[it, FAR, ch], part_recv.at[it, FAR, ch],
            ps_sem.at[FAR], pr_sem.at[ch], "region", peer[FAR],
        )

    def near_part(it):
        return remote(
            part_send.at[it, NEAR], part_recv.at[it, NEAR],
            ps_sem.at[NEAR], pr_sem.at[nch], "region", peer[NEAR],
        )

    def far_flow(it, ch):
        return remote(
            fw_own.at[it, ch], fw_in.at[it, FAR, ch],
            fs_sem.at[FAR], fr_sem.at[ch], "region", peer[FAR],
        )

    def near_flow(it):
        return remote(
            fw_own.at[it], fw_in.at[it, NEAR],
            fs_sem.at[NEAR], fr_sem.at[nch], "region", peer[NEAR],
        )

    def dual_copy(it):
        return remote(d_send.at[it], d_recv.at[it], tm_sem.at[0], tm_sem.at[2 + it], "tm", t_prev)

    def prev_copy(it):
        parts = pl.ds(0, 2 - it)
        return remote(
            v_send.at[it, parts], v_recv.at[it, parts], tm_sem.at[1], tm_sem.at[4 + it], "tm", t_next
        )

    def now_copy():
        return remote(
            now_send, now_recv, ahead_sem.at[0], ahead_sem.at[1], "region", peer[FAR]
        )

    def total_copy(ch):
        return remote(
            tot_send.at[ch], tot_recv.at[ch], ahead_sem.at[2], ahead_sem.at[3 + ch],
            "region", peer[FAR],
        )

    def sent(it):
        for side in (FAR, NEAR):
            @pl.when(has[side])
            def _():
                ref = part_send.at[it, side]
                pltpu.make_async_copy(ref, ref, ps_sem.at[side]).wait()
                ref = fw_own.at[it]
                if it == 1 and side == FAR:
                    ref = fw_own.at[it, pl.ds(early, nch - early)]
                pltpu.make_async_copy(ref, ref, fs_sem.at[side]).wait()

    at_near, at_own, at_gens = lines, 2 * lines, 3 * lines

    def build(group):
        n = n_gens if group == 3 else lb
        for i in range(n):
            window = 3 * lb + i if group == 3 else first_window[group] + i
            lo = group * lines + i * blk
            for b in range(bb):
                a_v[b * blk : (b + 1) * blk, lo : lo + blk] = tiles_v[table_s[0, b * width + window]]

    per_dot = 2 if nch % 2 == 0 else 1

    def far_sums(it, ch):
        sums = jnp.dot(
            pt_v[...], a_v[:, ch * cw : (ch + per_dot) * cw], preferred_element_type=f32
        )
        for i in range(per_dot):
            part_send[it, FAR, ch + i] = sums[:, i * cw : (i + 1) * cw]

    def send_far(it, ch):
        @pl.when(has[FAR])
        def _():
            for i in range(per_dot):
                far_part(it, ch + i).start()

    def pull_near(it):
        for ch in range(0, nch, per_dot):
            at = at_near + ch * cw
            sums = jnp.dot(
                pt_v[...], a_v[:, at : at + per_dot * cw], preferred_element_type=f32
            )
            for i in range(per_dot):
                part_send[it, NEAR, ch + i] = sums[:, i * cw : (i + 1) * cw]

        @pl.when(has[NEAR])
        def _():
            near_part(it).start()

    def pull_gens():
        own_v[:, lines:] = jnp.dot(pt_v[...], a_v[:, at_gens:], preferred_element_type=f32)

    def pull_own():
        own_v[:, :lines] = jnp.dot(
            pt_v[...], a_v[:, at_own:at_gens], preferred_element_type=f32
        )

    def set_pt(ref):
        for b in range(bb):
            pt_v[:, b * blk : (b + 1) * blk] = ref[b * blk : (b + 1) * blk, :].astype(bf16).T

    def row(ref, n):
        return jnp.concatenate([ref[i : i + 1, :] for i in range(n)], axis=1) if n > 1 else ref[...]

    def gen_pull(it):
        grad = row(caps_v.at[0], n_gens) - own_v[:, lines:] + dual_s[it]
        own_v[:, lines:] = grad
        v_send[it, 0] = grad[cols - scen :]
        if it == 0:
            v_send[it, 1] = gen_s[it][cols - scen :]
        prev_copy(it).start()

    def clipped(now, sp, grad):
        return jnp.minimum(jnp.maximum(now - sp * grad, 0.0), row(caps_v.at[1], n_gens))

    def gen_step(it, sp):
        dual_copy(it).wait_recv()
        nxt = d_recv[it]
        later = nxt if cols == scen else jnp.concatenate([dual_s[it][scen:], nxt], axis=0)
        gnow = gen_s[it]
        gnew = clipped(gnow, sp, own_v[:, lines:] - later)
        gbar = 2.0 * gnew - gnow
        gen_s[it + 1] = gnew
        genlow_v[...] = gbar.astype(bf16)
        return (gnew - gnow) ** 2, gbar

    def prev_bar(it, sp):
        now = v_recv[it, 1] if it == 0 else prev_v[...]
        new = clipped(now, sp, v_recv[it, 0] - dual_s[it][:scen])
        prev_v[...] = new
        return 2.0 * new - now

    def near_arrived(it):
        @pl.when(has[NEAR])
        def _():
            near_part(it).wait_recv()

    def total_at(it, ch):
        @pl.when(has[FAR])
        def _():
            far_part(it, ch).wait_recv()

        lo = ch * cw
        return own_v[:, lo : lo + cw] + part_recv[it, NEAR, ch] + part_recv[it, FAR, ch]

    per = cw // blk

    def flow_step(it, ch, sp, total, send=True):
        lo = ch * cw
        cap = jnp.concatenate(
            [fcap_v[ch * per + i : ch * per + i + 1, :] for i in range(per)], axis=1
        )
        now = flow_s[it, :, lo : lo + cw]
        new = jnp.minimum(jnp.maximum(now + sp * total, -cap), cap)
        fw_own[it, ch] = (2.0 * new - now).astype(bf16)

        if send:
            @pl.when(has[FAR])
            def _():
                far_flow(it, ch).start()

        flow_s[it + 1, :, lo : lo + cw] = new
        if it == 0 and ch < early:
            now_send[ch, :cols] = new
            now_send[ch, cols:] = jnp.broadcast_to(cap, (8, cw))
        return (new - now) ** 2

    def far_flows(sp):
        now_copy().wait_recv()
        lows = []
        for ch in range(early):
            total_copy(ch).wait_recv()
            now, cap = now_recv[ch, :cols], now_recv[ch, cols : cols + 1]
            new = jnp.minimum(jnp.maximum(now + sp * tot_recv[ch], -cap), cap)
            lows.append((2.0 * new - now).astype(bf16))
        return jnp.concatenate(lows, axis=1) if early > 1 else lows[0]

    def send_near(it):
        @pl.when(has[NEAR])
        def _():
            near_flow(it).start()

    nt_dims = (((1,), (1,)), ((), ()))

    def joined(get, n):
        return jnp.concatenate([get(ch) for ch in range(n)], axis=1) if n > 1 else get(0)

    def push_own(it):
        mine = jnp.concatenate([fw_own[it, ch] for ch in range(nch)] + [genlow_v[...]], axis=1)
        acc_v[...] = lax.dot_general(a_v[:, at_own:], mine, nt_dims, preferred_element_type=f32)

    def push_near(it):
        @pl.when(has[NEAR])
        def _():
            near_flow(it).wait_recv()

        other = joined(lambda ch: fw_in[it, NEAR, ch], nch)
        acc_v[...] += lax.dot_general(
            a_v[:, at_near:at_own], other, nt_dims, preferred_element_type=f32
        )

    def push_lines(first, low):
        return lax.dot_general(
            a_v[:, first * cw : first * cw + low.shape[1]], low, nt_dims, preferred_element_type=f32
        )

    def far_low(it, first, count):
        for ch in range(first, first + count):
            far_flow(it, ch).wait_recv()
        return joined(lambda ch: fw_in[it, FAR, first + ch], count)

    def push(it, ahead, meanwhile, early_low, finish):
        def far_first():
            if ahead > 0:
                @pl.when(has[FAR])
                def _():
                    acc_v[...] += push_lines(0, early_low())

        push_own(it)
        if it == 0:
            far_first()
            push_near(it)
            meanwhile()
        else:
            far_first()
            meanwhile()
            push_near(it)

        @pl.when(has[FAR])
        def _():
            finish(acc_v[...] + push_lines(ahead, far_low(it, ahead, nch - ahead)))

        @pl.when(jnp.logical_not(has[FAR]))
        def _():
            finish(acc_v[...])

    def ramp_step(it, gbar, prev, sd):
        earlier = prev if cols == scen else jnp.concatenate([prev, gbar[: cols - scen]], axis=0)
        dual = dual_s[it]
        lifted = dual + sd * (gbar - earlier)
        bound = row(caps_v.at[2], n_gens)
        return lifted - sd * jnp.minimum(jnp.maximum(lifted / sd, -bound), bound)

    zero_at = n_tiles + n_gens
    arrived(0, idx_v)
    slot = idx_v[0] * width + (idx_v[1] - (r - 1) * lb)
    down = lax.broadcasted_iota(jnp.int32, (n_tiles, n_tiles), 0)
    across = lax.broadcasted_iota(jnp.int32, (n_tiles, n_tiles), 1)
    upright = jnp.sum(jnp.where(down == across, slot, 0), axis=1, keepdims=True)
    places = lax.broadcasted_iota(jnp.int32, (n_tiles, 128), 1)
    ids = lax.broadcasted_iota(jnp.int32, (n_tiles, 128), 0)
    found = jnp.sum(jnp.where(upright == places, ids - zero_at, 0), axis=0, keepdims=True)
    lane = lax.broadcasted_iota(jnp.int32, (1, 128), 1)
    for g in range(n_gens):
        found = jnp.where(lane == gen_bus[g] * width + 3 * lb + g, n_tiles + g - zero_at, found)
    table_v[...] = jnp.clip(zero_at + found, 0, zero_at)
    to_scalar = pltpu.make_async_copy(table_v, table_s, table_sem.at[0])
    to_scalar.start()

    w1 = jnp.full((1, 1), weight[...], f32)
    arrived(1, price_v)
    set_pt(price_v)
    arrived(2, ramp_v)
    dual_s[0] = ramp_v[...].T
    d_send[0] = dual_s[0][:scen]
    arrived(3, all_tiles)
    to_scalar.wait()
    build(FAR)
    pl.semaphore_wait(barrier, nt - 1 + count[FAR] + count[NEAR])
    if n_stages > 0:
        stage_signal(0)
    dual_copy(0).start()
    for ch in range(0, nch, per_dot):
        far_sums(0, ch)
        send_far(0, ch)
    late_loads()
    build(NEAR)
    pull_near(0)
    build(3)
    pull_gens()
    arrived(4, late_v)
    arrived(5, caps_v)
    gen_s[0] = gen_v[...].T
    gen_pull(0)
    pass_on(0)
    build(2)
    pull_own()
    sd1 = step_scale * w1
    sp1 = step_scale / w1
    for b in range(lb):
        flow_s[0, :, b * blk : (b + 1) * blk] = flow_v[b * blk : (b + 1) * blk, :].T
    arrived(6, fcap_v)
    near_arrived(0)
    primal_acc = jnp.zeros((8, 128), f32)
    for ch in range(nch):
        primal_acc = primal_acc + fold(flow_step(0, ch, sp1, total_at(0, ch)))
        if ch == 0:
            pass_on(1)
    if early > 0:
        @pl.when(has[FAR])
        def _():
            now_copy().start()

    send_near(0)
    for stage in range(2, n_stages - 1):
        pass_on(stage)
    changed, gbar1 = gen_step(0, sp1)
    primal_acc = primal_acc + fold(changed)
    low = lax.broadcasted_iota(jnp.int32, (1, 128), 1) < 64
    primal_row = both_halves(primal_acc)

    def ramp_now():
        prev_copy(0).wait_recv()
        dual_one = ramp_step(0, gbar1, prev_bar(0, sp1), sd1)
        dual_s[1] = dual_one
        change_v[...] = fold((dual_one - dual_s[0]) ** 2)
        dual_copy(0).wait_send()
        d_send[1] = dual_one[:scen]
        dual_copy(1).start()

    def price_now(pushed):
        new = price_v[...] + sd1 * (demand_v[...] - pushed)
        price1_v[...] = new
        dual_row = both_halves(change_v[...] + fold((new - price_v[...]) ** 2))
        ar_s[...] = jnp.where(low, primal_row, dual_row)
        new_low = new.astype(bf16)
        for b in range(bb):
            pt_v[:, b * blk : (b + 1) * blk] = new_low[b * blk : (b + 1) * blk, :].T
        far_sums(1, 0)

    push(0, nch // 2, ramp_now, lambda: far_low(0, 0, nch // 2), price_now)

    if n_stages > 0:
        stage_wait(n_stages - 1)
    sent(0)
    others_t = partners(t, nt) + [(0, t)]
    others_r = partners(r, nr) + [(0, r)]
    for k, to_r in others_r:
        for j, to_t in others_t:
            if j or k:
                pltpu.make_async_remote_copy(
                    src_ref=ar_s,
                    dst_ref=ar_r.at[j * nr + k],
                    send_sem=ar_sem.at[0],
                    recv_sem=ar_sem.at[1],
                    device_id={"tm": to_t, "region": to_r},
                    device_id_type=MESH,
                ).start()
    others = ar_r.at[pl.ds(1, nt * nr - 1)]
    send_far(1, 0)
    for ch in range(per_dot, nch, per_dot):
        far_sums(1, ch)
        send_far(1, ch)
    pull_near(1)
    pull_gens()
    prev_copy(0).wait_send()
    gen_pull(1)
    pull_own()
    near_arrived(1)
    for ch in range(early):
        tot_send[ch] = total_at(1, ch)

        @pl.when(has[FAR])
        def _():
            total_copy(ch).start()

    pltpu.make_async_copy(others, others, ar_sem.at[1]).wait()
    summed = ar_s[...]
    for at in range(1, nt * nr):
        summed = summed + ar_r[at]
    primal_mean = jnp.sum(jnp.where(low, summed, 0.0), axis=1, keepdims=True) / count_p
    dual_mean = jnp.sum(jnp.where(low, 0.0, summed), axis=1, keepdims=True) / count_d
    w2 = jnp.sqrt(w1 * jnp.sqrt((dual_mean + tiny) / (primal_mean + tiny)))

    sd2 = step_scale * w2
    sp2 = step_scale / w2
    for ch in range(early, nch):
        flow_step(1, ch, sp2, total_at(1, ch))
    for ch in range(early):
        flow_step(1, ch, sp2, tot_send[ch], send=False)
    send_near(1)
    _, gbar2 = gen_step(1, sp2)

    def results():
        prev_copy(1).wait_recv()
        o_ramp[...] = ramp_step(1, gbar2, prev_bar(1, sp2), sd2).T
        for b in range(lb):
            o_flow[b * blk : (b + 1) * blk, :] = flow_s[2, :, b * blk : (b + 1) * blk].T
        o_gen[...] = gen_s[2].T

    def price_out(pushed):
        o_price[...] = price1_v[...] + sd2 * (demand_v[...] - pushed)

    push(1, early, results, lambda: far_flows(sp2), price_out)

    dual_copy(1).wait_send()
    prev_copy(1).wait_send()
    sent(1)
    if early > 0:
        @pl.when(has[FAR])
        def _():
            now_copy().wait_send()
            pltpu.make_async_copy(tot_send, tot_send, ahead_sem.at[2]).wait()

    pltpu.make_async_copy(others, others, ar_sem.at[0]).wait()


def shards(
    gen, flow, price, ramp_dual, demand, incid_tiles, tile_bus, tile_line, gen_tiles, gen_bus,
    gen_cost, gen_cap, ramp_cap, flow_cap, weight,
):
    gb, blk, hours, scen = gen.shape
    lb, bb = flow.shape[0], price.shape[0]
    n_tiles = incid_tiles.shape[0]
    cols = hours * scen
    nt, nr = lax.axis_size("tm"), lax.axis_size("region")
    lines, buses, gens = lb * blk, bb * blk, gb * blk
    width = 3 * lb + gb
    nch = lb
    early = nch - 1
    cw = lines // nch
    n_stages, reach = 0, 0
    while reach < nr - 1:
        reach += 2**n_stages
        n_stages += 1

    dims = (
        nt, nr, scen,
        float((gen.size + flow.size) * nt * nr), float((price.size + ramp_dual.size) * nt * nr),
    )
    any_spec = pl.BlockSpec(memory_space=pl.ANY)
    smem_spec = pl.BlockSpec(memory_space=pltpu.SMEM)
    dma = pltpu.SemaphoreType.DMA
    V = pltpu.VMEM
    scratch = [
        V((n_tiles + gb + 1, blk, blk), bf16),
        V((buses, width * blk), bf16),
        V((buses, cols), f32),
        V((gens, cols), f32),
        V((lines + buses + gens, cols), f32),
        V((3, gb, blk), f32),
        V((lb, blk), f32),
        V((cols, buses), bf16),
        V((cols, lines + gens), f32),
        V((buses, cols), f32),
        V((3, cols, lines), f32),
        V((3, cols, gens), f32),
        V((2, cols, gens), f32),
        V((cols, gens), bf16),
        V((2, 2, nch, cols, cw), f32),
        V((2, 2, nch, cols, cw), f32),
        V((2, nch, cols, cw), bf16),
        V((2, 2, nch, cols, cw), bf16),
        V((2, scen, gens), f32),
        V((2, scen, gens), f32),
        V((2, 2, scen, gens), f32),
        V((2, 2, scen, gens), f32),
        V((scen, gens), f32),
        V((early, cols + 8, cw), f32),
        V((early, cols + 8, cw), f32),
        V((early, cols, cw), f32),
        V((early, cols, cw), f32),
        V((1, 128), f32),
        V((nt * nr, 1, 128), f32),
        V((buses, cols), f32),
        V((8, 128), f32),
        V((2, 1, n_tiles), jnp.int32),
        V((1, 128), jnp.int32),
        pltpu.SMEM((1, 128), jnp.int32),
        dma((7,)),
        dma((2,)),
        dma((nch + 1,)),
        dma((2,)),
        dma((nch + 1,)),
        dma((6,)),
        dma((2,)),
        dma((3 + early,)),
        pltpu.SemaphoreType.REGULAR((n_stages,)),
        dma((1,)),
    ]
    vmem_spec = pl.BlockSpec(memory_space=pltpu.VMEM)
    shapes = ((gens, cols), (lines, cols), (buses, cols), (gens, cols))
    outs = pl.pallas_call(
        functools.partial(kernel, dims),
        out_shape=tuple(V(shape, f32) for shape in shapes),
        in_specs=[smem_spec, smem_spec] + [any_spec] * 13,
        out_specs=(vmem_spec,) * 4,
        scratch_shapes=scratch,
        compiler_params=pltpu.CompilerParams(collective_id=0, has_side_effects=True),
    )(
        gen_bus, weight, tile_bus.reshape(1, n_tiles), tile_line.reshape(1, n_tiles), incid_tiles, gen_tiles,
        price.reshape(buses, cols), flow.reshape(lines, cols), gen.reshape(gens, cols),
        ramp_dual.reshape(gens, cols), demand.reshape(buses, cols),
        gen_cost, gen_cap, ramp_cap, flow_cap,
    )
    outs = pl.pallas_call(
        writer,
        out_shape=tuple(jax.ShapeDtypeStruct(shape, f32) for shape in shapes),
        in_specs=[any_spec] * 4,
        out_specs=(any_spec,) * 4,
        scratch_shapes=[dma((4,))],
    )(*(pltpu.with_memory_space_constraint(out, pltpu.VMEM) for out in outs))
    return tuple(
        out.reshape(like.shape) for out, like in zip(outs, (gen, flow, price, ramp_dual))
    )


def solution(mesh):
    field = P("region", None, "tm", None)
    placed = (
        field, field, field, field, field,
        P("region", None, None), P("region"), P("region"), P("region", None, None), P("region"),
        P("region", None), P("region", None), P("region", None), P("region", None), P(),
    )
    return jax.shard_map(
        shards, mesh=mesh, in_specs=placed, out_specs=(field,) * 4, check_vma=False
    )
```

```python
import functools

import jax
import jax.numpy as jnp
from jax import lax
from jax.experimental import pallas as pl
from jax.experimental.pallas import tpu as pltpu
from jax.sharding import PartitionSpec as P

MESH = pl.DeviceIdType.MESH
step_scale = 0.4
tiny = 1e-06
f32 = jnp.float32
bf16 = jnp.bfloat16


def remote(src, dst, send_sem, recv_sem, axis, peer):
    return pltpu.make_async_remote_copy(
        src_ref=src,
        dst_ref=dst,
        send_sem=send_sem,
        recv_sem=recv_sem,
        device_id={axis: peer},
        device_id_type=MESH,
    )


def fold(x):
    rows, columns = x.shape
    y = jnp.sum(x.reshape(rows // 8, 8, columns), axis=0)
    out = y[:, :128]
    for at in range(128, columns, 128):
        out = out + y[:, at : at + 128]
    return out


def both_halves(x):
    row = jnp.sum(x, axis=0, keepdims=True)
    return row + pltpu.roll(row, 64, 1)


def writer(*refs):
    n = (len(refs) - 1) // 2
    copies = [pltpu.make_async_copy(refs[i], refs[n + i], refs[-1].at[i]) for i in range(n)]
    for c in copies:
        c.start()
    for c in copies:
        c.wait()


def flip(x, mask):
    bit = 1
    out = x
    while bit <= mask:
        if mask & bit:
            out = out + bit * (1 - 2 * lax.rem(x // bit, 2))
        bit *= 2
    return out


def partners(x, n):
    if n & (n - 1) == 0:
        return [(m, flip(x, m)) for m in [*range(n // 2, n), *range(n // 2 - 1, 0, -1)]]
    return [(m, lax.rem(x + m, n)) for m in range(1, n)]


FAR, NEAR = 0, 1


def kernel(
    dims,
    gen_bus, weight, tile_bus, tile_line, tiles, gtiles, price, flow, gen, ramp, demand, cost, gcap, rcap, fcap,
    o_gen, o_flow, o_price, o_ramp,
    tiles_v, a_v, first_v, late_v, caps_v, fcap_v,
    pt_v, own_v, price1_v, flow_s, gen_s, dual_s, genlow_v,
    part_send, part_recv, fw_own, fw_in, d_send, d_recv, v_send, v_recv, prev_v,
    now_send, now_recv, tot_send, tot_recv,
    ar_s, ar_r, acc_v, change_v, idx_v, table_v, table_s,
    in_sem, ps_sem, pr_sem, fs_sem, fr_sem, tm_sem, ar_sem, ahead_sem, ready,
):
    nt, nr, scen, count_p, count_d = dims
    t = lax.axis_index("tm")
    r = lax.axis_index("region")
    n_tiles, blk, _ = tiles.shape
    n_gens = gtiles.shape[0]
    lines, cols = flow.shape
    buses = price.shape[0]
    lb, bb = lines // blk, buses // blk
    width = 3 * lb + n_gens
    nch = part_send.shape[2]
    cw = lines // nch
    n_stages = ready.shape[0]
    early = tot_send.shape[0]

    odd = lax.rem(r, 2)
    place = (r - 1 + 2 * odd, r + 1 - 2 * odd)
    has = tuple((p >= 0) & (p < nr) for p in place)
    peer = tuple(jnp.clip(p, 0, nr - 1) for p in place)
    count = tuple(jnp.where(h, 1, 0) for h in has)
    first_window = (2 * lb * odd, 2 * lb * (1 - odd), lb)

    barrier = pltpu.get_barrier_semaphore()
    for side in (FAR, NEAR):
        @pl.when(has[side])
        def _():
            pl.semaphore_signal(
                barrier, inc=1, device_id={"region": peer[side]}, device_id_type=MESH
            )
    for k in range(1, nt):
        pl.semaphore_signal(
            barrier, inc=1, device_id={"tm": lax.rem(t + k, nt)}, device_id_type=MESH
        )

    def stage_signal(stage):
        step = 2**stage
        for to in (r - step, r + step):
            @pl.when((to >= 0) & (to < nr))
            def _():
                pl.semaphore_signal(
                    ready.at[stage], inc=1, device_id={"region": jnp.clip(to, 0, nr - 1)},
                    device_id_type=MESH,
                )

    def stage_wait(stage):
        step = 2**stage
        pl.semaphore_wait(
            ready.at[stage], jnp.where(r >= step, 1, 0) + jnp.where(r + step < nr, 1, 0)
        )

    def pass_on(stage):
        if stage < n_stages - 1:
            stage_wait(stage)
            stage_signal(stage + 1)

    def load(i, *pairs):
        copies = [pltpu.make_async_copy(src, dst, in_sem.at[i]) for src, dst in pairs]
        for c in copies:
            c.start()

    def arrived(i, ref):
        pltpu.make_async_copy(ref, ref, in_sem.at[i]).wait()

    load(0, (tile_bus, idx_v.at[0]), (tile_line, idx_v.at[1]))
    all_tiles = tiles_v.at[pl.ds(0, n_tiles + n_gens)]
    gens = gen.shape[0]
    price_v, ramp_v = first_v.at[pl.ds(0, buses)], first_v.at[pl.ds(buses, gens)]
    load(1, (price, price_v), (ramp, ramp_v))
    load(2, (tiles, tiles_v.at[pl.ds(0, n_tiles)]), (gtiles, tiles_v.at[pl.ds(n_tiles, n_gens)]))
    flow_v = late_v.at[pl.ds(0, lines)]
    demand_v = late_v.at[pl.ds(lines, buses)]
    gen_v = late_v.at[pl.ds(lines + buses, gens)]

    def late_loads():
        load(0, (flow, flow_v), (demand, demand_v), (gen, gen_v))
        load(1, (cost, caps_v.at[0]), (gcap, caps_v.at[1]), (rcap, caps_v.at[2]))
        load(2, (fcap, fcap_v))

    tiles_v[n_tiles + n_gens] = jnp.zeros((blk, blk), bf16)

    for side in (FAR, NEAR):
        @pl.when(jnp.logical_not(has[side]))
        def _():
            part_recv[:, side] = jnp.zeros_like(part_recv[:, side])
            fw_in[:, side] = jnp.zeros_like(fw_in[:, side])

    t_next, t_prev = lax.rem(t + 1, nt), lax.rem(t + nt - 1, nt)

    def far_part(it, ch):
        return remote(
            part_send.at[it, FAR, ch], part_recv.at[it, FAR, ch],
            ps_sem.at[FAR], pr_sem.at[ch], "region", peer[FAR],
        )

    def near_part(it):
        return remote(
            part_send.at[it, NEAR], part_recv.at[it, NEAR],
            ps_sem.at[NEAR], pr_sem.at[nch], "region", peer[NEAR],
        )

    def far_flow(it, ch):
        return remote(
            fw_own.at[it, ch], fw_in.at[it, FAR, ch],
            fs_sem.at[FAR], fr_sem.at[ch], "region", peer[FAR],
        )

    def near_flow(it):
        return remote(
            fw_own.at[it], fw_in.at[it, NEAR],
            fs_sem.at[NEAR], fr_sem.at[nch], "region", peer[NEAR],
        )

    def dual_copy(it):
        return remote(d_send.at[it], d_recv.at[it], tm_sem.at[0], tm_sem.at[2 + it], "tm", t_prev)

    def prev_copy(it):
        parts = pl.ds(0, 2 - it)
        return remote(
            v_send.at[it, parts], v_recv.at[it, parts], tm_sem.at[1], tm_sem.at[4 + it], "tm", t_next
        )

    def now_copy():
        return remote(
            now_send, now_recv, ahead_sem.at[0], ahead_sem.at[1], "region", peer[FAR]
        )

    def total_copy(ch):
        return remote(
            tot_send.at[ch], tot_recv.at[ch], ahead_sem.at[0], fr_sem.at[ch],
            "region", peer[FAR],
        )

    def sent(it):
        for side in (FAR, NEAR):
            @pl.when(has[side])
            def _():
                ref = part_send.at[it, side]
                pltpu.make_async_copy(ref, ref, ps_sem.at[side]).wait()
                ref = fw_own.at[it]
                if it == 1 and side == FAR:
                    ref = fw_own.at[it, pl.ds(early, nch - early)]
                pltpu.make_async_copy(ref, ref, fs_sem.at[side]).wait()

    at_near, at_own, at_gens = lines, 2 * lines, 3 * lines

    def build(group):
        n = n_gens if group == 3 else lb
        for i in range(n):
            window = 3 * lb + i if group == 3 else first_window[group] + i
            lo = group * lines + i * blk
            for b in range(bb):
                a_v[b * blk : (b + 1) * blk, lo : lo + blk] = tiles_v[table_s[0, b * width + window]]

    per_dot = 2 if nch % 2 == 0 else 1

    def far_sums(it, ch):
        sums = jnp.dot(
            pt_v[...], a_v[:, ch * cw : (ch + per_dot) * cw], preferred_element_type=f32
        )
        for i in range(per_dot):
            part_send[it, FAR, ch + i] = sums[:, i * cw : (i + 1) * cw]

    def send_far(it, ch):
        @pl.when(has[FAR])
        def _():
            for i in range(per_dot):
                far_part(it, ch + i).start()

    def pull_near(it):
        for ch in range(0, nch, per_dot):
            at = at_near + ch * cw
            sums = jnp.dot(
                pt_v[...], a_v[:, at : at + per_dot * cw], preferred_element_type=f32
            )
            for i in range(per_dot):
                part_send[it, NEAR, ch + i] = sums[:, i * cw : (i + 1) * cw]

        @pl.when(has[NEAR])
        def _():
            near_part(it).start()

    def pull_gens():
        own_v[:, lines:] = jnp.dot(pt_v[...], a_v[:, at_gens:], preferred_element_type=f32)

    def pull_own():
        own_v[:, :lines] = jnp.dot(
            pt_v[...], a_v[:, at_own:at_gens], preferred_element_type=f32
        )

    def set_pt(ref):
        for b in range(bb):
            pt_v[:, b * blk : (b + 1) * blk] = ref[b * blk : (b + 1) * blk, :].astype(bf16).T

    def row(ref, n):
        return jnp.concatenate([ref[i : i + 1, :] for i in range(n)], axis=1) if n > 1 else ref[...]

    def gen_pull(it):
        grad = row(caps_v.at[0], n_gens) - own_v[:, lines:] + dual_s[it]
        own_v[:, lines:] = grad
        v_send[it, 0] = grad[cols - scen :]
        if it == 0:
            v_send[it, 1] = gen_s[it][cols - scen :]
        prev_copy(it).start()

    def clipped(now, sp, grad):
        return jnp.minimum(jnp.maximum(now - sp * grad, 0.0), row(caps_v.at[1], n_gens))

    def gen_step(it, sp):
        dual_copy(it).wait_recv()
        nxt = d_recv[it]
        later = nxt if cols == scen else jnp.concatenate([dual_s[it][scen:], nxt], axis=0)
        gnow = gen_s[it]
        gnew = clipped(gnow, sp, own_v[:, lines:] - later)
        gbar = 2.0 * gnew - gnow
        gen_s[it + 1] = gnew
        genlow_v[...] = gbar.astype(bf16)
        return (gnew - gnow) ** 2, gbar

    def prev_bar(it, sp):
        now = v_recv[it, 1] if it == 0 else prev_v[...]
        new = clipped(now, sp, v_recv[it, 0] - dual_s[it][:scen])
        prev_v[...] = new
        return 2.0 * new - now

    def near_arrived(it):
        @pl.when(has[NEAR])
        def _():
            near_part(it).wait_recv()

    def total_at(it, ch):
        @pl.when(has[FAR])
        def _():
            far_part(it, ch).wait_recv()

        lo = ch * cw
        return own_v[:, lo : lo + cw] + part_recv[it, NEAR, ch] + part_recv[it, FAR, ch]

    per = cw // blk

    def flow_step(it, ch, sp, total, send=True):
        lo = ch * cw
        cap = jnp.concatenate(
            [fcap_v[ch * per + i : ch * per + i + 1, :] for i in range(per)], axis=1
        )
        now = flow_s[it, :, lo : lo + cw]
        new = jnp.minimum(jnp.maximum(now + sp * total, -cap), cap)
        fw_own[it, ch] = (2.0 * new - now).astype(bf16)

        if send:
            @pl.when(has[FAR])
            def _():
                far_flow(it, ch).start()

        flow_s[it + 1, :, lo : lo + cw] = new
        if it == 0 and ch < early:
            now_send[ch, :cols] = new
            now_send[ch, cols:] = jnp.broadcast_to(cap, (8, cw))
        return (new - now) ** 2

    def ahead_low(sp, ch):
        total_copy(ch).wait_recv()
        now, cap = now_recv[ch, :cols], now_recv[ch, cols : cols + 1]
        new = jnp.minimum(jnp.maximum(now + sp * tot_recv[ch], -cap), cap)
        return (2.0 * new - now).astype(bf16)

    def send_near(it):
        @pl.when(has[NEAR])
        def _():
            near_flow(it).start()

    nt_dims = (((1,), (1,)), ((), ()))

    def joined(get, n):
        return jnp.concatenate([get(ch) for ch in range(n)], axis=1) if n > 1 else get(0)

    def push_own(it):
        mine = jnp.concatenate([fw_own[it, ch] for ch in range(nch)] + [genlow_v[...]], axis=1)
        acc_v[...] = lax.dot_general(a_v[:, at_own:], mine, nt_dims, preferred_element_type=f32)

    def push_near(it):
        @pl.when(has[NEAR])
        def _():
            near_flow(it).wait_recv()

        other = joined(lambda ch: fw_in[it, NEAR, ch], nch)
        acc_v[...] += lax.dot_general(
            a_v[:, at_near:at_own], other, nt_dims, preferred_element_type=f32
        )

    def push_lines(first, low):
        return lax.dot_general(
            a_v[:, first * cw : first * cw + low.shape[1]], low, nt_dims, preferred_element_type=f32
        )

    half = nch // 2

    def far_low(it, sp, first, count):
        lows = []
        for ch in range(first, first + count):
            if it == 1 and ch < early:
                lows.append(ahead_low(sp, ch))
            else:
                far_flow(it, ch).wait_recv()
                lows.append(fw_in[it, FAR, ch])
        return jnp.concatenate(lows, axis=1) if count > 1 else lows[0]

    def push(it, sp, meanwhile, finish):
        push_own(it)
        if it == 1:
            meanwhile()
        if half > 0:
            @pl.when(has[FAR])
            def _():
                if it == 1:
                    now_copy().wait_recv()
                acc_v[...] += push_lines(0, far_low(it, sp, 0, half))

        push_near(it)
        if it == 0:
            meanwhile()

        @pl.when(has[FAR])
        def _():
            finish(acc_v[...] + push_lines(half, far_low(it, sp, half, nch - half)))

        @pl.when(jnp.logical_not(has[FAR]))
        def _():
            finish(acc_v[...])

    def ramp_step(it, gbar, prev, sd):
        earlier = prev if cols == scen else jnp.concatenate([prev, gbar[: cols - scen]], axis=0)
        dual = dual_s[it]
        lifted = dual + sd * (gbar - earlier)
        bound = row(caps_v.at[2], n_gens)
        return lifted - sd * jnp.minimum(jnp.maximum(lifted / sd, -bound), bound)

    zero_at = n_tiles + n_gens
    arrived(0, idx_v)
    slot = idx_v[0] * width + (idx_v[1] - (r - 1) * lb)
    down = lax.broadcasted_iota(jnp.int32, (n_tiles, n_tiles), 0)
    across = lax.broadcasted_iota(jnp.int32, (n_tiles, n_tiles), 1)
    upright = jnp.sum(jnp.where(down == across, slot, 0), axis=1, keepdims=True)
    places = lax.broadcasted_iota(jnp.int32, (n_tiles, 128), 1)
    ids = lax.broadcasted_iota(jnp.int32, (n_tiles, 128), 0)
    found = jnp.sum(jnp.where(upright == places, ids - zero_at, 0), axis=0, keepdims=True)
    lane = lax.broadcasted_iota(jnp.int32, (1, 128), 1)
    for g in range(n_gens):
        found = jnp.where(lane == gen_bus[g] * width + 3 * lb + g, n_tiles + g - zero_at, found)
    table_v[...] = jnp.clip(zero_at + found, 0, zero_at)
    to_scalar = pltpu.make_async_copy(table_v, table_s, in_sem.at[0])
    to_scalar.start()

    w1 = jnp.full((1, 1), weight[...], f32)
    arrived(1, first_v)
    set_pt(price_v)
    dual_s[0] = ramp_v[...].T
    d_send[0] = dual_s[0][:scen]
    arrived(2, all_tiles)
    to_scalar.wait()
    build(FAR)
    pl.semaphore_wait(barrier, nt - 1 + count[FAR] + count[NEAR])
    if n_stages > 0:
        stage_signal(0)
    dual_copy(0).start()
    for ch in range(0, nch, per_dot):
        far_sums(0, ch)
        send_far(0, ch)
    late_loads()
    build(NEAR)
    pull_near(0)
    build(3)
    pull_gens()
    arrived(0, late_v)
    arrived(1, caps_v)
    gen_s[0] = gen_v[...].T
    gen_pull(0)
    pass_on(0)
    build(2)
    pull_own()
    sd1 = step_scale * w1
    sp1 = step_scale / w1
    for b in range(lb):
        flow_s[0, :, b * blk : (b + 1) * blk] = flow_v[b * blk : (b + 1) * blk, :].T
    arrived(2, fcap_v)
    near_arrived(0)
    primal_acc = jnp.zeros((8, 128), f32)
    for ch in range(nch):
        primal_acc = primal_acc + fold(flow_step(0, ch, sp1, total_at(0, ch)))
        if ch == 0:
            pass_on(1)
    if early > 0:
        @pl.when(has[FAR])
        def _():
            now_copy().start()

    send_near(0)
    for stage in range(2, n_stages - 1):
        pass_on(stage)
    changed, gbar1 = gen_step(0, sp1)
    primal_acc = primal_acc + fold(changed)
    low = lax.broadcasted_iota(jnp.int32, (1, 128), 1) < 64
    primal_row = both_halves(primal_acc)

    def ramp_now():
        prev_copy(0).wait_recv()
        dual_one = ramp_step(0, gbar1, prev_bar(0, sp1), sd1)
        dual_s[1] = dual_one
        change_v[...] = fold((dual_one - dual_s[0]) ** 2)
        dual_copy(0).wait_send()
        d_send[1] = dual_one[:scen]
        dual_copy(1).start()

    def price_now(pushed):
        new = price_v[...] + sd1 * (demand_v[...] - pushed)
        price1_v[...] = new
        dual_row = both_halves(change_v[...] + fold((new - price_v[...]) ** 2))
        ar_s[...] = jnp.where(low, primal_row, dual_row)

    push(0, sp1, ramp_now, price_now)

    if n_stages > 0:
        stage_wait(n_stages - 1)
    sent(0)
    others_t = partners(t, nt) + [(0, t)]
    others_r = partners(r, nr) + [(0, r)]
    for k, to_r in others_r:
        for j, to_t in others_t:
            if j or k:
                pltpu.make_async_remote_copy(
                    src_ref=ar_s,
                    dst_ref=ar_r.at[j * nr + k],
                    send_sem=ar_sem.at[0],
                    recv_sem=ar_sem.at[1],
                    device_id={"tm": to_t, "region": to_r},
                    device_id_type=MESH,
                ).start()
    others = ar_r.at[pl.ds(1, nt * nr - 1)]
    set_pt(price1_v)
    for ch in range(0, nch, per_dot):
        far_sums(1, ch)
        send_far(1, ch)
    pull_near(1)
    pull_gens()
    prev_copy(0).wait_send()
    gen_pull(1)
    pull_own()
    near_arrived(1)
    for ch in range(early):
        tot_send[ch] = total_at(1, ch)

        @pl.when(has[FAR])
        def _():
            if ch == 0:
                now_copy().wait_send()
            total_copy(ch).start()

    pltpu.make_async_copy(others, others, ar_sem.at[1]).wait()
    summed = ar_s[...]
    for at in range(1, nt * nr):
        summed = summed + ar_r[at]
    primal_mean = jnp.sum(jnp.where(low, summed, 0.0), axis=1, keepdims=True) / count_p
    dual_mean = jnp.sum(jnp.where(low, 0.0, summed), axis=1, keepdims=True) / count_d
    w2 = jnp.sqrt(w1 * jnp.sqrt((dual_mean + tiny) / (primal_mean + tiny)))

    sd2 = step_scale * w2
    sp2 = step_scale / w2
    for ch in range(early, nch):
        flow_step(1, ch, sp2, total_at(1, ch))
    for ch in range(early):
        flow_step(1, ch, sp2, tot_send[ch], send=False)
    send_near(1)
    _, gbar2 = gen_step(1, sp2)

    def results():
        prev_copy(1).wait_recv()
        o_ramp[...] = ramp_step(1, gbar2, prev_bar(1, sp2), sd2).T
        for b in range(lb):
            o_flow[b * blk : (b + 1) * blk, :] = flow_s[2, :, b * blk : (b + 1) * blk].T
        o_gen[...] = gen_s[2].T

    def price_out(pushed):
        o_price[...] = price1_v[...] + sd2 * (demand_v[...] - pushed)

    push(1, sp2, results, price_out)

    dual_copy(1).wait_send()
    prev_copy(1).wait_send()
    sent(1)
    if early > 0:
        @pl.when(has[FAR])
        def _():
            pltpu.make_async_copy(tot_send, tot_send, ahead_sem.at[0]).wait()

    pltpu.make_async_copy(others, others, ar_sem.at[0]).wait()


def shards(
    gen, flow, price, ramp_dual, demand, incid_tiles, tile_bus, tile_line, gen_tiles, gen_bus,
    gen_cost, gen_cap, ramp_cap, flow_cap, weight,
):
    gb, blk, hours, scen = gen.shape
    lb, bb = flow.shape[0], price.shape[0]
    n_tiles = incid_tiles.shape[0]
    cols = hours * scen
    nt, nr = lax.axis_size("tm"), lax.axis_size("region")
    lines, buses, gens = lb * blk, bb * blk, gb * blk
    width = 3 * lb + gb
    nch = lb
    early = nch // 2
    cw = lines // nch
    n_stages, reach = 0, 0
    while reach < nr - 1:
        reach += 2**n_stages
        n_stages += 1

    dims = (
        nt, nr, scen,
        float((gen.size + flow.size) * nt * nr), float((price.size + ramp_dual.size) * nt * nr),
    )
    any_spec = pl.BlockSpec(memory_space=pl.ANY)
    smem_spec = pl.BlockSpec(memory_space=pltpu.SMEM)
    dma = pltpu.SemaphoreType.DMA
    V = pltpu.VMEM
    scratch = [
        V((n_tiles + gb + 1, blk, blk), bf16),
        V((buses, width * blk), bf16),
        V((buses + gens, cols), f32),
        V((lines + buses + gens, cols), f32),
        V((3, gb, blk), f32),
        V((lb, blk), f32),
        V((cols, buses), bf16),
        V((cols, lines + gens), f32),
        V((buses, cols), f32),
        V((3, cols, lines), f32),
        V((3, cols, gens), f32),
        V((2, cols, gens), f32),
        V((cols, gens), bf16),
        V((2, 2, nch, cols, cw), f32),
        V((2, 2, nch, cols, cw), f32),
        V((2, nch, cols, cw), bf16),
        V((2, 2, nch, cols, cw), bf16),
        V((2, scen, gens), f32),
        V((2, scen, gens), f32),
        V((2, 2, scen, gens), f32),
        V((2, 2, scen, gens), f32),
        V((scen, gens), f32),
        V((early, cols + 8, cw), f32),
        V((early, cols + 8, cw), f32),
        V((early, cols, cw), f32),
        V((early, cols, cw), f32),
        V((1, 128), f32),
        V((nt * nr, 1, 128), f32),
        V((buses, cols), f32),
        V((8, 128), f32),
        V((2, 1, n_tiles), jnp.int32),
        V((1, 128), jnp.int32),
        pltpu.SMEM((1, 128), jnp.int32),
        dma((3,)),
        dma((2,)),
        dma((nch + 1,)),
        dma((2,)),
        dma((nch + 1,)),
        dma((6,)),
        dma((2,)),
        dma((2,)),
        pltpu.SemaphoreType.REGULAR((n_stages,)),
    ]
    vmem_spec = pl.BlockSpec(memory_space=pltpu.VMEM)
    shapes = ((gens, cols), (lines, cols), (buses, cols), (gens, cols))
    outs = pl.pallas_call(
        functools.partial(kernel, dims),
        out_shape=tuple(V(shape, f32) for shape in shapes),
        in_specs=[smem_spec, smem_spec] + [any_spec] * 13,
        out_specs=(vmem_spec,) * 4,
        scratch_shapes=scratch,
        compiler_params=pltpu.CompilerParams(collective_id=0, has_side_effects=True),
    )(
        gen_bus, weight, tile_bus.reshape(1, n_tiles), tile_line.reshape(1, n_tiles), incid_tiles, gen_tiles,
        price.reshape(buses, cols), flow.reshape(lines, cols), gen.reshape(gens, cols),
        ramp_dual.reshape(gens, cols), demand.reshape(buses, cols),
        gen_cost, gen_cap, ramp_cap, flow_cap,
    )
    outs = pl.pallas_call(
        writer,
        out_shape=tuple(jax.ShapeDtypeStruct(shape, f32) for shape in shapes),
        in_specs=[any_spec] * 4,
        out_specs=(any_spec,) * 4,
        scratch_shapes=[dma((4,))],
    )(*(pltpu.with_memory_space_constraint(out, pltpu.VMEM) for out in outs))
    return tuple(
        out.reshape(like.shape) for out, like in zip(outs, (gen, flow, price, ramp_dual))
    )


def solution(mesh):
    field = P("region", None, "tm", None)
    placed = (
        field, field, field, field, field,
        P("region", None, None), P("region"), P("region"), P("region", None, None), P("region"),
        P("region", None), P("region", None), P("region", None), P("region", None), P(),
    )
    return jax.shard_map(
        shards, mesh=mesh, in_specs=placed, out_specs=(field,) * 4, check_vma=False
    )
```

```python
import functools

import jax
import jax.numpy as jnp
from jax import lax
from jax.experimental import pallas as pl
from jax.experimental.pallas import tpu as pltpu
from jax.sharding import PartitionSpec as P

MESH = pl.DeviceIdType.MESH
step_scale = 0.4
tiny = 1e-06
f32 = jnp.float32
bf16 = jnp.bfloat16


def remote(src, dst, send_sem, recv_sem, axis, peer):
    return pltpu.make_async_remote_copy(
        src_ref=src,
        dst_ref=dst,
        send_sem=send_sem,
        recv_sem=recv_sem,
        device_id={axis: peer},
        device_id_type=MESH,
    )


def fold(x):
    rows, columns = x.shape
    y = jnp.sum(x.reshape(rows // 8, 8, columns), axis=0)
    out = y[:, :128]
    for at in range(128, columns, 128):
        out = out + y[:, at : at + 128]
    return out


def both_halves(x):
    row = jnp.sum(x, axis=0, keepdims=True)
    return row + pltpu.roll(row, 64, 1)


def writer(*refs):
    n = (len(refs) - 1) // 2
    copies = [pltpu.make_async_copy(refs[i], refs[n + i], refs[-1].at[i]) for i in range(n)]
    for c in copies:
        c.start()
    for c in copies:
        c.wait()


def flip(x, mask):
    bit = 1
    out = x
    while bit <= mask:
        if mask & bit:
            out = out + bit * (1 - 2 * lax.rem(x // bit, 2))
        bit *= 2
    return out


def partners(x, n):
    if n & (n - 1) == 0:
        return [(m, flip(x, m)) for m in [*range(n // 2, n), *range(n // 2 - 1, 0, -1)]]
    return [(m, lax.rem(x + m, n)) for m in range(1, n)]


FAR, NEAR = 0, 1


def kernel(
    dims,
    gen_bus, weight, tile_bus, tile_line, tiles, gtiles, price, flow, gen, ramp, demand, cost, gcap, rcap, fcap,
    o_gen, o_flow, o_price, o_ramp,
    tiles_v, a_v, first_v, late_v, caps_v, fcap_v,
    pt_v, own_v, price1_v, flow_s, gen_s, dual_s, genlow_v,
    part_send, part_recv, fw_own, fw_in, d_send, d_recv, v_send, v_recv, prev_v,
    ahead_send, ahead_recv, state_send, state_recv, far_new,
    ar_s, ar_r, acc_v, change_v, idx_v, table_v, table_s,
    in_sem, ps_sem, pr_sem, fs_sem, fr_sem, tm_sem, ar_sem, ahead_sem, ready,
):
    nt, nr, scen, count_p, count_d, early = dims
    t = lax.axis_index("tm")
    r = lax.axis_index("region")
    n_tiles, blk, _ = tiles.shape
    n_gens = gtiles.shape[0]
    lines, cols = flow.shape
    buses = price.shape[0]
    lb, bb = lines // blk, buses // blk
    width = 3 * lb + n_gens
    nch = part_send.shape[2]
    cw = lines // nch
    n_stages = ready.shape[0]
    known = min(early, 1)
    ahead_rows = (2 * cols + 8, early * cols)

    odd = lax.rem(r, 2)
    place = (r - 1 + 2 * odd, r + 1 - 2 * odd)
    has = tuple((p >= 0) & (p < nr) for p in place)
    peer = tuple(jnp.clip(p, 0, nr - 1) for p in place)
    count = tuple(jnp.where(h, 1, 0) for h in has)
    first_window = (2 * lb * odd, 2 * lb * (1 - odd), lb)

    barrier = pltpu.get_barrier_semaphore()
    for side in (FAR, NEAR):
        @pl.when(has[side])
        def _():
            pl.semaphore_signal(
                barrier, inc=1, device_id={"region": peer[side]}, device_id_type=MESH
            )
    for k in range(1, nt):
        pl.semaphore_signal(
            barrier, inc=1, device_id={"tm": lax.rem(t + k, nt)}, device_id_type=MESH
        )

    def stage_signal(stage):
        step = 2**stage
        for to in (r - step, r + step):
            @pl.when((to >= 0) & (to < nr))
            def _():
                pl.semaphore_signal(
                    ready.at[stage], inc=1, device_id={"region": jnp.clip(to, 0, nr - 1)},
                    device_id_type=MESH,
                )

    def stage_wait(stage):
        step = 2**stage
        pl.semaphore_wait(
            ready.at[stage], jnp.where(r >= step, 1, 0) + jnp.where(r + step < nr, 1, 0)
        )

    def pass_on(stage):
        if stage < n_stages - 1:
            stage_wait(stage)
            stage_signal(stage + 1)

    def load(i, *pairs):
        copies = [pltpu.make_async_copy(src, dst, in_sem.at[i]) for src, dst in pairs]
        for c in copies:
            c.start()

    def arrived(i, ref):
        pltpu.make_async_copy(ref, ref, in_sem.at[i]).wait()

    load(0, (tile_bus, idx_v.at[0]), (tile_line, idx_v.at[1]))
    all_tiles = tiles_v.at[pl.ds(0, n_tiles + n_gens)]
    gens = gen.shape[0]
    price_v, ramp_v = first_v.at[pl.ds(0, buses)], first_v.at[pl.ds(buses, gens)]
    load(1, (price, price_v), (ramp, ramp_v))
    load(2, (tiles, tiles_v.at[pl.ds(0, n_tiles)]), (gtiles, tiles_v.at[pl.ds(n_tiles, n_gens)]))
    flow_v = late_v.at[pl.ds(0, lines)]
    demand_v = late_v.at[pl.ds(lines, buses)]
    gen_v = late_v.at[pl.ds(lines + buses, gens)]

    def late_loads():
        load(0, (flow, flow_v), (demand, demand_v), (gen, gen_v))
        load(1, (cost, caps_v.at[0]), (gcap, caps_v.at[1]), (rcap, caps_v.at[2]))
        load(2, (fcap, fcap_v))

    tiles_v[n_tiles + n_gens] = jnp.zeros((blk, blk), bf16)

    for side in (FAR, NEAR):
        @pl.when(jnp.logical_not(has[side]))
        def _():
            part_recv[:, side] = jnp.zeros_like(part_recv[:, side])
            fw_in[:, side] = jnp.zeros_like(fw_in[:, side])

    t_next, t_prev = lax.rem(t + 1, nt), lax.rem(t + nt - 1, nt)

    def far_part(it, ch):
        return remote(
            part_send.at[it, FAR, ch], part_recv.at[it, FAR, ch],
            ps_sem.at[FAR], pr_sem.at[nch + 1 if it == 1 and ch >= nch - known else ch],
            "region", peer[FAR],
        )

    def near_part(it):
        return remote(
            part_send.at[it, NEAR], part_recv.at[it, NEAR],
            ps_sem.at[NEAR], pr_sem.at[nch], "region", peer[NEAR],
        )

    def far_flow(it, ch):
        return remote(
            fw_own.at[it, ch], fw_in.at[it, FAR, ch],
            fs_sem.at[FAR], fr_sem.at[ch], "region", peer[FAR],
        )

    def near_flow(it):
        return remote(
            fw_own.at[it], fw_in.at[it, NEAR],
            fs_sem.at[NEAR], fr_sem.at[nch], "region", peer[NEAR],
        )

    def dual_copy(it):
        return remote(d_send.at[it], d_recv.at[it], tm_sem.at[0], tm_sem.at[2 + it], "tm", t_prev)

    def prev_copy(it):
        parts = pl.ds(0, 2 - it)
        return remote(
            v_send.at[it, parts], v_recv.at[it, parts], tm_sem.at[1], tm_sem.at[4 + it], "tm", t_next
        )

    def ahead_copy(it):
        rows = pl.ds(0, ahead_rows[it])
        return remote(
            ahead_send.at[it, rows], ahead_recv.at[it, rows],
            ahead_sem.at[0], ahead_sem.at[1 + it], "region", peer[FAR],
        )

    def state_copy():
        return remote(
            state_send, state_recv, ahead_sem.at[0], ahead_sem.at[3], "region", peer[FAR]
        )

    def sent(it):
        for side in (FAR, NEAR):
            @pl.when(has[side])
            def _():
                ref = part_send.at[it, side]
                pltpu.make_async_copy(ref, ref, ps_sem.at[side]).wait()
                ref = fw_own.at[it]
                if side == FAR:
                    ref = fw_own.at[it, pl.ds(0, nch - (known, early)[it])]
                pltpu.make_async_copy(ref, ref, fs_sem.at[side]).wait()

    at_near, at_own, at_gens = lines, 2 * lines, 3 * lines

    def build(group):
        n = n_gens if group == 3 else lb
        for i in range(n):
            window = 3 * lb + i if group == 3 else first_window[group] + i
            lo = group * lines + i * blk
            for b in range(bb):
                a_v[b * blk : (b + 1) * blk, lo : lo + blk] = tiles_v[table_s[0, b * width + window]]

    per_dot = 2 if nch % 2 == 0 else 1

    def far_sums(it, ch):
        sums = jnp.dot(
            pt_v[...], a_v[:, ch * cw : (ch + per_dot) * cw], preferred_element_type=f32
        )
        for i in range(per_dot):
            part_send[it, FAR, ch + i] = sums[:, i * cw : (i + 1) * cw]

    def send_far(it, ch):
        @pl.when(has[FAR])
        def _():
            for i in range(per_dot):
                far_part(it, ch + i).start()

    def pull_near(it):
        for ch in range(0, nch, per_dot):
            at = at_near + ch * cw
            sums = jnp.dot(
                pt_v[...], a_v[:, at : at + per_dot * cw], preferred_element_type=f32
            )
            for i in range(per_dot):
                part_send[it, NEAR, ch + i] = sums[:, i * cw : (i + 1) * cw]

        @pl.when(has[NEAR])
        def _():
            near_part(it).start()

    def pull_gens():
        own_v[:, lines:] = jnp.dot(pt_v[...], a_v[:, at_gens:], preferred_element_type=f32)

    def pull_own():
        own_v[:, :lines] = jnp.dot(
            pt_v[...], a_v[:, at_own:at_gens], preferred_element_type=f32
        )

    def set_pt(ref):
        for b in range(bb):
            pt_v[:, b * blk : (b + 1) * blk] = ref[b * blk : (b + 1) * blk, :].astype(bf16).T

    def row(ref, n):
        return jnp.concatenate([ref[i : i + 1, :] for i in range(n)], axis=1) if n > 1 else ref[...]

    def gen_pull(it):
        grad = row(caps_v.at[0], n_gens) - own_v[:, lines:] + dual_s[it]
        own_v[:, lines:] = grad
        v_send[it, 0] = grad[cols - scen :]
        if it == 0:
            v_send[it, 1] = gen_s[it][cols - scen :]
        prev_copy(it).start()

    def clipped(now, sp, grad):
        return jnp.minimum(jnp.maximum(now - sp * grad, 0.0), row(caps_v.at[1], n_gens))

    def gen_step(it, sp):
        dual_copy(it).wait_recv()
        nxt = d_recv[it]
        later = nxt if cols == scen else jnp.concatenate([dual_s[it][scen:], nxt], axis=0)
        gnow = gen_s[it]
        gnew = clipped(gnow, sp, own_v[:, lines:] - later)
        gbar = 2.0 * gnew - gnow
        gen_s[it + 1] = gnew
        genlow_v[...] = gbar.astype(bf16)
        return (gnew - gnow) ** 2, gbar

    def prev_bar(it, sp):
        now = v_recv[it, 1] if it == 0 else prev_v[...]
        new = clipped(now, sp, v_recv[it, 0] - dual_s[it][:scen])
        prev_v[...] = new
        return 2.0 * new - now

    def near_arrived(it):
        @pl.when(has[NEAR])
        def _():
            near_part(it).wait_recv()

    def total_at(it, ch):
        @pl.when(has[FAR])
        def _():
            far_part(it, ch).wait_recv()

        lo = ch * cw
        return own_v[:, lo : lo + cw] + part_recv[it, NEAR, ch] + part_recv[it, FAR, ch]

    per = cw // blk

    def caps_of(ch):
        return jnp.concatenate(
            [fcap_v[ch * per + i : ch * per + i + 1, :] for i in range(per)], axis=1
        )

    def stepped(now, sp, total, cap):
        return jnp.minimum(jnp.maximum(now + sp * total, -cap), cap)

    def flow_step(it, ch, sp, total):
        lo = ch * cw
        now = flow_s[it, :, lo : lo + cw]
        new = stepped(now, sp, total, caps_of(ch))
        fw_own[it, ch] = (2.0 * new - now).astype(bf16)

        if ch < nch - (known, early)[it]:
            @pl.when(has[FAR])
            def _():
                far_flow(it, ch).start()

        flow_s[it + 1, :, lo : lo + cw] = new
        return (new - now) ** 2

    def put_state(ref, it, ch):
        ref[:cols] = flow_s[it, :, ch * cw : (ch + 1) * cw]
        ref[cols:] = jnp.broadcast_to(caps_of(ch), (8, cw))

    def ahead_start(it):
        count = (known, early)[it]
        for s in range(count):
            lo = (nch - count + s) * cw
            ahead_send[it, s * cols : (s + 1) * cols] = (
                own_v[:, lo : lo + cw] + part_recv[it, NEAR, nch - count + s]
            )
        if it == 0:
            put_state(ahead_send.at[0, pl.ds(cols, cols + 8)], 0, nch - 1)

        @pl.when(has[FAR])
        def _():
            if it == 1:
                (state_copy() if early > known else ahead_copy(0)).wait_send()
            ahead_copy(it).start()

    def state_start():
        for s in range(early - known):
            put_state(state_send.at[s], 1, nch - early + s)

        @pl.when(has[FAR])
        def _():
            ahead_copy(0).wait_send()
            state_copy().start()

    def ahead_low(it, sp, ch):
        count = (known, early)[it]
        s = ch - (nch - count)
        total = ahead_recv[it, s * cols : (s + 1) * cols] + part_send[it, FAR, ch]
        if it == 0 or ch >= nch - known:
            now = far_new[...] if it == 1 else ahead_recv[0, cols : 2 * cols]
            cap = ahead_recv[0, 2 * cols : 2 * cols + 1]
        else:
            now, cap = state_recv[s, :cols], state_recv[s, cols : cols + 1]
        new = stepped(now, sp, total, cap)
        if it == 0:
            far_new[...] = new
        return (2.0 * new - now).astype(bf16)

    def send_near(it):
        @pl.when(has[NEAR])
        def _():
            near_flow(it).start()

    nt_dims = (((1,), (1,)), ((), ()))

    def joined(get, n):
        return jnp.concatenate([get(ch) for ch in range(n)], axis=1) if n > 1 else get(0)

    def push_own(it):
        mine = jnp.concatenate([fw_own[it, ch] for ch in range(nch)] + [genlow_v[...]], axis=1)
        acc_v[...] = lax.dot_general(a_v[:, at_own:], mine, nt_dims, preferred_element_type=f32)

    def push_near(it):
        @pl.when(has[NEAR])
        def _():
            near_flow(it).wait_recv()

        other = joined(lambda ch: fw_in[it, NEAR, ch], nch)
        acc_v[...] += lax.dot_general(
            a_v[:, at_near:at_own], other, nt_dims, preferred_element_type=f32
        )

    def push_far(it, sp, chunks):
        lows = []
        for ch in chunks:
            if ch >= nch - (known, early)[it]:
                lows.append(ahead_low(it, sp, ch))
            else:
                far_flow(it, ch).wait_recv()
                lows.append(fw_in[it, FAR, ch])
        wide = [a_v[:, ch * cw : (ch + 1) * cw] for ch in chunks]
        many = len(chunks) > 1
        return lax.dot_general(
            jnp.concatenate(wide, axis=1) if many else wide[0],
            jnp.concatenate(lows, axis=1) if many else lows[0],
            nt_dims, preferred_element_type=f32,
        )

    def push(it, sp, meanwhile, finish):
        count = (known, early)[it]
        more = max(nch // 2 - count, 0)
        first = [*range(nch - count, nch), *range(more)]
        last = [*range(more, nch - count)]
        if it == 0 and early > known:
            state_start()
        push_own(it)
        if it == 1:
            meanwhile()
        if count > 0:
            @pl.when(has[FAR])
            def _():
                ahead_copy(it).wait_recv()
                if it == 1 and early > known:
                    state_copy().wait_recv()
                acc_v[...] += push_far(it, sp, first)

        push_near(it)
        if it == 0:
            meanwhile()

        @pl.when(has[FAR])
        def _():
            finish(acc_v[...] + push_far(it, sp, last))

        @pl.when(jnp.logical_not(has[FAR]))
        def _():
            finish(acc_v[...])

    def ramp_step(it, gbar, prev, sd):
        earlier = prev if cols == scen else jnp.concatenate([prev, gbar[: cols - scen]], axis=0)
        dual = dual_s[it]
        lifted = dual + sd * (gbar - earlier)
        bound = row(caps_v.at[2], n_gens)
        return lifted - sd * jnp.minimum(jnp.maximum(lifted / sd, -bound), bound)

    zero_at = n_tiles + n_gens
    arrived(0, idx_v)
    slot = idx_v[0] * width + (idx_v[1] - (r - 1) * lb)
    down = lax.broadcasted_iota(jnp.int32, (n_tiles, n_tiles), 0)
    across = lax.broadcasted_iota(jnp.int32, (n_tiles, n_tiles), 1)
    upright = jnp.sum(jnp.where(down == across, slot, 0), axis=1, keepdims=True)
    places = lax.broadcasted_iota(jnp.int32, (n_tiles, 128), 1)
    ids = lax.broadcasted_iota(jnp.int32, (n_tiles, 128), 0)
    found = jnp.sum(jnp.where(upright == places, ids - zero_at, 0), axis=0, keepdims=True)
    lane = lax.broadcasted_iota(jnp.int32, (1, 128), 1)
    for g in range(n_gens):
        found = jnp.where(lane == gen_bus[g] * width + 3 * lb + g, n_tiles + g - zero_at, found)
    table_v[...] = jnp.clip(zero_at + found, 0, zero_at)
    to_scalar = pltpu.make_async_copy(table_v, table_s, in_sem.at[0])
    to_scalar.start()

    w1 = jnp.full((1, 1), weight[...], f32)
    arrived(1, first_v)
    set_pt(price_v)
    dual_s[0] = ramp_v[...].T
    d_send[0] = dual_s[0][:scen]
    arrived(2, all_tiles)
    to_scalar.wait()
    build(FAR)
    pl.semaphore_wait(barrier, nt - 1 + count[FAR] + count[NEAR])
    if n_stages > 0:
        stage_signal(0)
    dual_copy(0).start()
    for ch in range(0, nch, per_dot):
        far_sums(0, ch)
        send_far(0, ch)
    late_loads()
    build(NEAR)
    pull_near(0)
    build(3)
    pull_gens()
    arrived(0, late_v)
    arrived(1, caps_v)
    gen_s[0] = gen_v[...].T
    gen_pull(0)
    pass_on(0)
    build(2)
    pull_own()
    sd1 = step_scale * w1
    sp1 = step_scale / w1
    for b in range(lb):
        flow_s[0, :, b * blk : (b + 1) * blk] = flow_v[b * blk : (b + 1) * blk, :].T
    arrived(2, fcap_v)
    near_arrived(0)
    if early > 0:
        ahead_start(0)
    primal_acc = jnp.zeros((8, 128), f32)
    for ch in range(nch):
        primal_acc = primal_acc + fold(flow_step(0, ch, sp1, total_at(0, ch)))
        if ch == 0:
            pass_on(1)
    send_near(0)
    for stage in range(2, n_stages - 1):
        pass_on(stage)
    changed, gbar1 = gen_step(0, sp1)
    primal_acc = primal_acc + fold(changed)
    low = lax.broadcasted_iota(jnp.int32, (1, 128), 1) < 64
    primal_row = both_halves(primal_acc)

    def ramp_now():
        prev_copy(0).wait_recv()
        dual_one = ramp_step(0, gbar1, prev_bar(0, sp1), sd1)
        dual_s[1] = dual_one
        change_v[...] = fold((dual_one - dual_s[0]) ** 2)
        dual_copy(0).wait_send()
        d_send[1] = dual_one[:scen]
        dual_copy(1).start()

    def price_now(pushed):
        new = price_v[...] + sd1 * (demand_v[...] - pushed)
        price1_v[...] = new
        dual_row = both_halves(change_v[...] + fold((new - price_v[...]) ** 2))
        ar_s[...] = jnp.where(low, primal_row, dual_row)

    push(0, sp1, ramp_now, price_now)

    if n_stages > 0:
        stage_wait(n_stages - 1)
    sent(0)
    others_t = partners(t, nt) + [(0, t)]
    others_r = partners(r, nr) + [(0, r)]
    for k, to_r in others_r:
        for j, to_t in others_t:
            if j or k:
                pltpu.make_async_remote_copy(
                    src_ref=ar_s,
                    dst_ref=ar_r.at[j * nr + k],
                    send_sem=ar_sem.at[0],
                    recv_sem=ar_sem.at[1],
                    device_id={"tm": to_t, "region": to_r},
                    device_id_type=MESH,
                ).start()
    others = ar_r.at[pl.ds(1, nt * nr - 1)]
    set_pt(price1_v)
    for ch in range(0, nch, per_dot):
        far_sums(1, ch)
        send_far(1, ch)
    pull_near(1)
    pull_gens()
    prev_copy(0).wait_send()
    gen_pull(1)
    pull_own()
    near_arrived(1)
    if early > 0:
        ahead_start(1)
    pltpu.make_async_copy(others, others, ar_sem.at[1]).wait()
    summed = ar_s[...]
    for at in range(1, nt * nr):
        summed = summed + ar_r[at]
    primal_mean = jnp.sum(jnp.where(low, summed, 0.0), axis=1, keepdims=True) / count_p
    dual_mean = jnp.sum(jnp.where(low, 0.0, summed), axis=1, keepdims=True) / count_d
    w2 = jnp.sqrt(w1 * jnp.sqrt((dual_mean + tiny) / (primal_mean + tiny)))

    sd2 = step_scale * w2
    sp2 = step_scale / w2
    for ch in range(nch):
        flow_step(1, ch, sp2, total_at(1, ch))
    send_near(1)
    _, gbar2 = gen_step(1, sp2)

    def results():
        prev_copy(1).wait_recv()
        o_ramp[...] = ramp_step(1, gbar2, prev_bar(1, sp2), sd2).T
        for b in range(lb):
            o_flow[b * blk : (b + 1) * blk, :] = flow_s[2, :, b * blk : (b + 1) * blk].T
        o_gen[...] = gen_s[2].T

    def price_out(pushed):
        o_price[...] = price1_v[...] + sd2 * (demand_v[...] - pushed)

    push(1, sp2, results, price_out)

    dual_copy(1).wait_send()
    prev_copy(1).wait_send()
    sent(1)
    if early > 0:
        @pl.when(has[FAR])
        def _():
            ahead_copy(1).wait_send()

    pltpu.make_async_copy(others, others, ar_sem.at[0]).wait()


def shards(
    gen, flow, price, ramp_dual, demand, incid_tiles, tile_bus, tile_line, gen_tiles, gen_bus,
    gen_cost, gen_cap, ramp_cap, flow_cap, weight,
):
    gb, blk, hours, scen = gen.shape
    lb, bb = flow.shape[0], price.shape[0]
    n_tiles = incid_tiles.shape[0]
    cols = hours * scen
    nt, nr = lax.axis_size("tm"), lax.axis_size("region")
    lines, buses, gens = lb * blk, bb * blk, gb * blk
    width = 3 * lb + gb
    nch = lb
    early = nch // 2
    ahead_rows = max(2 * cols + 8, early * cols)
    cw = lines // nch
    n_stages, reach = 0, 0
    while reach < nr - 1:
        reach += 2**n_stages
        n_stages += 1

    dims = (
        nt, nr, scen,
        float((gen.size + flow.size) * nt * nr), float((price.size + ramp_dual.size) * nt * nr), early,
    )
    any_spec = pl.BlockSpec(memory_space=pl.ANY)
    smem_spec = pl.BlockSpec(memory_space=pltpu.SMEM)
    dma = pltpu.SemaphoreType.DMA
    V = pltpu.VMEM
    scratch = [
        V((n_tiles + gb + 1, blk, blk), bf16),
        V((buses, width * blk), bf16),
        V((buses + gens, cols), f32),
        V((lines + buses + gens, cols), f32),
        V((3, gb, blk), f32),
        V((lb, blk), f32),
        V((cols, buses), bf16),
        V((cols, lines + gens), f32),
        V((buses, cols), f32),
        V((3, cols, lines), f32),
        V((3, cols, gens), f32),
        V((2, cols, gens), f32),
        V((cols, gens), bf16),
        V((2, 2, nch, cols, cw), f32),
        V((2, 2, nch, cols, cw), f32),
        V((2, nch, cols, cw), bf16),
        V((2, 2, nch, cols, cw), bf16),
        V((2, scen, gens), f32),
        V((2, scen, gens), f32),
        V((2, 2, scen, gens), f32),
        V((2, 2, scen, gens), f32),
        V((scen, gens), f32),
        V((2, ahead_rows, cw), f32),
        V((2, ahead_rows, cw), f32),
        V((max(early - 1, 1), cols + 8, cw), f32),
        V((max(early - 1, 1), cols + 8, cw), f32),
        V((cols, cw), f32),
        V((1, 128), f32),
        V((nt * nr, 1, 128), f32),
        V((buses, cols), f32),
        V((8, 128), f32),
        V((2, 1, n_tiles), jnp.int32),
        V((1, 128), jnp.int32),
        pltpu.SMEM((1, 128), jnp.int32),
        dma((3,)),
        dma((2,)),
        dma((nch + 2,)),
        dma((2,)),
        dma((nch + 1,)),
        dma((6,)),
        dma((2,)),
        dma((4,)),
        pltpu.SemaphoreType.REGULAR((n_stages,)),
    ]
    vmem_spec = pl.BlockSpec(memory_space=pltpu.VMEM)
    shapes = ((gens, cols), (lines, cols), (buses, cols), (gens, cols))
    outs = pl.pallas_call(
        functools.partial(kernel, dims),
        out_shape=tuple(V(shape, f32) for shape in shapes),
        in_specs=[smem_spec, smem_spec] + [any_spec] * 13,
        out_specs=(vmem_spec,) * 4,
        scratch_shapes=scratch,
        compiler_params=pltpu.CompilerParams(collective_id=0, has_side_effects=True),
    )(
        gen_bus, weight, tile_bus.reshape(1, n_tiles), tile_line.reshape(1, n_tiles), incid_tiles, gen_tiles,
        price.reshape(buses, cols), flow.reshape(lines, cols), gen.reshape(gens, cols),
        ramp_dual.reshape(gens, cols), demand.reshape(buses, cols),
        gen_cost, gen_cap, ramp_cap, flow_cap,
    )
    outs = pl.pallas_call(
        writer,
        out_shape=tuple(jax.ShapeDtypeStruct(shape, f32) for shape in shapes),
        in_specs=[any_spec] * 4,
        out_specs=(any_spec,) * 4,
        scratch_shapes=[dma((4,))],
    )(*(pltpu.with_memory_space_constraint(out, pltpu.VMEM) for out in outs))
    return tuple(
        out.reshape(like.shape) for out, like in zip(outs, (gen, flow, price, ramp_dual))
    )


def solution(mesh):
    field = P("region", None, "tm", None)
    placed = (
        field, field, field, field, field,
        P("region", None, None), P("region"), P("region"), P("region", None, None), P("region"),
        P("region", None), P("region", None), P("region", None), P("region", None), P(),
    )
    return jax.shard_map(
        shards, mesh=mesh, in_specs=placed, out_specs=(field,) * 4, check_vma=False
    )
```

```python
import functools

import jax
import jax.numpy as jnp
from jax import lax
from jax.experimental import pallas as pl
from jax.experimental.pallas import tpu as pltpu
from jax.sharding import PartitionSpec as P

MESH = pl.DeviceIdType.MESH
step_scale = 0.4
tiny = 1e-06
f32 = jnp.float32
bf16 = jnp.bfloat16


def remote(src, dst, send_sem, recv_sem, axis, peer):
    return pltpu.make_async_remote_copy(
        src_ref=src,
        dst_ref=dst,
        send_sem=send_sem,
        recv_sem=recv_sem,
        device_id={axis: peer},
        device_id_type=MESH,
    )


def fold(x):
    rows, columns = x.shape
    y = jnp.sum(x.reshape(rows // 8, 8, columns), axis=0)
    out = y[:, :128]
    for at in range(128, columns, 128):
        out = out + y[:, at : at + 128]
    return out


def both_halves(x):
    row = jnp.sum(x, axis=0, keepdims=True)
    return row + pltpu.roll(row, 64, 1)


def writer(*refs):
    n = (len(refs) - 1) // 2
    copies = [pltpu.make_async_copy(refs[i], refs[n + i], refs[-1].at[i]) for i in range(n)]
    for c in copies:
        c.start()
    for c in copies:
        c.wait()


def flip(x, mask):
    bit = 1
    out = x
    while bit <= mask:
        if mask & bit:
            out = out + bit * (1 - 2 * lax.rem(x // bit, 2))
        bit *= 2
    return out


def partners(x, n):
    if n & (n - 1) == 0:
        return [(m, flip(x, m)) for m in [*range(n // 2, n), *range(n // 2 - 1, 0, -1)]]
    return [(m, lax.rem(x + m, n)) for m in range(1, n)]


FAR, NEAR = 0, 1


def kernel(
    dims,
    gen_bus, weight, tile_bus, tile_line, tiles, gtiles, price, flow, gen, ramp, demand, cost, gcap, rcap, fcap,
    o_gen, o_flow, o_price, o_ramp,
    tiles_v, a_v, first_v, late_v, caps_v, fcap_v,
    pt_v, own_v, price1_v, flow_s, gen_s, dual_s, genlow_v,
    part_send, part_recv, fw_own, fw_in, d_send, d_recv, v_send, v_recv, prev_v,
    ahead_send, ahead_recv, state_send, state_recv,
    ar_s, ar_r, acc_v, change_v, idx_v, table_v, table_s,
    in_sem, ps_sem, pr_sem, fs_sem, fr_sem, tm_sem, ar_sem, ahead_sem, ready,
):
    nt, nr, scen, count_p, count_d, early = dims
    t = lax.axis_index("tm")
    r = lax.axis_index("region")
    n_tiles, blk, _ = tiles.shape
    n_gens = gtiles.shape[0]
    lines, cols = flow.shape
    buses = price.shape[0]
    lb, bb = lines // blk, buses // blk
    width = 3 * lb + n_gens
    nch = part_send.shape[2]
    cw = lines // nch
    n_stages = ready.shape[0]
    known = min(early, 1)
    ahead_rows = (2 * cols + 8, early * cols)

    odd = lax.rem(r, 2)
    place = (r - 1 + 2 * odd, r + 1 - 2 * odd)
    has = tuple((p >= 0) & (p < nr) for p in place)
    peer = tuple(jnp.clip(p, 0, nr - 1) for p in place)
    count = tuple(jnp.where(h, 1, 0) for h in has)
    is_odd = odd == 1
    far_of = (has[FAR] & (odd == 0), has[FAR] & is_odd)
    first_window = (2 * lb * odd, 2 * lb * (1 - odd), lb)

    barrier = pltpu.get_barrier_semaphore()
    for side in (FAR, NEAR):
        @pl.when(has[side])
        def _():
            pl.semaphore_signal(
                barrier, inc=1, device_id={"region": peer[side]}, device_id_type=MESH
            )
    for k in range(1, nt):
        pl.semaphore_signal(
            barrier, inc=1, device_id={"tm": lax.rem(t + k, nt)}, device_id_type=MESH
        )

    def stage_signal(stage):
        step = 2**stage
        for to in (r - step, r + step):
            @pl.when((to >= 0) & (to < nr))
            def _():
                pl.semaphore_signal(
                    ready.at[stage], inc=1, device_id={"region": jnp.clip(to, 0, nr - 1)},
                    device_id_type=MESH,
                )

    def stage_wait(stage):
        step = 2**stage
        pl.semaphore_wait(
            ready.at[stage], jnp.where(r >= step, 1, 0) + jnp.where(r + step < nr, 1, 0)
        )

    def pass_on(stage):
        if stage < n_stages - 1:
            stage_wait(stage)
            stage_signal(stage + 1)

    def load(i, *pairs):
        copies = [pltpu.make_async_copy(src, dst, in_sem.at[i]) for src, dst in pairs]
        for c in copies:
            c.start()

    def arrived(i, ref):
        pltpu.make_async_copy(ref, ref, in_sem.at[i]).wait()

    load(0, (tile_bus, idx_v.at[0]), (tile_line, idx_v.at[1]))
    all_tiles = tiles_v.at[pl.ds(0, n_tiles + n_gens)]
    gens = gen.shape[0]
    price_v, ramp_v = first_v.at[pl.ds(0, buses)], first_v.at[pl.ds(buses, gens)]
    load(1, (price, price_v), (ramp, ramp_v))
    load(2, (tiles, tiles_v.at[pl.ds(0, n_tiles)]), (gtiles, tiles_v.at[pl.ds(n_tiles, n_gens)]))
    flow_v = late_v.at[pl.ds(0, lines)]
    demand_v = late_v.at[pl.ds(lines, buses)]
    gen_v = late_v.at[pl.ds(lines + buses, gens)]

    def late_loads():
        load(0, (flow, flow_v), (demand, demand_v), (gen, gen_v))
        load(1, (cost, caps_v.at[0]), (gcap, caps_v.at[1]), (rcap, caps_v.at[2]))
        load(2, (fcap, fcap_v))

    tiles_v[n_tiles + n_gens] = jnp.zeros((blk, blk), bf16)

    for side in (FAR, NEAR):
        @pl.when(jnp.logical_not(has[side]))
        def _():
            part_recv[:, side] = jnp.zeros_like(part_recv[:, side])
            fw_in[:, side] = jnp.zeros_like(fw_in[:, side])

    t_next, t_prev = lax.rem(t + 1, nt), lax.rem(t + nt - 1, nt)

    def far_part(it, ch):
        return remote(
            part_send.at[it, FAR, ch], part_recv.at[it, FAR, ch],
            ps_sem.at[FAR], pr_sem.at[nch + 1 if it == 1 and ch >= nch - known else ch],
            "region", peer[FAR],
        )

    def near_part(it):
        return remote(
            part_send.at[it, NEAR], part_recv.at[it, NEAR],
            ps_sem.at[NEAR], pr_sem.at[nch], "region", peer[NEAR],
        )

    def far_flow(it, ch):
        return remote(
            fw_own.at[it, ch], fw_in.at[it, FAR, ch],
            fs_sem.at[FAR], fr_sem.at[ch], "region", peer[FAR],
        )

    def near_flow(it):
        return remote(
            fw_own.at[it], fw_in.at[it, NEAR],
            fs_sem.at[NEAR], fr_sem.at[nch], "region", peer[NEAR],
        )

    def dual_copy(it):
        return remote(d_send.at[it], d_recv.at[it], tm_sem.at[0], tm_sem.at[2 + it], "tm", t_prev)

    def prev_copy(it):
        parts = pl.ds(0, 2 - it)
        return remote(
            v_send.at[it, parts], v_recv.at[it, parts], tm_sem.at[1], tm_sem.at[4 + it], "tm", t_next
        )

    def ahead_copy(it):
        rows = pl.ds(0, ahead_rows[it])
        return remote(
            ahead_send.at[it, rows], ahead_recv.at[it, rows],
            ahead_sem.at[0], ahead_sem.at[1 + it], "region", peer[FAR],
        )

    def state_copy(count):
        slots = pl.ds(0, count)
        return remote(
            state_send.at[slots], state_recv.at[slots], ahead_sem.at[0], ahead_sem.at[3],
            "region", peer[FAR],
        )

    def sent(it):
        for side in (FAR, NEAR):
            @pl.when(has[side])
            def _():
                ref = part_send.at[it, side]
                pltpu.make_async_copy(ref, ref, ps_sem.at[side]).wait()
                if it == 1 or side == NEAR:
                    ref = fw_own.at[it, pl.ds(0, nch - early if side == FAR else nch)]
                    pltpu.make_async_copy(ref, ref, fs_sem.at[side]).wait()
        if it == 0:
            for parity in (0, 1):
                @pl.when(far_of[parity])
                def _():
                    ref = fw_own.at[0, pl.ds(0, nch - parity * known)]
                    pltpu.make_async_copy(ref, ref, fs_sem.at[FAR]).wait()

    at_near, at_own, at_gens = lines, 2 * lines, 3 * lines

    def build(group):
        n = n_gens if group == 3 else lb
        for i in range(n):
            window = 3 * lb + i if group == 3 else first_window[group] + i
            lo = group * lines + i * blk
            for b in range(bb):
                a_v[b * blk : (b + 1) * blk, lo : lo + blk] = tiles_v[table_s[0, b * width + window]]

    per_dot = 2 if nch % 2 == 0 else 1

    def far_sums(it, ch):
        sums = jnp.dot(
            pt_v[...], a_v[:, ch * cw : (ch + per_dot) * cw], preferred_element_type=f32
        )
        for i in range(per_dot):
            part_send[it, FAR, ch + i] = sums[:, i * cw : (i + 1) * cw]

    def send_far(it, ch):
        @pl.when(has[FAR])
        def _():
            for i in range(per_dot):
                far_part(it, ch + i).start()

    def pull_near(it):
        for ch in range(0, nch, per_dot):
            at = at_near + ch * cw
            sums = jnp.dot(
                pt_v[...], a_v[:, at : at + per_dot * cw], preferred_element_type=f32
            )
            for i in range(per_dot):
                part_send[it, NEAR, ch + i] = sums[:, i * cw : (i + 1) * cw]

        @pl.when(has[NEAR])
        def _():
            near_part(it).start()

    def pull_gens():
        own_v[:, lines:] = jnp.dot(pt_v[...], a_v[:, at_gens:], preferred_element_type=f32)

    def pull_own():
        own_v[:, :lines] = jnp.dot(
            pt_v[...], a_v[:, at_own:at_gens], preferred_element_type=f32
        )

    def set_pt(ref):
        for b in range(bb):
            pt_v[:, b * blk : (b + 1) * blk] = ref[b * blk : (b + 1) * blk, :].astype(bf16).T

    def row(ref, n):
        return jnp.concatenate([ref[i : i + 1, :] for i in range(n)], axis=1) if n > 1 else ref[...]

    def gen_pull(it):
        grad = row(caps_v.at[0], n_gens) - own_v[:, lines:] + dual_s[it]
        own_v[:, lines:] = grad
        v_send[it, 0] = grad[cols - scen :]
        if it == 0:
            v_send[it, 1] = gen_s[it][cols - scen :]
        prev_copy(it).start()

    def clipped(now, sp, grad):
        return jnp.minimum(jnp.maximum(now - sp * grad, 0.0), row(caps_v.at[1], n_gens))

    def gen_step(it, sp):
        dual_copy(it).wait_recv()
        nxt = d_recv[it]
        later = nxt if cols == scen else jnp.concatenate([dual_s[it][scen:], nxt], axis=0)
        gnow = gen_s[it]
        gnew = clipped(gnow, sp, own_v[:, lines:] - later)
        gbar = 2.0 * gnew - gnow
        gen_s[it + 1] = gnew
        genlow_v[...] = gbar.astype(bf16)
        return (gnew - gnow) ** 2, gbar

    def prev_bar(it, sp):
        now = v_recv[it, 1] if it == 0 else prev_v[...]
        new = clipped(now, sp, v_recv[it, 0] - dual_s[it][:scen])
        prev_v[...] = new
        return 2.0 * new - now

    def near_arrived(it):
        @pl.when(has[NEAR])
        def _():
            near_part(it).wait_recv()

    def total_at(it, ch):
        @pl.when(has[FAR])
        def _():
            far_part(it, ch).wait_recv()

        lo = ch * cw
        return own_v[:, lo : lo + cw] + part_recv[it, NEAR, ch] + part_recv[it, FAR, ch]

    per = cw // blk

    def caps_of(ch):
        return jnp.concatenate(
            [fcap_v[ch * per + i : ch * per + i + 1, :] for i in range(per)], axis=1
        )

    def stepped(now, sp, total, cap):
        return jnp.minimum(jnp.maximum(now + sp * total, -cap), cap)

    def flow_step(it, ch, sp, total):
        lo = ch * cw
        now = flow_s[it, :, lo : lo + cw]
        new = stepped(now, sp, total, caps_of(ch))
        fw_own[it, ch] = (2.0 * new - now).astype(bf16)

        if ch < nch - (known, early)[it] or it == 0:
            @pl.when(has[FAR] if ch < nch - (known, early)[it] else far_of[0])
            def _():
                far_flow(it, ch).start()

        flow_s[it + 1, :, lo : lo + cw] = new
        return (new - now) ** 2

    def put_state(ref, it, ch):
        ref[:cols] = flow_s[it, :, ch * cw : (ch + 1) * cw]
        ref[cols:] = jnp.broadcast_to(caps_of(ch), (8, cw))

    def ahead_start(it):
        count = (known, early)[it]
        for s in range(count):
            lo = (nch - count + s) * cw
            ahead_send[it, s * cols : (s + 1) * cols] = (
                own_v[:, lo : lo + cw] + part_recv[it, NEAR, nch - count + s]
            )
        if it == 0:
            put_state(ahead_send.at[0, pl.ds(cols, cols + 8)], 0, nch - 1)

            @pl.when(far_of[1])
            def _():
                ahead_copy(0).start()
        else:
            for parity in (0, 1):
                @pl.when(far_of[parity])
                def _():
                    slots = early - parity * known
                    (state_copy(slots) if slots else ahead_copy(0)).wait_send()
                    ahead_copy(1).start()

    def state_start():
        for s in range(early):
            put_state(state_send.at[s], 1, nch - early + s)
        for parity in (0, 1):
            slots = early - parity * known
            if slots:
                @pl.when(far_of[parity])
                def _():
                    if parity == 1:
                        ahead_copy(0).wait_send()
                    state_copy(slots).start()

    def ahead_low(it, sp, ch):
        count = (known, early)[it]
        s = ch - (nch - count)
        total = ahead_recv[it, s * cols : (s + 1) * cols] + part_send[it, FAR, ch]
        if it == 0:
            now, cap = ahead_recv[0, cols : 2 * cols], ahead_recv[0, 2 * cols : 2 * cols + 1]
        else:
            now, cap = state_recv[s, :cols], state_recv[s, cols : cols + 1]
        new = stepped(now, sp, total, cap)
        if it == 0:
            state_recv[early - 1, :cols] = new
            state_recv[early - 1, cols:] = ahead_recv[0, 2 * cols :  2 * cols + 8]
        return (2.0 * new - now).astype(bf16)

    def send_near(it):
        @pl.when(has[NEAR])
        def _():
            near_flow(it).start()

    nt_dims = (((1,), (1,)), ((), ()))

    def joined(get, n):
        return jnp.concatenate([get(ch) for ch in range(n)], axis=1) if n > 1 else get(0)

    def push_own(it):
        mine = jnp.concatenate([fw_own[it, ch] for ch in range(nch)] + [genlow_v[...]], axis=1)
        acc_v[...] = lax.dot_general(a_v[:, at_own:], mine, nt_dims, preferred_element_type=f32)

    def push_near(it):
        @pl.when(has[NEAR])
        def _():
            near_flow(it).wait_recv()

        other = joined(lambda ch: fw_in[it, NEAR, ch], nch)
        acc_v[...] += lax.dot_general(
            a_v[:, at_near:at_own], other, nt_dims, preferred_element_type=f32
        )

    def push_far(it, sp, chunks, ahead):
        lows = []
        for ch in chunks:
            if ch in ahead:
                lows.append(ahead_low(it, sp, ch))
            else:
                far_flow(it, ch).wait_recv()
                lows.append(fw_in[it, FAR, ch])
        wide = [a_v[:, ch * cw : (ch + 1) * cw] for ch in chunks]
        many = len(chunks) > 1
        return lax.dot_general(
            jnp.concatenate(wide, axis=1) if many else wide[0],
            jnp.concatenate(lows, axis=1) if many else lows[0],
            nt_dims, preferred_element_type=f32,
        )

    def push(it, sp, meanwhile, finish):
        if it == 0 and early > 0:
            state_start()
        push_own(it)
        if it == 1:
            meanwhile()
        plans = []
        for parity in (0, 1):
            n = early if it == 1 else known * (1 - parity)
            more = max(nch // 2 - n, 0)
            plans.append(
                ([*range(nch - n, nch)], [*range(nch - n, nch), *range(more)], [*range(more, nch - n)])
            )

        def far_first(parity):
            ahead, first, _ = plans[parity]
            if first:
                @pl.when(far_of[parity])
                def _():
                    if ahead:
                        ahead_copy(it).wait_recv()
                    if it == 1 and early - (1 - parity) * known:
                        state_copy(early - (1 - parity) * known).wait_recv()
                    acc_v[...] += push_far(it, sp, first, ahead)

        far_first(0)
        if it == 1:
            far_first(1)
        push_near(it)
        if it == 0:
            far_first(1)
            meanwhile()

        for parity in (0, 1):
            @pl.when(far_of[parity])
            def _():
                ahead, _, last = plans[parity]
                finish(acc_v[...] + push_far(it, sp, last, ahead))

        @pl.when(jnp.logical_not(has[FAR]))
        def _():
            finish(acc_v[...])

    def ramp_step(it, gbar, prev, sd):
        earlier = prev if cols == scen else jnp.concatenate([prev, gbar[: cols - scen]], axis=0)
        dual = dual_s[it]
        lifted = dual + sd * (gbar - earlier)
        bound = row(caps_v.at[2], n_gens)
        return lifted - sd * jnp.minimum(jnp.maximum(lifted / sd, -bound), bound)

    zero_at = n_tiles + n_gens
    arrived(0, idx_v)
    slot = idx_v[0] * width + (idx_v[1] - (r - 1) * lb)
    down = lax.broadcasted_iota(jnp.int32, (n_tiles, n_tiles), 0)
    across = lax.broadcasted_iota(jnp.int32, (n_tiles, n_tiles), 1)
    upright = jnp.sum(jnp.where(down == across, slot, 0), axis=1, keepdims=True)
    places = lax.broadcasted_iota(jnp.int32, (n_tiles, 128), 1)
    ids = lax.broadcasted_iota(jnp.int32, (n_tiles, 128), 0)
    found = jnp.sum(jnp.where(upright == places, ids - zero_at, 0), axis=0, keepdims=True)
    lane = lax.broadcasted_iota(jnp.int32, (1, 128), 1)
    for g in range(n_gens):
        found = jnp.where(lane == gen_bus[g] * width + 3 * lb + g, n_tiles + g - zero_at, found)
    table_v[...] = jnp.clip(zero_at + found, 0, zero_at)
    to_scalar = pltpu.make_async_copy(table_v, table_s, in_sem.at[0])
    to_scalar.start()

    w1 = jnp.full((1, 1), weight[...], f32)
    arrived(1, first_v)
    set_pt(price_v)
    dual_s[0] = ramp_v[...].T
    d_send[0] = dual_s[0][:scen]
    arrived(2, all_tiles)
    to_scalar.wait()
    build(FAR)
    pl.semaphore_wait(barrier, nt - 1 + count[FAR] + count[NEAR])
    if n_stages > 0:
        stage_signal(0)
    dual_copy(0).start()
    for ch in range(0, nch, per_dot):
        far_sums(0, ch)
        send_far(0, ch)
    late_loads()
    build(NEAR)
    pull_near(0)
    build(3)
    pull_gens()
    arrived(0, late_v)
    arrived(1, caps_v)
    gen_s[0] = gen_v[...].T
    gen_pull(0)
    pass_on(0)
    build(2)
    pull_own()
    sd1 = step_scale * w1
    sp1 = step_scale / w1
    for b in range(lb):
        flow_s[0, :, b * blk : (b + 1) * blk] = flow_v[b * blk : (b + 1) * blk, :].T
    arrived(2, fcap_v)
    near_arrived(0)
    if early > 0:
        ahead_start(0)
    primal_acc = jnp.zeros((8, 128), f32)
    for ch in range(nch):
        primal_acc = primal_acc + fold(flow_step(0, ch, sp1, total_at(0, ch)))
        if ch == 0:
            pass_on(1)
    send_near(0)
    for stage in range(2, n_stages - 1):
        pass_on(stage)
    changed, gbar1 = gen_step(0, sp1)
    primal_acc = primal_acc + fold(changed)
    low = lax.broadcasted_iota(jnp.int32, (1, 128), 1) < 64
    primal_row = both_halves(primal_acc)

    def ramp_now():
        prev_copy(0).wait_recv()
        dual_one = ramp_step(0, gbar1, prev_bar(0, sp1), sd1)
        dual_s[1] = dual_one
        change_v[...] = fold((dual_one - dual_s[0]) ** 2)
        dual_copy(0).wait_send()
        d_send[1] = dual_one[:scen]
        dual_copy(1).start()

    def price_now(pushed):
        new = price_v[...] + sd1 * (demand_v[...] - pushed)
        price1_v[...] = new
        dual_row = both_halves(change_v[...] + fold((new - price_v[...]) ** 2))
        ar_s[...] = jnp.where(low, primal_row, dual_row)

    push(0, sp1, ramp_now, price_now)

    if n_stages > 0:
        stage_wait(n_stages - 1)
    sent(0)
    others_t = partners(t, nt) + [(0, t)]
    others_r = partners(r, nr) + [(0, r)]
    for k, to_r in others_r:
        for j, to_t in others_t:
            if j or k:
                pltpu.make_async_remote_copy(
                    src_ref=ar_s,
                    dst_ref=ar_r.at[j * nr + k],
                    send_sem=ar_sem.at[0],
                    recv_sem=ar_sem.at[1],
                    device_id={"tm": to_t, "region": to_r},
                    device_id_type=MESH,
                ).start()
    others = ar_r.at[pl.ds(1, nt * nr - 1)]
    set_pt(price1_v)
    for ch in range(0, nch, per_dot):
        far_sums(1, ch)
        send_far(1, ch)
    pull_near(1)
    pull_gens()
    prev_copy(0).wait_send()
    gen_pull(1)
    pull_own()
    near_arrived(1)
    if early > 0:
        ahead_start(1)
    pltpu.make_async_copy(others, others, ar_sem.at[1]).wait()
    summed = ar_s[...]
    for at in range(1, nt * nr):
        summed = summed + ar_r[at]
    primal_mean = jnp.sum(jnp.where(low, summed, 0.0), axis=1, keepdims=True) / count_p
    dual_mean = jnp.sum(jnp.where(low, 0.0, summed), axis=1, keepdims=True) / count_d
    w2 = jnp.sqrt(w1 * jnp.sqrt((dual_mean + tiny) / (primal_mean + tiny)))

    sd2 = step_scale * w2
    sp2 = step_scale / w2
    for ch in range(nch):
        flow_step(1, ch, sp2, total_at(1, ch))
    send_near(1)
    _, gbar2 = gen_step(1, sp2)

    def results():
        prev_copy(1).wait_recv()
        o_ramp[...] = ramp_step(1, gbar2, prev_bar(1, sp2), sd2).T
        for b in range(lb):
            o_flow[b * blk : (b + 1) * blk, :] = flow_s[2, :, b * blk : (b + 1) * blk].T
        o_gen[...] = gen_s[2].T

    def price_out(pushed):
        o_price[...] = price1_v[...] + sd2 * (demand_v[...] - pushed)

    push(1, sp2, results, price_out)

    dual_copy(1).wait_send()
    prev_copy(1).wait_send()
    sent(1)
    if early > 0:
        @pl.when(has[FAR])
        def _():
            ahead_copy(1).wait_send()

    pltpu.make_async_copy(others, others, ar_sem.at[0]).wait()


def shards(
    gen, flow, price, ramp_dual, demand, incid_tiles, tile_bus, tile_line, gen_tiles, gen_bus,
    gen_cost, gen_cap, ramp_cap, flow_cap, weight,
):
    gb, blk, hours, scen = gen.shape
    lb, bb = flow.shape[0], price.shape[0]
    n_tiles = incid_tiles.shape[0]
    cols = hours * scen
    nt, nr = lax.axis_size("tm"), lax.axis_size("region")
    lines, buses, gens = lb * blk, bb * blk, gb * blk
    width = 3 * lb + gb
    nch = lb
    early = nch // 2
    ahead_rows = max(2 * cols + 8, early * cols)
    cw = lines // nch
    n_stages, reach = 0, 0
    while reach < nr - 1:
        reach += 2**n_stages
        n_stages += 1

    dims = (
        nt, nr, scen,
        float((gen.size + flow.size) * nt * nr), float((price.size + ramp_dual.size) * nt * nr), early,
    )
    any_spec = pl.BlockSpec(memory_space=pl.ANY)
    smem_spec = pl.BlockSpec(memory_space=pltpu.SMEM)
    dma = pltpu.SemaphoreType.DMA
    V = pltpu.VMEM
    scratch = [
        V((n_tiles + gb + 1, blk, blk), bf16),
        V((buses, width * blk), bf16),
        V((buses + gens, cols), f32),
        V((lines + buses + gens, cols), f32),
        V((3, gb, blk), f32),
        V((lb, blk), f32),
        V((cols, buses), bf16),
        V((cols, lines + gens), f32),
        V((buses, cols), f32),
        V((3, cols, lines), f32),
        V((3, cols, gens), f32),
        V((2, cols, gens), f32),
        V((cols, gens), bf16),
        V((2, 2, nch, cols, cw), f32),
        V((2, 2, nch, cols, cw), f32),
        V((2, nch, cols, cw), bf16),
        V((2, 2, nch, cols, cw), bf16),
        V((2, scen, gens), f32),
        V((2, scen, gens), f32),
        V((2, 2, scen, gens), f32),
        V((2, 2, scen, gens), f32),
        V((scen, gens), f32),
        V((2, ahead_rows, cw), f32),
        V((2, ahead_rows, cw), f32),
        V((max(early, 1), cols + 8, cw), f32),
        V((max(early, 1), cols + 8, cw), f32),
        V((1, 128), f32),
        V((nt * nr, 1, 128), f32),
        V((buses, cols), f32),
        V((8, 128), f32),
        V((2, 1, n_tiles), jnp.int32),
        V((1, 128), jnp.int32),
        pltpu.SMEM((1, 128), jnp.int32),
        dma((3,)),
        dma((2,)),
        dma((nch + 2,)),
        dma((2,)),
        dma((nch + 1,)),
        dma((6,)),
        dma((2,)),
        dma((4,)),
        pltpu.SemaphoreType.REGULAR((n_stages,)),
    ]
    vmem_spec = pl.BlockSpec(memory_space=pltpu.VMEM)
    shapes = ((gens, cols), (lines, cols), (buses, cols), (gens, cols))
    outs = pl.pallas_call(
        functools.partial(kernel, dims),
        out_shape=tuple(V(shape, f32) for shape in shapes),
        in_specs=[smem_spec, smem_spec] + [any_spec] * 13,
        out_specs=(vmem_spec,) * 4,
        scratch_shapes=scratch,
        compiler_params=pltpu.CompilerParams(collective_id=0, has_side_effects=True),
    )(
        gen_bus, weight, tile_bus.reshape(1, n_tiles), tile_line.reshape(1, n_tiles), incid_tiles, gen_tiles,
        price.reshape(buses, cols), flow.reshape(lines, cols), gen.reshape(gens, cols),
        ramp_dual.reshape(gens, cols), demand.reshape(buses, cols),
        gen_cost, gen_cap, ramp_cap, flow_cap,
    )
    outs = pl.pallas_call(
        writer,
        out_shape=tuple(jax.ShapeDtypeStruct(shape, f32) for shape in shapes),
        in_specs=[any_spec] * 4,
        out_specs=(any_spec,) * 4,
        scratch_shapes=[dma((4,))],
    )(*(pltpu.with_memory_space_constraint(out, pltpu.VMEM) for out in outs))
    return tuple(
        out.reshape(like.shape) for out, like in zip(outs, (gen, flow, price, ramp_dual))
    )


def solution(mesh):
    field = P("region", None, "tm", None)
    placed = (
        field, field, field, field, field,
        P("region", None, None), P("region"), P("region"), P("region", None, None), P("region"),
        P("region", None), P("region", None), P("region", None), P("region", None), P(),
    )
    return jax.shard_map(
        shards, mesh=mesh, in_specs=placed, out_specs=(field,) * 4, check_vma=False
    )
```

```python
import functools

import jax
import jax.numpy as jnp
from jax import lax
from jax.experimental import pallas as pl
from jax.experimental.pallas import tpu as pltpu
from jax.sharding import PartitionSpec as P

MESH = pl.DeviceIdType.MESH
step_scale = 0.4
tiny = 1e-06
f32 = jnp.float32
bf16 = jnp.bfloat16


def remote(src, dst, send_sem, recv_sem, axis, peer):
    return pltpu.make_async_remote_copy(
        src_ref=src,
        dst_ref=dst,
        send_sem=send_sem,
        recv_sem=recv_sem,
        device_id={axis: peer},
        device_id_type=MESH,
    )


def fold(x):
    rows, columns = x.shape
    y = jnp.sum(x.reshape(rows // 8, 8, columns), axis=0)
    out = y[:, :128]
    for at in range(128, columns, 128):
        out = out + y[:, at : at + 128]
    return out


def both_halves(x):
    row = jnp.sum(x, axis=0, keepdims=True)
    return row + pltpu.roll(row, 64, 1)


def writer(*refs):
    n = (len(refs) - 1) // 2
    copies = [pltpu.make_async_copy(refs[i], refs[n + i], refs[-1].at[i]) for i in range(n)]
    for c in copies:
        c.start()
    for c in copies:
        c.wait()


def flip(x, mask):
    bit = 1
    out = x
    while bit <= mask:
        if mask & bit:
            out = out + bit * (1 - 2 * lax.rem(x // bit, 2))
        bit *= 2
    return out


def partners(x, n):
    if n & (n - 1) == 0:
        return [(m, flip(x, m)) for m in [*range(n // 2, n), *range(n // 2 - 1, 0, -1)]]
    return [(m, lax.rem(x + m, n)) for m in range(1, n)]


FAR, NEAR = 0, 1


def kernel(
    dims,
    gen_bus, weight, tile_bus, tile_line, tiles, gtiles, price, flow, gen, ramp, demand, cost, gcap, rcap, fcap,
    o_gen, o_flow, o_price, o_ramp,
    tiles_v, a_v, first_v, late_v, caps_v, fcap_v,
    pt_v, own_v, price1_v, flow_s, gen_s, dual_s, genlow_v,
    part_send, part_recv, fw_own, fw_in, d_send, d_recv, v_send, v_recv, prev_v,
    ahead_send, ahead_recv, state_send, state_recv,
    ar_s, ar_r, acc_v, change_v, idx_v, table_v, table_s,
    in_sem, ps_sem, pr_sem, fs_sem, fr_sem, tm_sem, ar_sem, ahead_sem, ready,
):
    nt, nr, scen, count_p, count_d, early = dims
    t = lax.axis_index("tm")
    r = lax.axis_index("region")
    n_tiles, blk, _ = tiles.shape
    n_gens = gtiles.shape[0]
    lines, cols = flow.shape
    buses = price.shape[0]
    lb, bb = lines // blk, buses // blk
    width = 3 * lb + n_gens
    nch = part_send.shape[2]
    cw = lines // nch
    n_stages = ready.shape[0]
    known = min(early, 1)
    ahead_rows = (2 * cols + 8, early * cols)

    odd = lax.rem(r, 2)
    place = (r - 1 + 2 * odd, r + 1 - 2 * odd)
    has = tuple((p >= 0) & (p < nr) for p in place)
    peer = tuple(jnp.clip(p, 0, nr - 1) for p in place)
    count = tuple(jnp.where(h, 1, 0) for h in has)
    is_odd = odd == 1
    far_of = (has[FAR] & (odd == 0), has[FAR] & is_odd)
    first_window = (2 * lb * odd, 2 * lb * (1 - odd), lb)

    barrier = pltpu.get_barrier_semaphore()
    for side in (FAR, NEAR):
        @pl.when(has[side])
        def _():
            pl.semaphore_signal(
                barrier, inc=1, device_id={"region": peer[side]}, device_id_type=MESH
            )
    for k in range(1, nt):
        pl.semaphore_signal(
            barrier, inc=1, device_id={"tm": lax.rem(t + k, nt)}, device_id_type=MESH
        )

    def stage_signal(stage):
        step = 2**stage
        for to in (r - step, r + step):
            @pl.when((to >= 0) & (to < nr))
            def _():
                pl.semaphore_signal(
                    ready.at[stage], inc=1, device_id={"region": jnp.clip(to, 0, nr - 1)},
                    device_id_type=MESH,
                )

    def stage_wait(stage):
        step = 2**stage
        pl.semaphore_wait(
            ready.at[stage], jnp.where(r >= step, 1, 0) + jnp.where(r + step < nr, 1, 0)
        )

    def pass_on(stage):
        if stage < n_stages - 1:
            stage_wait(stage)
            stage_signal(stage + 1)

    def load(i, *pairs):
        copies = [pltpu.make_async_copy(src, dst, in_sem.at[i]) for src, dst in pairs]
        for c in copies:
            c.start()

    def arrived(i, ref):
        pltpu.make_async_copy(ref, ref, in_sem.at[i]).wait()

    load(0, (tile_bus, idx_v.at[0]), (tile_line, idx_v.at[1]))
    all_tiles = tiles_v.at[pl.ds(0, n_tiles + n_gens)]
    gens = gen.shape[0]
    price_v, ramp_v = first_v.at[pl.ds(0, buses)], first_v.at[pl.ds(buses, gens)]
    load(1, (price, price_v), (ramp, ramp_v))
    load(2, (tiles, tiles_v.at[pl.ds(0, n_tiles)]), (gtiles, tiles_v.at[pl.ds(n_tiles, n_gens)]))
    flow_v = late_v.at[pl.ds(0, lines)]
    demand_v = late_v.at[pl.ds(lines, buses)]
    gen_v = late_v.at[pl.ds(lines + buses, gens)]

    def late_loads():
        load(0, (flow, flow_v), (demand, demand_v), (gen, gen_v))
        load(1, (cost, caps_v.at[0]), (gcap, caps_v.at[1]), (rcap, caps_v.at[2]))
        load(2, (fcap, fcap_v))

    tiles_v[n_tiles + n_gens] = jnp.zeros((blk, blk), bf16)

    for side in (FAR, NEAR):
        @pl.when(jnp.logical_not(has[side]))
        def _():
            part_recv[:, side] = jnp.zeros_like(part_recv[:, side])
            fw_in[:, side] = jnp.zeros_like(fw_in[:, side])

    t_next, t_prev = lax.rem(t + 1, nt), lax.rem(t + nt - 1, nt)

    def far_part(it, ch):
        return remote(
            part_send.at[it, FAR, ch], part_recv.at[it, FAR, ch],
            ps_sem.at[FAR], pr_sem.at[nch + 1 if it == 1 and ch >= nch - known else ch],
            "region", peer[FAR],
        )

    def near_part(it):
        return remote(
            part_send.at[it, NEAR], part_recv.at[it, NEAR],
            ps_sem.at[NEAR], pr_sem.at[nch], "region", peer[NEAR],
        )

    def far_flow(it, ch):
        return remote(
            fw_own.at[it, ch], fw_in.at[it, FAR, ch],
            fs_sem.at[FAR], fr_sem.at[ch], "region", peer[FAR],
        )

    def near_flow(it):
        return remote(
            fw_own.at[it], fw_in.at[it, NEAR],
            fs_sem.at[NEAR], fr_sem.at[nch], "region", peer[NEAR],
        )

    def dual_copy(it):
        return remote(d_send.at[it], d_recv.at[it], tm_sem.at[0], tm_sem.at[2 + it], "tm", t_prev)

    def prev_copy(it):
        parts = pl.ds(0, 2 - it)
        return remote(
            v_send.at[it, parts], v_recv.at[it, parts], tm_sem.at[1], tm_sem.at[4 + it], "tm", t_next
        )

    def ahead_copy(it):
        rows = pl.ds(0, ahead_rows[it])
        return remote(
            ahead_send.at[it, rows], ahead_recv.at[it, rows],
            ahead_sem.at[0], ahead_sem.at[1 + it], "region", peer[FAR],
        )

    def state_copy(count):
        slots = pl.ds(0, count)
        return remote(
            state_send.at[slots], state_recv.at[slots], ahead_sem.at[0], ahead_sem.at[3],
            "region", peer[FAR],
        )

    def sent(it):
        for side in (FAR, NEAR):
            @pl.when(has[side])
            def _():
                ref = part_send.at[it, side]
                pltpu.make_async_copy(ref, ref, ps_sem.at[side]).wait()
                if it == 1 or side == NEAR:
                    ref = fw_own.at[it, pl.ds(0, nch - early if side == FAR else nch)]
                    pltpu.make_async_copy(ref, ref, fs_sem.at[side]).wait()
        if it == 0:
            for parity in (0, 1):
                @pl.when(far_of[parity])
                def _():
                    ref = fw_own.at[0, pl.ds(0, nch - parity * known)]
                    pltpu.make_async_copy(ref, ref, fs_sem.at[FAR]).wait()

    at_near, at_own, at_gens = lines, 2 * lines, 3 * lines

    def build(group):
        n = n_gens if group == 3 else lb
        for i in range(n):
            window = 3 * lb + i if group == 3 else first_window[group] + i
            lo = group * lines + i * blk
            for b in range(bb):
                a_v[b * blk : (b + 1) * blk, lo : lo + blk] = tiles_v[table_s[0, b * width + window]]

    per_dot = 2 if nch % 2 == 0 else 1

    def far_sums(it, ch):
        sums = jnp.dot(
            pt_v[...], a_v[:, ch * cw : (ch + per_dot) * cw], preferred_element_type=f32
        )
        for i in range(per_dot):
            part_send[it, FAR, ch + i] = sums[:, i * cw : (i + 1) * cw]

    def send_far(it, ch):
        @pl.when(has[FAR])
        def _():
            for i in range(per_dot):
                far_part(it, ch + i).start()

    def pull_near(it):
        for ch in range(0, nch, per_dot):
            at = at_near + ch * cw
            sums = jnp.dot(
                pt_v[...], a_v[:, at : at + per_dot * cw], preferred_element_type=f32
            )
            for i in range(per_dot):
                part_send[it, NEAR, ch + i] = sums[:, i * cw : (i + 1) * cw]

        @pl.when(has[NEAR])
        def _():
            near_part(it).start()

    def pull_gens():
        own_v[:, lines:] = jnp.dot(pt_v[...], a_v[:, at_gens:], preferred_element_type=f32)

    def pull_own():
        own_v[:, :lines] = jnp.dot(
            pt_v[...], a_v[:, at_own:at_gens], preferred_element_type=f32
        )

    def set_pt(ref):
        for b in range(bb):
            pt_v[:, b * blk : (b + 1) * blk] = ref[b * blk : (b + 1) * blk, :].astype(bf16).T

    def row(ref, n):
        return jnp.concatenate([ref[i : i + 1, :] for i in range(n)], axis=1) if n > 1 else ref[...]

    def gen_pull(it):
        grad = row(caps_v.at[0], n_gens) - own_v[:, lines:] + dual_s[it]
        own_v[:, lines:] = grad
        v_send[it, 0] = grad[cols - scen :]
        if it == 0:
            v_send[it, 1] = gen_s[it][cols - scen :]
        prev_copy(it).start()

    def clipped(now, sp, grad):
        return jnp.minimum(jnp.maximum(now - sp * grad, 0.0), row(caps_v.at[1], n_gens))

    def gen_step(it, sp):
        dual_copy(it).wait_recv()
        nxt = d_recv[it]
        later = nxt if cols == scen else jnp.concatenate([dual_s[it][scen:], nxt], axis=0)
        gnow = gen_s[it]
        gnew = clipped(gnow, sp, own_v[:, lines:] - later)
        gbar = 2.0 * gnew - gnow
        gen_s[it + 1] = gnew
        genlow_v[...] = gbar.astype(bf16)
        return (gnew - gnow) ** 2, gbar

    def prev_bar(it, sp):
        now = v_recv[it, 1] if it == 0 else prev_v[...]
        new = clipped(now, sp, v_recv[it, 0] - dual_s[it][:scen])
        prev_v[...] = new
        return 2.0 * new - now

    def near_arrived(it):
        @pl.when(has[NEAR])
        def _():
            near_part(it).wait_recv()

    def total_at(it, ch):
        @pl.when(has[FAR])
        def _():
            far_part(it, ch).wait_recv()

        lo = ch * cw
        return own_v[:, lo : lo + cw] + part_recv[it, NEAR, ch] + part_recv[it, FAR, ch]

    per = cw // blk

    def caps_of(ch):
        return jnp.concatenate(
            [fcap_v[ch * per + i : ch * per + i + 1, :] for i in range(per)], axis=1
        )

    def stepped(now, sp, total, cap):
        return jnp.minimum(jnp.maximum(now + sp * total, -cap), cap)

    def flow_step(it, ch, sp, total):
        lo = ch * cw
        now = flow_s[it, :, lo : lo + cw]
        new = stepped(now, sp, total, caps_of(ch))
        fw_own[it, ch] = (2.0 * new - now).astype(bf16)

        if ch < nch - (known, early)[it] or it == 0:
            @pl.when(has[FAR] if ch < nch - (known, early)[it] else far_of[0])
            def _():
                far_flow(it, ch).start()

        flow_s[it + 1, :, lo : lo + cw] = new
        return (new - now) ** 2

    def put_state(ref, it, ch):
        ref[:cols] = flow_s[it, :, ch * cw : (ch + 1) * cw]
        ref[cols:] = jnp.broadcast_to(caps_of(ch), (8, cw))

    def ahead_start(it):
        count = (known, early)[it]
        for s in range(count):
            lo = (nch - count + s) * cw
            ahead_send[it, s * cols : (s + 1) * cols] = (
                own_v[:, lo : lo + cw] + part_recv[it, NEAR, nch - count + s]
            )
        if it == 0:
            put_state(ahead_send.at[0, pl.ds(cols, cols + 8)], 0, nch - 1)

            @pl.when(far_of[1])
            def _():
                ahead_copy(0).start()
        else:
            for parity in (0, 1):
                @pl.when(far_of[parity])
                def _():
                    slots = early - parity * known
                    (state_copy(slots) if slots else ahead_copy(0)).wait_send()
                    ahead_copy(1).start()

    def state_start():
        for s in range(early):
            put_state(state_send.at[s], 1, nch - early + s)
        for parity in (0, 1):
            slots = early - parity * known
            if slots:
                @pl.when(far_of[parity])
                def _():
                    if parity == 1:
                        ahead_copy(0).wait_send()
                    state_copy(slots).start()

    def ahead_low(it, sp, ch):
        count = (known, early)[it]
        s = ch - (nch - count)
        total = ahead_recv[it, s * cols : (s + 1) * cols] + part_send[it, FAR, ch]
        if it == 0:
            now, cap = ahead_recv[0, cols : 2 * cols], ahead_recv[0, 2 * cols : 2 * cols + 1]
        else:
            now, cap = state_recv[s, :cols], state_recv[s, cols : cols + 1]
        new = stepped(now, sp, total, cap)
        if it == 0:
            state_recv[early - 1, :cols] = new
            state_recv[early - 1, cols:] = ahead_recv[0, 2 * cols :  2 * cols + 8]
        return (2.0 * new - now).astype(bf16)

    def send_near(it):
        @pl.when(has[NEAR])
        def _():
            near_flow(it).start()

    nt_dims = (((1,), (1,)), ((), ()))
    push_rows = buses // 2 if bb % 2 == 0 else buses

    def joined(get, n):
        return jnp.concatenate([get(ch) for ch in range(n)], axis=1) if n > 1 else get(0)

    rows_at = [pl.ds(at, push_rows) for at in range(0, buses, push_rows)]

    def add_up(lines_of, low, use):
        for rows in rows_at:
            wide = [a_v[rows, at] for at in lines_of]
            use(
                rows,
                lax.dot_general(
                    jnp.concatenate(wide, axis=1) if len(wide) > 1 else wide[0], low, nt_dims,
                    preferred_element_type=f32,
                ),
            )

    def keep(rows, sums):
        acc_v[rows] = sums

    def accumulate(rows, sums):
        acc_v[rows] += sums

    def push_own(it):
        mine = jnp.concatenate([fw_own[it, ch] for ch in range(nch)] + [genlow_v[...]], axis=1)
        add_up([pl.ds(at_own, lines + gens)], mine, keep)

    def push_near(it):
        @pl.when(has[NEAR])
        def _():
            near_flow(it).wait_recv()

        other = joined(lambda ch: fw_in[it, NEAR, ch], nch)
        add_up([pl.ds(at_near, lines)], other, accumulate)

    def push_far(it, sp, chunks, ahead, use):
        lows = []
        for ch in chunks:
            if ch in ahead:
                lows.append(ahead_low(it, sp, ch))
            else:
                far_flow(it, ch).wait_recv()
                lows.append(fw_in[it, FAR, ch])
        add_up(
            [pl.ds(ch * cw, cw) for ch in chunks],
            jnp.concatenate(lows, axis=1) if len(lows) > 1 else lows[0], use,
        )

    def push(it, sp, meanwhile, finish, done):
        if it == 0 and early > 0:
            state_start()
        push_own(it)
        if it == 1:
            meanwhile()
        plans = []
        for parity in (0, 1):
            n = early if it == 1 else known * (1 - parity)
            more = max(nch // 2 - n, 0)
            plans.append(
                ([*range(nch - n, nch)], [*range(nch - n, nch), *range(more)], [*range(more, nch - n)])
            )

        def far_first(parity):
            ahead, first, _ = plans[parity]
            if first:
                @pl.when(far_of[parity])
                def _():
                    if ahead:
                        ahead_copy(it).wait_recv()
                    if it == 1 and early - (1 - parity) * known:
                        state_copy(early - (1 - parity) * known).wait_recv()
                    push_far(it, sp, first, ahead, accumulate)

        far_first(0)
        if it == 1:
            far_first(1)
        push_near(it)
        if it == 0:
            far_first(1)
            meanwhile()

        for parity in (0, 1):
            @pl.when(far_of[parity])
            def _():
                ahead, _, last = plans[parity]
                push_far(it, sp, last, ahead, lambda rows, sums: finish(rows, acc_v[rows] + sums))
                done()

        @pl.when(jnp.logical_not(has[FAR]))
        def _():
            for rows in rows_at:
                finish(rows, acc_v[rows])
            done()

    def ramp_step(it, gbar, prev, sd):
        earlier = prev if cols == scen else jnp.concatenate([prev, gbar[: cols - scen]], axis=0)
        dual = dual_s[it]
        lifted = dual + sd * (gbar - earlier)
        bound = row(caps_v.at[2], n_gens)
        return lifted - sd * jnp.minimum(jnp.maximum(lifted / sd, -bound), bound)

    zero_at = n_tiles + n_gens
    arrived(0, idx_v)
    slot = idx_v[0] * width + (idx_v[1] - (r - 1) * lb)
    down = lax.broadcasted_iota(jnp.int32, (n_tiles, n_tiles), 0)
    across = lax.broadcasted_iota(jnp.int32, (n_tiles, n_tiles), 1)
    upright = jnp.sum(jnp.where(down == across, slot, 0), axis=1, keepdims=True)
    places = lax.broadcasted_iota(jnp.int32, (n_tiles, 128), 1)
    ids = lax.broadcasted_iota(jnp.int32, (n_tiles, 128), 0)
    found = jnp.sum(jnp.where(upright == places, ids - zero_at, 0), axis=0, keepdims=True)
    lane = lax.broadcasted_iota(jnp.int32, (1, 128), 1)
    for g in range(n_gens):
        found = jnp.where(lane == gen_bus[g] * width + 3 * lb + g, n_tiles + g - zero_at, found)
    table_v[...] = jnp.clip(zero_at + found, 0, zero_at)
    to_scalar = pltpu.make_async_copy(table_v, table_s, in_sem.at[0])
    to_scalar.start()

    w1 = jnp.full((1, 1), weight[...], f32)
    arrived(1, first_v)
    set_pt(price_v)
    dual_s[0] = ramp_v[...].T
    d_send[0] = dual_s[0][:scen]
    arrived(2, all_tiles)
    to_scalar.wait()
    build(FAR)
    pl.semaphore_wait(barrier, nt - 1 + count[FAR] + count[NEAR])
    if n_stages > 0:
        stage_signal(0)
    dual_copy(0).start()
    for ch in range(0, nch, per_dot):
        far_sums(0, ch)
        send_far(0, ch)
    late_loads()
    build(NEAR)
    pull_near(0)
    build(3)
    pull_gens()
    arrived(0, late_v)
    arrived(1, caps_v)
    gen_s[0] = gen_v[...].T
    gen_pull(0)
    pass_on(0)
    build(2)
    pull_own()
    sd1 = step_scale * w1
    sp1 = step_scale / w1
    for b in range(lb):
        flow_s[0, :, b * blk : (b + 1) * blk] = flow_v[b * blk : (b + 1) * blk, :].T
    arrived(2, fcap_v)
    near_arrived(0)
    if early > 0:
        ahead_start(0)
    primal_acc = jnp.zeros((8, 128), f32)
    for ch in range(nch):
        primal_acc = primal_acc + fold(flow_step(0, ch, sp1, total_at(0, ch)))
        if ch == 0:
            pass_on(1)
    send_near(0)
    for stage in range(2, n_stages - 1):
        pass_on(stage)
    changed, gbar1 = gen_step(0, sp1)
    primal_acc = primal_acc + fold(changed)
    low = lax.broadcasted_iota(jnp.int32, (1, 128), 1) < 64
    primal_row = both_halves(primal_acc)

    def ramp_now():
        prev_copy(0).wait_recv()
        dual_one = ramp_step(0, gbar1, prev_bar(0, sp1), sd1)
        dual_s[1] = dual_one
        change_v[...] = fold((dual_one - dual_s[0]) ** 2)
        dual_copy(0).wait_send()
        d_send[1] = dual_one[:scen]
        dual_copy(1).start()

    def price_now(rows, pushed):
        old = price_v[rows]
        new = old + sd1 * (demand_v[rows] - pushed)
        price1_v[rows] = new
        change_v[...] += fold((new - old) ** 2)

    def rows_ready():
        ar_s[...] = jnp.where(low, primal_row, both_halves(change_v[...]))

    push(0, sp1, ramp_now, price_now, rows_ready)

    if n_stages > 0:
        stage_wait(n_stages - 1)
    sent(0)
    others_t = partners(t, nt) + [(0, t)]
    others_r = partners(r, nr) + [(0, r)]
    for k, to_r in others_r:
        for j, to_t in others_t:
            if j or k:
                pltpu.make_async_remote_copy(
                    src_ref=ar_s,
                    dst_ref=ar_r.at[j * nr + k],
                    send_sem=ar_sem.at[0],
                    recv_sem=ar_sem.at[1],
                    device_id={"tm": to_t, "region": to_r},
                    device_id_type=MESH,
                ).start()
    others = ar_r.at[pl.ds(1, nt * nr - 1)]
    set_pt(price1_v)
    for ch in range(0, nch, per_dot):
        far_sums(1, ch)
        send_far(1, ch)
    pull_near(1)
    pull_gens()
    prev_copy(0).wait_send()
    gen_pull(1)
    pull_own()
    near_arrived(1)
    if early > 0:
        ahead_start(1)
    pltpu.make_async_copy(others, others, ar_sem.at[1]).wait()
    summed = ar_s[...]
    for at in range(1, nt * nr):
        summed = summed + ar_r[at]
    primal_mean = jnp.sum(jnp.where(low, summed, 0.0), axis=1, keepdims=True) / count_p
    dual_mean = jnp.sum(jnp.where(low, 0.0, summed), axis=1, keepdims=True) / count_d
    w2 = jnp.sqrt(w1 * jnp.sqrt((dual_mean + tiny) / (primal_mean + tiny)))

    sd2 = step_scale * w2
    sp2 = step_scale / w2
    for ch in range(nch):
        flow_step(1, ch, sp2, total_at(1, ch))
    send_near(1)
    _, gbar2 = gen_step(1, sp2)

    def results():
        prev_copy(1).wait_recv()
        o_ramp[...] = ramp_step(1, gbar2, prev_bar(1, sp2), sd2).T
        for b in range(lb):
            o_flow[b * blk : (b + 1) * blk, :] = flow_s[2, :, b * blk : (b + 1) * blk].T
        o_gen[...] = gen_s[2].T

    def price_out(rows, pushed):
        o_price[rows] = price1_v[rows] + sd2 * (demand_v[rows] - pushed)

    push(1, sp2, results, price_out, lambda: None)

    dual_copy(1).wait_send()
    prev_copy(1).wait_send()
    sent(1)
    if early > 0:
        @pl.when(has[FAR])
        def _():
            ahead_copy(1).wait_send()

    pltpu.make_async_copy(others, others, ar_sem.at[0]).wait()


def shards(
    gen, flow, price, ramp_dual, demand, incid_tiles, tile_bus, tile_line, gen_tiles, gen_bus,
    gen_cost, gen_cap, ramp_cap, flow_cap, weight,
):
    gb, blk, hours, scen = gen.shape
    lb, bb = flow.shape[0], price.shape[0]
    n_tiles = incid_tiles.shape[0]
    cols = hours * scen
    nt, nr = lax.axis_size("tm"), lax.axis_size("region")
    lines, buses, gens = lb * blk, bb * blk, gb * blk
    width = 3 * lb + gb
    nch = lb
    early = nch // 2
    ahead_rows = max(2 * cols + 8, early * cols)
    cw = lines // nch
    n_stages, reach = 0, 0
    while reach < nr - 1:
        reach += 2**n_stages
        n_stages += 1

    dims = (
        nt, nr, scen,
        float((gen.size + flow.size) * nt * nr), float((price.size + ramp_dual.size) * nt * nr), early,
    )
    any_spec = pl.BlockSpec(memory_space=pl.ANY)
    smem_spec = pl.BlockSpec(memory_space=pltpu.SMEM)
    dma = pltpu.SemaphoreType.DMA
    V = pltpu.VMEM
    scratch = [
        V((n_tiles + gb + 1, blk, blk), bf16),
        V((buses, width * blk), bf16),
        V((buses + gens, cols), f32),
        V((lines + buses + gens, cols), f32),
        V((3, gb, blk), f32),
        V((lb, blk), f32),
        V((cols, buses), bf16),
        V((cols, lines + gens), f32),
        V((buses, cols), f32),
        V((3, cols, lines), f32),
        V((3, cols, gens), f32),
        V((2, cols, gens), f32),
        V((cols, gens), bf16),
        V((2, 2, nch, cols, cw), f32),
        V((2, 2, nch, cols, cw), f32),
        V((2, nch, cols, cw), bf16),
        V((2, 2, nch, cols, cw), bf16),
        V((2, scen, gens), f32),
        V((2, scen, gens), f32),
        V((2, 2, scen, gens), f32),
        V((2, 2, scen, gens), f32),
        V((scen, gens), f32),
        V((2, ahead_rows, cw), f32),
        V((2, ahead_rows, cw), f32),
        V((max(early, 1), cols + 8, cw), f32),
        V((max(early, 1), cols + 8, cw), f32),
        V((1, 128), f32),
        V((nt * nr, 1, 128), f32),
        V((buses, cols), f32),
        V((8, 128), f32),
        V((2, 1, n_tiles), jnp.int32),
        V((1, 128), jnp.int32),
        pltpu.SMEM((1, 128), jnp.int32),
        dma((3,)),
        dma((2,)),
        dma((nch + 2,)),
        dma((2,)),
        dma((nch + 1,)),
        dma((6,)),
        dma((2,)),
        dma((4,)),
        pltpu.SemaphoreType.REGULAR((n_stages,)),
    ]
    vmem_spec = pl.BlockSpec(memory_space=pltpu.VMEM)
    shapes = ((gens, cols), (lines, cols), (buses, cols), (gens, cols))
    outs = pl.pallas_call(
        functools.partial(kernel, dims),
        out_shape=tuple(V(shape, f32) for shape in shapes),
        in_specs=[smem_spec, smem_spec] + [any_spec] * 13,
        out_specs=(vmem_spec,) * 4,
        scratch_shapes=scratch,
        compiler_params=pltpu.CompilerParams(collective_id=0, has_side_effects=True),
    )(
        gen_bus, weight, tile_bus.reshape(1, n_tiles), tile_line.reshape(1, n_tiles), incid_tiles, gen_tiles,
        price.reshape(buses, cols), flow.reshape(lines, cols), gen.reshape(gens, cols),
        ramp_dual.reshape(gens, cols), demand.reshape(buses, cols),
        gen_cost, gen_cap, ramp_cap, flow_cap,
    )
    outs = pl.pallas_call(
        writer,
        out_shape=tuple(jax.ShapeDtypeStruct(shape, f32) for shape in shapes),
        in_specs=[any_spec] * 4,
        out_specs=(any_spec,) * 4,
        scratch_shapes=[dma((4,))],
    )(*(pltpu.with_memory_space_constraint(out, pltpu.VMEM) for out in outs))
    return tuple(
        out.reshape(like.shape) for out, like in zip(outs, (gen, flow, price, ramp_dual))
    )


def solution(mesh):
    field = P("region", None, "tm", None)
    placed = (
        field, field, field, field, field,
        P("region", None, None), P("region"), P("region"), P("region", None, None), P("region"),
        P("region", None), P("region", None), P("region", None), P("region", None), P(),
    )
    return jax.shard_map(
        shards, mesh=mesh, in_specs=placed, out_specs=(field,) * 4, check_vma=False
    )
```

```python
import functools

import jax
import jax.numpy as jnp
from jax import lax
from jax.experimental import pallas as pl
from jax.experimental.pallas import tpu as pltpu
from jax.sharding import PartitionSpec as P

MESH = pl.DeviceIdType.MESH
step_scale = 0.4
tiny = 1e-06
f32 = jnp.float32
bf16 = jnp.bfloat16


def remote(src, dst, send_sem, recv_sem, axis, peer):
    return pltpu.make_async_remote_copy(
        src_ref=src,
        dst_ref=dst,
        send_sem=send_sem,
        recv_sem=recv_sem,
        device_id={axis: peer},
        device_id_type=MESH,
    )


def fold(x):
    rows, columns = x.shape
    y = jnp.sum(x.reshape(rows // 8, 8, columns), axis=0)
    out = y[:, :128]
    for at in range(128, columns, 128):
        out = out + y[:, at : at + 128]
    return out


def both_halves(x):
    row = jnp.sum(x, axis=0, keepdims=True)
    return row + pltpu.roll(row, 64, 1)


def writer(*refs):
    n = (len(refs) - 1) // 2
    copies = [pltpu.make_async_copy(refs[i], refs[n + i], refs[-1].at[i]) for i in range(n)]
    for c in copies:
        c.start()
    for c in copies:
        c.wait()


def flip(x, mask):
    bit = 1
    out = x
    while bit <= mask:
        if mask & bit:
            out = out + bit * (1 - 2 * lax.rem(x // bit, 2))
        bit *= 2
    return out


def partners(x, n):
    if n & (n - 1) == 0:
        return [(m, flip(x, m)) for m in [n // 2, *range(n - 1, n // 2, -1), *range(n // 2 - 1, 0, -1)]]
    return [(m, lax.rem(x + m, n)) for m in range(1, n)]


FAR, NEAR = 0, 1


def kernel(
    dims,
    gen_bus, weight, tile_bus, tile_line, tiles, gtiles, price, flow, gen, ramp, demand, cost, gcap, rcap, fcap,
    o_gen, o_flow, o_price, o_ramp,
    tiles_v, a_v, first_v, late_v, caps_v, fcap_v,
    pt_v, own_v, price1_v, flow_s, gen_s, dual_s, genlow_v,
    part_send, part_recv, fw_own, fw_in, d_send, d_recv, v_send, v_recv, prev_v,
    ahead_send, ahead_recv, state_send, state_recv,
    ar_s, ar_r, acc_v, change_v, idx_v, table_v, table_s,
    in_sem, ps_sem, pr_sem, fs_sem, fr_sem, tm_sem, ar_sem, ahead_sem, ready,
):
    nt, nr, scen, count_p, count_d, early = dims
    t = lax.axis_index("tm")
    r = lax.axis_index("region")
    n_tiles, blk, _ = tiles.shape
    n_gens = gtiles.shape[0]
    lines, cols = flow.shape
    buses = price.shape[0]
    lb, bb = lines // blk, buses // blk
    width = 3 * lb + n_gens
    nch = part_send.shape[2]
    cw = lines // nch
    n_stages = ready.shape[0]
    known = min(early, 1)
    ahead_rows = (2 * cols + 8, early * cols)

    odd = lax.rem(r, 2)
    place = (r - 1 + 2 * odd, r + 1 - 2 * odd)
    has = tuple((p >= 0) & (p < nr) for p in place)
    peer = tuple(jnp.clip(p, 0, nr - 1) for p in place)
    count = tuple(jnp.where(h, 1, 0) for h in has)
    is_odd = odd == 1
    far_of = (has[FAR] & (odd == 0), has[FAR] & is_odd)
    first_window = (2 * lb * odd, 2 * lb * (1 - odd), lb)

    barrier = pltpu.get_barrier_semaphore()
    for side in (FAR, NEAR):
        @pl.when(has[side])
        def _():
            pl.semaphore_signal(
                barrier, inc=1, device_id={"region": peer[side]}, device_id_type=MESH
            )
    for k in range(1, nt):
        pl.semaphore_signal(
            barrier, inc=1, device_id={"tm": lax.rem(t + k, nt)}, device_id_type=MESH
        )

    def stage_signal(stage):
        step = 2**stage
        for to in (r - step, r + step):
            @pl.when((to >= 0) & (to < nr))
            def _():
                pl.semaphore_signal(
                    ready.at[stage], inc=1, device_id={"region": jnp.clip(to, 0, nr - 1)},
                    device_id_type=MESH,
                )

    def stage_wait(stage):
        step = 2**stage
        pl.semaphore_wait(
            ready.at[stage], jnp.where(r >= step, 1, 0) + jnp.where(r + step < nr, 1, 0)
        )

    def pass_on(stage):
        if stage < n_stages - 1:
            stage_wait(stage)
            stage_signal(stage + 1)

    def load(i, *pairs):
        copies = [pltpu.make_async_copy(src, dst, in_sem.at[i]) for src, dst in pairs]
        for c in copies:
            c.start()

    def arrived(i, ref):
        pltpu.make_async_copy(ref, ref, in_sem.at[i]).wait()

    load(0, (tile_bus, idx_v.at[0]), (tile_line, idx_v.at[1]))
    all_tiles = tiles_v.at[pl.ds(0, n_tiles + n_gens)]
    gens = gen.shape[0]
    price_v, ramp_v = first_v.at[pl.ds(0, buses)], first_v.at[pl.ds(buses, gens)]
    load(1, (price, price_v), (ramp, ramp_v))
    load(2, (tiles, tiles_v.at[pl.ds(0, n_tiles)]), (gtiles, tiles_v.at[pl.ds(n_tiles, n_gens)]))
    flow_v = late_v.at[pl.ds(0, lines)]
    demand_v = late_v.at[pl.ds(lines, buses)]
    gen_v = late_v.at[pl.ds(lines + buses, gens)]

    def late_loads():
        load(0, (flow, flow_v), (demand, demand_v), (gen, gen_v))
        load(1, (cost, caps_v.at[0]), (gcap, caps_v.at[1]), (rcap, caps_v.at[2]))
        load(2, (fcap, fcap_v))

    tiles_v[n_tiles + n_gens] = jnp.zeros((blk, blk), bf16)

    for side in (FAR, NEAR):
        @pl.when(jnp.logical_not(has[side]))
        def _():
            part_recv[:, side] = jnp.zeros_like(part_recv[:, side])
            fw_in[:, side] = jnp.zeros_like(fw_in[:, side])

    t_next, t_prev = lax.rem(t + 1, nt), lax.rem(t + nt - 1, nt)

    def far_part(it, ch):
        return remote(
            part_send.at[it, FAR, ch], part_recv.at[it, FAR, ch],
            ps_sem.at[FAR], pr_sem.at[nch + 1 if it == 1 and ch >= nch - known else ch],
            "region", peer[FAR],
        )

    def near_part(it):
        return remote(
            part_send.at[it, NEAR], part_recv.at[it, NEAR],
            ps_sem.at[NEAR], pr_sem.at[nch], "region", peer[NEAR],
        )

    def far_flow(it, ch):
        return remote(
            fw_own.at[it, ch], fw_in.at[it, FAR, ch],
            fs_sem.at[FAR], fr_sem.at[ch], "region", peer[FAR],
        )

    def near_flow(it):
        return remote(
            fw_own.at[it], fw_in.at[it, NEAR],
            fs_sem.at[NEAR], fr_sem.at[nch], "region", peer[NEAR],
        )

    def dual_copy(it):
        return remote(d_send.at[it], d_recv.at[it], tm_sem.at[0], tm_sem.at[2 + it], "tm", t_prev)

    def prev_copy(it):
        parts = pl.ds(0, 2 - it)
        return remote(
            v_send.at[it, parts], v_recv.at[it, parts], tm_sem.at[1], tm_sem.at[4 + it], "tm", t_next
        )

    def ahead_copy(it):
        rows = pl.ds(0, ahead_rows[it])
        return remote(
            ahead_send.at[it, rows], ahead_recv.at[it, rows],
            ahead_sem.at[0], ahead_sem.at[1 + it], "region", peer[FAR],
        )

    def state_copy(count):
        slots = pl.ds(0, count)
        return remote(
            state_send.at[slots], state_recv.at[slots], ahead_sem.at[0], ahead_sem.at[3],
            "region", peer[FAR],
        )

    def sent(it):
        for side in (FAR, NEAR):
            @pl.when(has[side])
            def _():
                ref = part_send.at[it, side]
                pltpu.make_async_copy(ref, ref, ps_sem.at[side]).wait()
                if it == 1 or side == NEAR:
                    ref = fw_own.at[it, pl.ds(0, nch - early if side == FAR else nch)]
                    pltpu.make_async_copy(ref, ref, fs_sem.at[side]).wait()
        if it == 0:
            for parity in (0, 1):
                @pl.when(far_of[parity])
                def _():
                    ref = fw_own.at[0, pl.ds(0, nch - parity * known)]
                    pltpu.make_async_copy(ref, ref, fs_sem.at[FAR]).wait()

    at_near, at_own, at_gens = lines, 2 * lines, 3 * lines

    def build(group):
        n = n_gens if group == 3 else lb
        for i in range(n):
            window = 3 * lb + i if group == 3 else first_window[group] + i
            lo = group * lines + i * blk
            for b in range(bb):
                a_v[b * blk : (b + 1) * blk, lo : lo + blk] = tiles_v[table_s[0, b * width + window]]

    per_dot = 2 if nch % 2 == 0 else 1

    def far_sums(it, ch):
        sums = jnp.dot(
            pt_v[...], a_v[:, ch * cw : (ch + per_dot) * cw], preferred_element_type=f32
        )
        for i in range(per_dot):
            part_send[it, FAR, ch + i] = sums[:, i * cw : (i + 1) * cw]

    def send_far(it, ch):
        @pl.when(has[FAR])
        def _():
            for i in range(per_dot):
                far_part(it, ch + i).start()

    def pull_near(it):
        for ch in range(0, nch, per_dot):
            at = at_near + ch * cw
            sums = jnp.dot(
                pt_v[...], a_v[:, at : at + per_dot * cw], preferred_element_type=f32
            )
            for i in range(per_dot):
                part_send[it, NEAR, ch + i] = sums[:, i * cw : (i + 1) * cw]

        @pl.when(has[NEAR])
        def _():
            near_part(it).start()

    def pull_gens():
        own_v[:, lines:] = jnp.dot(pt_v[...], a_v[:, at_gens:], preferred_element_type=f32)

    def pull_own():
        own_v[:, :lines] = jnp.dot(
            pt_v[...], a_v[:, at_own:at_gens], preferred_element_type=f32
        )

    def set_pt(ref):
        for b in range(bb):
            pt_v[:, b * blk : (b + 1) * blk] = ref[b * blk : (b + 1) * blk, :].astype(bf16).T

    def row(ref, n):
        return jnp.concatenate([ref[i : i + 1, :] for i in range(n)], axis=1) if n > 1 else ref[...]

    def gen_pull(it):
        grad = row(caps_v.at[0], n_gens) - own_v[:, lines:] + dual_s[it]
        own_v[:, lines:] = grad
        v_send[it, 0] = grad[cols - scen :]
        if it == 0:
            v_send[it, 1] = gen_s[it][cols - scen :]
        prev_copy(it).start()

    def clipped(now, sp, grad):
        return jnp.minimum(jnp.maximum(now - sp * grad, 0.0), row(caps_v.at[1], n_gens))

    def gen_step(it, sp):
        dual_copy(it).wait_recv()
        nxt = d_recv[it]
        later = nxt if cols == scen else jnp.concatenate([dual_s[it][scen:], nxt], axis=0)
        gnow = gen_s[it]
        gnew = clipped(gnow, sp, own_v[:, lines:] - later)
        gbar = 2.0 * gnew - gnow
        gen_s[it + 1] = gnew
        genlow_v[...] = gbar.astype(bf16)
        return (gnew - gnow) ** 2, gbar

    def prev_bar(it, sp):
        now = v_recv[it, 1] if it == 0 else prev_v[...]
        new = clipped(now, sp, v_recv[it, 0] - dual_s[it][:scen])
        prev_v[...] = new
        return 2.0 * new - now

    def near_arrived(it):
        @pl.when(has[NEAR])
        def _():
            near_part(it).wait_recv()

    def total_at(it, ch):
        @pl.when(has[FAR])
        def _():
            far_part(it, ch).wait_recv()

        lo = ch * cw
        return own_v[:, lo : lo + cw] + part_recv[it, NEAR, ch] + part_recv[it, FAR, ch]

    per = cw // blk

    def caps_of(ch):
        return jnp.concatenate(
            [fcap_v[ch * per + i : ch * per + i + 1, :] for i in range(per)], axis=1
        )

    def stepped(now, sp, total, cap):
        return jnp.minimum(jnp.maximum(now + sp * total, -cap), cap)

    def flow_step(it, ch, sp, total):
        lo = ch * cw
        now = flow_s[it, :, lo : lo + cw]
        new = stepped(now, sp, total, caps_of(ch))
        fw_own[it, ch] = (2.0 * new - now).astype(bf16)

        if ch < nch - (known, early)[it] or it == 0:
            @pl.when(has[FAR] if ch < nch - (known, early)[it] else far_of[0])
            def _():
                far_flow(it, ch).start()

        flow_s[it + 1, :, lo : lo + cw] = new
        return (new - now) ** 2

    def put_state(ref, it, ch):
        ref[:cols] = flow_s[it, :, ch * cw : (ch + 1) * cw]
        ref[cols:] = jnp.broadcast_to(caps_of(ch), (8, cw))

    def ahead_start(it):
        count = (known, early)[it]
        for s in range(count):
            lo = (nch - count + s) * cw
            ahead_send[it, s * cols : (s + 1) * cols] = (
                own_v[:, lo : lo + cw] + part_recv[it, NEAR, nch - count + s]
            )
        if it == 0:
            put_state(ahead_send.at[0, pl.ds(cols, cols + 8)], 0, nch - 1)

            @pl.when(far_of[1])
            def _():
                ahead_copy(0).start()
        else:
            for parity in (0, 1):
                @pl.when(far_of[parity])
                def _():
                    slots = early - parity * known
                    (state_copy(slots) if slots else ahead_copy(0)).wait_send()
                    ahead_copy(1).start()

    def state_start():
        for s in range(early):
            put_state(state_send.at[s], 1, nch - early + s)
        for parity in (0, 1):
            slots = early - parity * known
            if slots:
                @pl.when(far_of[parity])
                def _():
                    if parity == 1:
                        ahead_copy(0).wait_send()
                    state_copy(slots).start()

    def ahead_low(it, sp, ch):
        count = (known, early)[it]
        s = ch - (nch - count)
        total = ahead_recv[it, s * cols : (s + 1) * cols] + part_send[it, FAR, ch]
        if it == 0:
            now, cap = ahead_recv[0, cols : 2 * cols], ahead_recv[0, 2 * cols : 2 * cols + 1]
        else:
            now, cap = state_recv[s, :cols], state_recv[s, cols : cols + 1]
        new = stepped(now, sp, total, cap)
        if it == 0:
            state_recv[early - 1, :cols] = new
            state_recv[early - 1, cols:] = ahead_recv[0, 2 * cols :  2 * cols + 8]
        return (2.0 * new - now).astype(bf16)

    def send_near(it):
        @pl.when(has[NEAR])
        def _():
            near_flow(it).start()

    nt_dims = (((1,), (1,)), ((), ()))
    push_rows = buses // 2 if bb % 2 == 0 else buses

    def joined(get, n):
        return jnp.concatenate([get(ch) for ch in range(n)], axis=1) if n > 1 else get(0)

    rows_at = [pl.ds(at, push_rows) for at in range(0, buses, push_rows)]

    def add_up(lines_of, low, use):
        for rows in rows_at:
            wide = [a_v[rows, at] for at in lines_of]
            use(
                rows,
                lax.dot_general(
                    jnp.concatenate(wide, axis=1) if len(wide) > 1 else wide[0], low, nt_dims,
                    preferred_element_type=f32,
                ),
            )

    def keep(rows, sums):
        acc_v[rows] = sums

    def accumulate(rows, sums):
        acc_v[rows] += sums

    def push_own(it):
        mine = jnp.concatenate([fw_own[it, ch] for ch in range(nch)] + [genlow_v[...]], axis=1)
        add_up([pl.ds(at_own, lines + gens)], mine, keep)

    def push_near(it):
        @pl.when(has[NEAR])
        def _():
            near_flow(it).wait_recv()

        other = joined(lambda ch: fw_in[it, NEAR, ch], nch)
        add_up([pl.ds(at_near, lines)], other, accumulate)

    def push_far(it, sp, chunks, ahead, use):
        lows = []
        for ch in chunks:
            if ch in ahead:
                lows.append(ahead_low(it, sp, ch))
            else:
                far_flow(it, ch).wait_recv()
                lows.append(fw_in[it, FAR, ch])
        add_up(
            [pl.ds(ch * cw, cw) for ch in chunks],
            jnp.concatenate(lows, axis=1) if len(lows) > 1 else lows[0], use,
        )

    def push(it, sp, meanwhile, finish, done):
        if it == 0 and early > 0:
            state_start()
        push_own(it)
        if it == 1:
            meanwhile()
        plans = []
        for parity in (0, 1):
            n = early if it == 1 else known * (1 - parity)
            more = max(nch // 2 - n, 0)
            plans.append(
                ([*range(nch - n, nch)], [*range(nch - n, nch), *range(more)], [*range(more, nch - n)])
            )

        def far_first(parity):
            ahead, first, _ = plans[parity]
            if first:
                @pl.when(far_of[parity])
                def _():
                    if ahead:
                        ahead_copy(it).wait_recv()
                    if it == 1 and early - (1 - parity) * known:
                        state_copy(early - (1 - parity) * known).wait_recv()
                    push_far(it, sp, first, ahead, accumulate)

        far_first(0)
        if it == 1:
            far_first(1)
        push_near(it)
        if it == 0:
            far_first(1)
            meanwhile()

        for parity in (0, 1):
            @pl.when(far_of[parity])
            def _():
                ahead, _, last = plans[parity]
                push_far(it, sp, last, ahead, lambda rows, sums: finish(rows, acc_v[rows] + sums))
                done()

        @pl.when(jnp.logical_not(has[FAR]))
        def _():
            for rows in rows_at:
                finish(rows, acc_v[rows])
            done()

    def ramp_step(it, gbar, prev, sd):
        earlier = prev if cols == scen else jnp.concatenate([prev, gbar[: cols - scen]], axis=0)
        dual = dual_s[it]
        lifted = dual + sd * (gbar - earlier)
        bound = row(caps_v.at[2], n_gens)
        return lifted - sd * jnp.minimum(jnp.maximum(lifted / sd, -bound), bound)

    zero_at = n_tiles + n_gens
    arrived(0, idx_v)
    slot = idx_v[0] * width + (idx_v[1] - (r - 1) * lb)
    down = lax.broadcasted_iota(jnp.int32, (n_tiles, n_tiles), 0)
    across = lax.broadcasted_iota(jnp.int32, (n_tiles, n_tiles), 1)
    upright = jnp.sum(jnp.where(down == across, slot, 0), axis=1, keepdims=True)
    places = lax.broadcasted_iota(jnp.int32, (n_tiles, 128), 1)
    ids = lax.broadcasted_iota(jnp.int32, (n_tiles, 128), 0)
    found = jnp.sum(jnp.where(upright == places, ids - zero_at, 0), axis=0, keepdims=True)
    lane = lax.broadcasted_iota(jnp.int32, (1, 128), 1)
    for g in range(n_gens):
        found = jnp.where(lane == gen_bus[g] * width + 3 * lb + g, n_tiles + g - zero_at, found)
    table_v[...] = jnp.clip(zero_at + found, 0, zero_at)
    to_scalar = pltpu.make_async_copy(table_v, table_s, in_sem.at[0])
    to_scalar.start()

    w1 = jnp.full((1, 1), weight[...], f32)
    arrived(1, first_v)
    set_pt(price_v)
    dual_s[0] = ramp_v[...].T
    d_send[0] = dual_s[0][:scen]
    arrived(2, all_tiles)
    to_scalar.wait()
    build(FAR)
    pl.semaphore_wait(barrier, nt - 1 + count[FAR] + count[NEAR])
    if n_stages > 0:
        stage_signal(0)
    dual_copy(0).start()
    for ch in range(0, nch, per_dot):
        far_sums(0, ch)
        send_far(0, ch)
    late_loads()
    build(NEAR)
    pull_near(0)
    build(3)
    pull_gens()
    arrived(0, late_v)
    arrived(1, caps_v)
    gen_s[0] = gen_v[...].T
    gen_pull(0)
    pass_on(0)
    build(2)
    pull_own()
    sd1 = step_scale * w1
    sp1 = step_scale / w1
    for b in range(lb):
        flow_s[0, :, b * blk : (b + 1) * blk] = flow_v[b * blk : (b + 1) * blk, :].T
    arrived(2, fcap_v)
    near_arrived(0)
    if early > 0:
        ahead_start(0)
    primal_acc = jnp.zeros((8, 128), f32)
    for ch in range(nch):
        primal_acc = primal_acc + fold(flow_step(0, ch, sp1, total_at(0, ch)))
        if ch == 0:
            pass_on(1)
    send_near(0)
    for stage in range(2, n_stages - 1):
        pass_on(stage)
    changed, gbar1 = gen_step(0, sp1)
    primal_acc = primal_acc + fold(changed)
    low = lax.broadcasted_iota(jnp.int32, (1, 128), 1) < 64
    primal_row = both_halves(primal_acc)

    def ramp_now():
        prev_copy(0).wait_recv()
        dual_one = ramp_step(0, gbar1, prev_bar(0, sp1), sd1)
        dual_s[1] = dual_one
        change_v[...] = fold((dual_one - dual_s[0]) ** 2)
        dual_copy(0).wait_send()
        d_send[1] = dual_one[:scen]
        dual_copy(1).start()

    def price_now(rows, pushed):
        old = price_v[rows]
        new = old + sd1 * (demand_v[rows] - pushed)
        price1_v[rows] = new
        change_v[...] += fold((new - old) ** 2)

    def rows_ready():
        ar_s[...] = jnp.where(low, primal_row, both_halves(change_v[...]))

    push(0, sp1, ramp_now, price_now, rows_ready)

    if n_stages > 0:
        stage_wait(n_stages - 1)
    others_t = partners(t, nt) + [(0, t)]
    others_r = partners(r, nr) + [(0, r)]
    for k, to_r in others_r:
        for j, to_t in others_t:
            if j or k:
                pltpu.make_async_remote_copy(
                    src_ref=ar_s,
                    dst_ref=ar_r.at[j * nr + k],
                    send_sem=ar_sem.at[0],
                    recv_sem=ar_sem.at[1],
                    device_id={"tm": to_t, "region": to_r},
                    device_id_type=MESH,
                ).start()
    others = ar_r.at[pl.ds(1, nt * nr - 1)]
    sent(0)
    set_pt(price1_v)
    for ch in range(0, nch, per_dot):
        far_sums(1, ch)
        send_far(1, ch)
    pull_near(1)
    pull_gens()
    prev_copy(0).wait_send()
    gen_pull(1)
    pull_own()
    near_arrived(1)
    if early > 0:
        ahead_start(1)
    pltpu.make_async_copy(others, others, ar_sem.at[1]).wait()
    parts = [ar_s[...]] + [ar_r[at] for at in range(1, nt * nr)]
    while len(parts) > 1:
        parts = [a + b for a, b in zip(parts[::2], parts[1::2])] + parts[len(parts) // 2 * 2 :]
    summed = parts[0]
    primal_mean = jnp.sum(jnp.where(low, summed, 0.0), axis=1, keepdims=True) / count_p
    dual_mean = jnp.sum(jnp.where(low, 0.0, summed), axis=1, keepdims=True) / count_d
    w2 = jnp.sqrt(w1 * jnp.sqrt((dual_mean + tiny) / (primal_mean + tiny)))

    sd2 = step_scale * w2
    sp2 = step_scale / w2
    for ch in range(nch):
        flow_step(1, ch, sp2, total_at(1, ch))
    send_near(1)
    _, gbar2 = gen_step(1, sp2)

    def results():
        prev_copy(1).wait_recv()
        o_ramp[...] = ramp_step(1, gbar2, prev_bar(1, sp2), sd2).T
        for b in range(lb):
            o_flow[b * blk : (b + 1) * blk, :] = flow_s[2, :, b * blk : (b + 1) * blk].T
        o_gen[...] = gen_s[2].T

    def price_out(rows, pushed):
        o_price[rows] = price1_v[rows] + sd2 * (demand_v[rows] - pushed)

    push(1, sp2, results, price_out, lambda: None)

    dual_copy(1).wait_send()
    prev_copy(1).wait_send()
    sent(1)
    if early > 0:
        @pl.when(has[FAR])
        def _():
            ahead_copy(1).wait_send()

    pltpu.make_async_copy(others, others, ar_sem.at[0]).wait()


def shards(
    gen, flow, price, ramp_dual, demand, incid_tiles, tile_bus, tile_line, gen_tiles, gen_bus,
    gen_cost, gen_cap, ramp_cap, flow_cap, weight,
):
    gb, blk, hours, scen = gen.shape
    lb, bb = flow.shape[0], price.shape[0]
    n_tiles = incid_tiles.shape[0]
    cols = hours * scen
    nt, nr = lax.axis_size("tm"), lax.axis_size("region")
    lines, buses, gens = lb * blk, bb * blk, gb * blk
    width = 3 * lb + gb
    nch = lb
    early = nch // 2
    ahead_rows = max(2 * cols + 8, early * cols)
    cw = lines // nch
    n_stages, reach = 0, 0
    while reach < nr - 1:
        reach += 2**n_stages
        n_stages += 1

    dims = (
        nt, nr, scen,
        float((gen.size + flow.size) * nt * nr), float((price.size + ramp_dual.size) * nt * nr), early,
    )
    any_spec = pl.BlockSpec(memory_space=pl.ANY)
    smem_spec = pl.BlockSpec(memory_space=pltpu.SMEM)
    dma = pltpu.SemaphoreType.DMA
    V = pltpu.VMEM
    scratch = [
        V((n_tiles + gb + 1, blk, blk), bf16),
        V((buses, width * blk), bf16),
        V((buses + gens, cols), f32),
        V((lines + buses + gens, cols), f32),
        V((3, gb, blk), f32),
        V((lb, blk), f32),
        V((cols, buses), bf16),
        V((cols, lines + gens), f32),
        V((buses, cols), f32),
        V((3, cols, lines), f32),
        V((3, cols, gens), f32),
        V((2, cols, gens), f32),
        V((cols, gens), bf16),
        V((2, 2, nch, cols, cw), f32),
        V((2, 2, nch, cols, cw), f32),
        V((2, nch, cols, cw), bf16),
        V((2, 2, nch, cols, cw), bf16),
        V((2, scen, gens), f32),
        V((2, scen, gens), f32),
        V((2, 2, scen, gens), f32),
        V((2, 2, scen, gens), f32),
        V((scen, gens), f32),
        V((2, ahead_rows, cw), f32),
        V((2, ahead_rows, cw), f32),
        V((max(early, 1), cols + 8, cw), f32),
        V((max(early, 1), cols + 8, cw), f32),
        V((1, 128), f32),
        V((nt * nr, 1, 128), f32),
        V((buses, cols), f32),
        V((8, 128), f32),
        V((2, 1, n_tiles), jnp.int32),
        V((1, 128), jnp.int32),
        pltpu.SMEM((1, 128), jnp.int32),
        dma((3,)),
        dma((2,)),
        dma((nch + 2,)),
        dma((2,)),
        dma((nch + 1,)),
        dma((6,)),
        dma((2,)),
        dma((4,)),
        pltpu.SemaphoreType.REGULAR((n_stages,)),
    ]
    vmem_spec = pl.BlockSpec(memory_space=pltpu.VMEM)
    shapes = ((gens, cols), (lines, cols), (buses, cols), (gens, cols))
    outs = pl.pallas_call(
        functools.partial(kernel, dims),
        out_shape=tuple(V(shape, f32) for shape in shapes),
        in_specs=[smem_spec, smem_spec] + [any_spec] * 13,
        out_specs=(vmem_spec,) * 4,
        scratch_shapes=scratch,
        compiler_params=pltpu.CompilerParams(collective_id=0, has_side_effects=True),
    )(
        gen_bus, weight, tile_bus.reshape(1, n_tiles), tile_line.reshape(1, n_tiles), incid_tiles, gen_tiles,
        price.reshape(buses, cols), flow.reshape(lines, cols), gen.reshape(gens, cols),
        ramp_dual.reshape(gens, cols), demand.reshape(buses, cols),
        gen_cost, gen_cap, ramp_cap, flow_cap,
    )
    outs = pl.pallas_call(
        writer,
        out_shape=tuple(jax.ShapeDtypeStruct(shape, f32) for shape in shapes),
        in_specs=[any_spec] * 4,
        out_specs=(any_spec,) * 4,
        scratch_shapes=[dma((4,))],
    )(*(pltpu.with_memory_space_constraint(out, pltpu.VMEM) for out in outs))
    return tuple(
        out.reshape(like.shape) for out, like in zip(outs, (gen, flow, price, ramp_dual))
    )


def solution(mesh):
    field = P("region", None, "tm", None)
    placed = (
        field, field, field, field, field,
        P("region", None, None), P("region"), P("region"), P("region", None, None), P("region"),
        P("region", None), P("region", None), P("region", None), P("region", None), P(),
    )
    return jax.shard_map(
        shards, mesh=mesh, in_specs=placed, out_specs=(field,) * 4, check_vma=False
    )
```

```python
import functools

import jax
import jax.numpy as jnp
from jax import lax
from jax.experimental import pallas as pl
from jax.experimental.pallas import tpu as pltpu
from jax.sharding import PartitionSpec as P

MESH = pl.DeviceIdType.MESH
step_scale = 0.4
tiny = 1e-06
f32 = jnp.float32
bf16 = jnp.bfloat16


def remote(src, dst, send_sem, recv_sem, axis, peer):
    return pltpu.make_async_remote_copy(
        src_ref=src,
        dst_ref=dst,
        send_sem=send_sem,
        recv_sem=recv_sem,
        device_id={axis: peer},
        device_id_type=MESH,
    )


def fold(x):
    rows, columns = x.shape
    y = jnp.sum(x.reshape(rows // 8, 8, columns), axis=0)
    out = y[:, :128]
    for at in range(128, columns, 128):
        out = out + y[:, at : at + 128]
    return out


def both_halves(x):
    row = jnp.sum(x, axis=0, keepdims=True)
    return row + pltpu.roll(row, 64, 1)


def writer(*refs):
    n = (len(refs) - 1) // 2
    copies = [pltpu.make_async_copy(refs[i], refs[n + i], refs[-1].at[i]) for i in range(n)]
    for c in copies:
        c.start()
    for c in copies:
        c.wait()


def flip(x, mask):
    bit = 1
    out = x
    while bit <= mask:
        if mask & bit:
            out = out + bit * (1 - 2 * lax.rem(x // bit, 2))
        bit *= 2
    return out


def partners(x, n):
    if n & (n - 1) == 0:
        return [(m, flip(x, m)) for m in [n // 2, *range(n - 1, n // 2, -1), *range(n // 2 - 1, 0, -1)]]
    return [(m, lax.rem(x + m, n)) for m in range(1, n)]


FAR, NEAR = 0, 1


def kernel(
    dims,
    gen_bus, weight, tile_bus, tile_line, tiles, gtiles, price, flow, gen, ramp, demand, cost, gcap, rcap, fcap,
    o_gen, o_flow, o_price, o_ramp,
    tiles_v, a_v, first_v, late_v, caps_v, fcap_v,
    pt_v, own_v, price1_v, flow_s, gen_s, dual_s, genlow_v,
    part_send, part_recv, fw_own, fw_in, d_send, d_recv, v_send, v_recv, prev_v,
    ahead_send, ahead_recv, state_send, state_recv,
    ar_s, ar_r, acc_v, change_v, idx_v, table_v, table_s,
    in_sem, ps_sem, pr_sem, fs_sem, fr_sem, tm_sem, ar_sem, ahead_sem, ready,
):
    nt, nr, scen, count_p, count_d, early = dims
    t = lax.axis_index("tm")
    r = lax.axis_index("region")
    n_tiles, blk, _ = tiles.shape
    n_gens = gtiles.shape[0]
    lines, cols = flow.shape
    buses = price.shape[0]
    lb, bb = lines // blk, buses // blk
    width = 3 * lb + n_gens
    nch = part_send.shape[2]
    cw = lines // nch
    n_stages = ready.shape[0]
    known = min(early, 1)
    ahead_rows = (2 * cols + 8, early * cols)

    odd = lax.rem(r, 2)
    place = (r - 1 + 2 * odd, r + 1 - 2 * odd)
    has = tuple((p >= 0) & (p < nr) for p in place)
    peer = tuple(jnp.clip(p, 0, nr - 1) for p in place)
    count = tuple(jnp.where(h, 1, 0) for h in has)
    is_odd = odd == 1
    far_of = (has[FAR] & (odd == 0), has[FAR] & is_odd)
    first_window = (2 * lb * odd, 2 * lb * (1 - odd), lb)

    barrier = pltpu.get_barrier_semaphore()
    for side in (FAR, NEAR):
        @pl.when(has[side])
        def _():
            pl.semaphore_signal(
                barrier, inc=1, device_id={"region": peer[side]}, device_id_type=MESH
            )
    for k in range(1, nt):
        pl.semaphore_signal(
            barrier, inc=1, device_id={"tm": lax.rem(t + k, nt)}, device_id_type=MESH
        )

    def stage_signal(stage):
        step = 2**stage
        for to in (r - step, r + step):
            @pl.when((to >= 0) & (to < nr))
            def _():
                pl.semaphore_signal(
                    ready.at[stage], inc=1, device_id={"region": jnp.clip(to, 0, nr - 1)},
                    device_id_type=MESH,
                )

    def stage_wait(stage):
        step = 2**stage
        pl.semaphore_wait(
            ready.at[stage], jnp.where(r >= step, 1, 0) + jnp.where(r + step < nr, 1, 0)
        )

    def pass_on(stage):
        if stage < n_stages - 1:
            stage_wait(stage)
            stage_signal(stage + 1)

    def load(i, *pairs):
        copies = [pltpu.make_async_copy(src, dst, in_sem.at[i]) for src, dst in pairs]
        for c in copies:
            c.start()

    def arrived(i, ref):
        pltpu.make_async_copy(ref, ref, in_sem.at[i]).wait()

    load(0, (tile_bus, idx_v.at[0]), (tile_line, idx_v.at[1]))
    all_tiles = tiles_v.at[pl.ds(0, n_tiles + n_gens)]
    gens = gen.shape[0]
    price_v, ramp_v = first_v.at[pl.ds(0, buses)], first_v.at[pl.ds(buses, gens)]
    load(1, (price, price_v), (ramp, ramp_v))
    load(2, (tiles, tiles_v.at[pl.ds(0, n_tiles)]), (gtiles, tiles_v.at[pl.ds(n_tiles, n_gens)]))
    flow_v = late_v.at[pl.ds(0, lines)]
    demand_v = late_v.at[pl.ds(lines, buses)]
    gen_v = late_v.at[pl.ds(lines + buses, gens)]

    def late_loads():
        load(0, (flow, flow_v), (demand, demand_v), (gen, gen_v))
        load(1, (cost, caps_v.at[0]), (gcap, caps_v.at[1]), (rcap, caps_v.at[2]))
        load(2, (fcap, fcap_v))

    tiles_v[n_tiles + n_gens] = jnp.zeros((blk, blk), bf16)

    for side in (FAR, NEAR):
        @pl.when(jnp.logical_not(has[side]))
        def _():
            part_recv[:, side] = jnp.zeros_like(part_recv[:, side])
            fw_in[:, side] = jnp.zeros_like(fw_in[:, side])

    t_next, t_prev = lax.rem(t + 1, nt), lax.rem(t + nt - 1, nt)

    def far_part(it, ch):
        return remote(
            part_send.at[it, FAR, ch], part_recv.at[it, FAR, ch],
            ps_sem.at[FAR], pr_sem.at[nch + 1 if it == 1 and ch >= nch - known else ch],
            "region", peer[FAR],
        )

    def near_part(it):
        return remote(
            part_send.at[it, NEAR], part_recv.at[it, NEAR],
            ps_sem.at[NEAR], pr_sem.at[nch], "region", peer[NEAR],
        )

    def far_flow(it, ch):
        return remote(
            fw_own.at[it, ch], fw_in.at[it, FAR, ch],
            fs_sem.at[FAR], fr_sem.at[ch], "region", peer[FAR],
        )

    def near_flow(it):
        return remote(
            fw_own.at[it], fw_in.at[it, NEAR],
            fs_sem.at[NEAR], fr_sem.at[nch], "region", peer[NEAR],
        )

    def dual_copy(it):
        return remote(d_send.at[it], d_recv.at[it], tm_sem.at[0], tm_sem.at[2 + it], "tm", t_prev)

    def prev_copy(it):
        parts = pl.ds(0, 2 - it)
        return remote(
            v_send.at[it, parts], v_recv.at[it, parts], tm_sem.at[1], tm_sem.at[4 + it], "tm", t_next
        )

    def ahead_copy(it):
        rows = pl.ds(0, ahead_rows[it])
        return remote(
            ahead_send.at[it, rows], ahead_recv.at[it, rows],
            ahead_sem.at[0], ahead_sem.at[1 + it], "region", peer[FAR],
        )

    def state_copy(count):
        slots = pl.ds(0, count)
        return remote(
            state_send.at[slots], state_recv.at[slots], ahead_sem.at[0], ahead_sem.at[3],
            "region", peer[FAR],
        )

    def sent(it):
        for side in (FAR, NEAR):
            @pl.when(has[side])
            def _():
                ref = part_send.at[it, side]
                pltpu.make_async_copy(ref, ref, ps_sem.at[side]).wait()
                if it == 1 or side == NEAR:
                    ref = fw_own.at[it, pl.ds(0, nch - early if side == FAR else nch)]
                    pltpu.make_async_copy(ref, ref, fs_sem.at[side]).wait()
        if it == 0:
            for parity in (0, 1):
                @pl.when(far_of[parity])
                def _():
                    ref = fw_own.at[0, pl.ds(0, nch - parity * known)]
                    pltpu.make_async_copy(ref, ref, fs_sem.at[FAR]).wait()

    at_near, at_own, at_gens = lines, 2 * lines, 3 * lines

    def build(group):
        n = n_gens if group == 3 else lb
        for i in range(n):
            window = 3 * lb + i if group == 3 else first_window[group] + i
            lo = group * lines + i * blk
            for b in range(bb):
                a_v[b * blk : (b + 1) * blk, lo : lo + blk] = tiles_v[table_s[0, b * width + window]]

    per_dot = 2 if nch % 2 == 0 else 1

    def far_sums(it, ch):
        sums = jnp.dot(
            pt_v[...], a_v[:, ch * cw : (ch + per_dot) * cw], preferred_element_type=f32
        )
        for i in range(per_dot):
            part_send[it, FAR, ch + i] = sums[:, i * cw : (i + 1) * cw]

    def send_far(it, ch):
        @pl.when(has[FAR])
        def _():
            for i in range(per_dot):
                far_part(it, ch + i).start()

    def pull_near(it):
        for ch in range(0, nch, per_dot):
            at = at_near + ch * cw
            sums = jnp.dot(
                pt_v[...], a_v[:, at : at + per_dot * cw], preferred_element_type=f32
            )
            for i in range(per_dot):
                part_send[it, NEAR, ch + i] = sums[:, i * cw : (i + 1) * cw]

        @pl.when(has[NEAR])
        def _():
            near_part(it).start()

    def pull_gens():
        own_v[:, lines:] = jnp.dot(pt_v[...], a_v[:, at_gens:], preferred_element_type=f32)

    def pull_own():
        own_v[:, :lines] = jnp.dot(
            pt_v[...], a_v[:, at_own:at_gens], preferred_element_type=f32
        )

    def set_pt(ref):
        for b in range(bb):
            pt_v[:, b * blk : (b + 1) * blk] = ref[b * blk : (b + 1) * blk, :].astype(bf16).T

    def row(ref, n):
        return jnp.concatenate([ref[i : i + 1, :] for i in range(n)], axis=1) if n > 1 else ref[...]

    def gen_pull(it):
        grad = row(caps_v.at[0], n_gens) - own_v[:, lines:] + dual_s[it]
        own_v[:, lines:] = grad
        v_send[it, 0] = grad[cols - scen :]
        if it == 0:
            v_send[it, 1] = gen_s[it][cols - scen :]
        prev_copy(it).start()

    def clipped(now, sp, grad):
        return jnp.minimum(jnp.maximum(now - sp * grad, 0.0), row(caps_v.at[1], n_gens))

    def gen_step(it, sp):
        dual_copy(it).wait_recv()
        nxt = d_recv[it]
        later = nxt if cols == scen else jnp.concatenate([dual_s[it][scen:], nxt], axis=0)
        gnow = gen_s[it]
        gnew = clipped(gnow, sp, own_v[:, lines:] - later)
        gbar = 2.0 * gnew - gnow
        gen_s[it + 1] = gnew
        genlow_v[...] = gbar.astype(bf16)
        return (gnew - gnow) ** 2, gbar

    def prev_bar(it, sp):
        now = v_recv[it, 1] if it == 0 else prev_v[...]
        new = clipped(now, sp, v_recv[it, 0] - dual_s[it][:scen])
        prev_v[...] = new
        return 2.0 * new - now

    def near_arrived(it):
        @pl.when(has[NEAR])
        def _():
            near_part(it).wait_recv()

    def total_at(it, ch):
        @pl.when(has[FAR])
        def _():
            far_part(it, ch).wait_recv()

        lo = ch * cw
        return own_v[:, lo : lo + cw] + part_recv[it, NEAR, ch] + part_recv[it, FAR, ch]

    per = cw // blk

    def caps_of(ch):
        return jnp.concatenate(
            [fcap_v[ch * per + i : ch * per + i + 1, :] for i in range(per)], axis=1
        )

    def stepped(now, sp, total, cap):
        return jnp.minimum(jnp.maximum(now + sp * total, -cap), cap)

    def flow_step(it, ch, sp, total):
        lo = ch * cw
        now = flow_s[it, :, lo : lo + cw]
        new = stepped(now, sp, total, caps_of(ch))
        fw_own[it, ch] = (2.0 * new - now).astype(bf16)

        if ch < nch - (known, early)[it] or it == 0:
            @pl.when(has[FAR] if ch < nch - (known, early)[it] else far_of[0])
            def _():
                far_flow(it, ch).start()

        flow_s[it + 1, :, lo : lo + cw] = new
        return (new - now) ** 2

    def put_state(ref, it, ch):
        ref[:cols] = flow_s[it, :, ch * cw : (ch + 1) * cw]
        ref[cols:] = jnp.broadcast_to(caps_of(ch), (8, cw))

    def ahead_start(it):
        count = (known, early)[it]
        for s in range(count):
            lo = (nch - count + s) * cw
            ahead_send[it, s * cols : (s + 1) * cols] = (
                own_v[:, lo : lo + cw] + part_recv[it, NEAR, nch - count + s]
            )
        if it == 0:
            put_state(ahead_send.at[0, pl.ds(cols, cols + 8)], 0, nch - 1)

            @pl.when(far_of[1])
            def _():
                ahead_copy(0).start()
        else:
            for parity in (0, 1):
                @pl.when(far_of[parity])
                def _():
                    slots = early - parity * known
                    (state_copy(slots) if slots else ahead_copy(0)).wait_send()
                    ahead_copy(1).start()

    def state_start():
        for s in range(early):
            put_state(state_send.at[s], 1, nch - early + s)
        for parity in (0, 1):
            slots = early - parity * known
            if slots:
                @pl.when(far_of[parity])
                def _():
                    if parity == 1:
                        ahead_copy(0).wait_send()
                    state_copy(slots).start()

    def ahead_low(it, sp, ch):
        count = (known, early)[it]
        s = ch - (nch - count)
        total = ahead_recv[it, s * cols : (s + 1) * cols] + part_send[it, FAR, ch]
        if it == 0:
            now, cap = ahead_recv[0, cols : 2 * cols], ahead_recv[0, 2 * cols : 2 * cols + 1]
        else:
            now, cap = state_recv[s, :cols], state_recv[s, cols : cols + 1]
        new = stepped(now, sp, total, cap)
        if it == 0:
            state_recv[early - 1, :cols] = new
            state_recv[early - 1, cols:] = ahead_recv[0, 2 * cols :  2 * cols + 8]
        return (2.0 * new - now).astype(bf16)

    def send_near(it):
        @pl.when(has[NEAR])
        def _():
            near_flow(it).start()

    nt_dims = (((1,), (1,)), ((), ()))
    push_rows = buses // 2 if bb % 2 == 0 else buses

    def joined(get, n):
        return jnp.concatenate([get(ch) for ch in range(n)], axis=1) if n > 1 else get(0)

    rows_at = [pl.ds(at, push_rows) for at in range(0, buses, push_rows)]

    def add_up(lines_of, low, use):
        for rows in rows_at:
            wide = [a_v[rows, at] for at in lines_of]
            use(
                rows,
                lax.dot_general(
                    jnp.concatenate(wide, axis=1) if len(wide) > 1 else wide[0], low, nt_dims,
                    preferred_element_type=f32,
                ),
            )

    def keep(rows, sums):
        acc_v[rows] = sums

    def accumulate(rows, sums):
        acc_v[rows] += sums

    def push_own(it):
        mine = jnp.concatenate([fw_own[it, ch] for ch in range(nch)] + [genlow_v[...]], axis=1)
        add_up([pl.ds(at_own, lines + gens)], mine, keep)

    def push_near(it):
        @pl.when(has[NEAR])
        def _():
            near_flow(it).wait_recv()

        other = joined(lambda ch: fw_in[it, NEAR, ch], nch)
        add_up([pl.ds(at_near, lines)], other, accumulate)

    def push_far(it, sp, chunks, ahead, use):
        lows = []
        for ch in chunks:
            if ch in ahead:
                lows.append(ahead_low(it, sp, ch))
            else:
                far_flow(it, ch).wait_recv()
                lows.append(fw_in[it, FAR, ch])
        add_up(
            [pl.ds(ch * cw, cw) for ch in chunks],
            jnp.concatenate(lows, axis=1) if len(lows) > 1 else lows[0], use,
        )

    def push(it, sp, meanwhile, settle, finish, done):
        if it == 0 and early > 0:
            state_start()
        push_own(it)
        if it == 1:
            meanwhile()
        plans = []
        for parity in (0, 1):
            n = early if it == 1 else known * (1 - parity)
            more = max(nch // 2 - n, 0)
            plans.append(
                ([*range(nch - n, nch)], [*range(nch - n, nch), *range(more)], [*range(more, nch - n)])
            )

        def far_first(parity):
            ahead, first, _ = plans[parity]
            if first:
                @pl.when(far_of[parity])
                def _():
                    if ahead:
                        ahead_copy(it).wait_recv()
                    if it == 1 and early - (1 - parity) * known:
                        state_copy(early - (1 - parity) * known).wait_recv()
                    push_far(it, sp, first, ahead, accumulate)

        far_first(0)
        if it == 1:
            far_first(1)
        push_near(it)
        if it == 0:
            far_first(1)
            meanwhile()
        settle()

        for parity in (0, 1):
            @pl.when(far_of[parity])
            def _():
                ahead, _, last = plans[parity]
                push_far(it, sp, last, ahead, finish)
                done()

        @pl.when(jnp.logical_not(has[FAR]))
        def _():
            for rows in rows_at:
                finish(rows, None)
            done()

    def ramp_step(it, gbar, prev, sd):
        earlier = prev if cols == scen else jnp.concatenate([prev, gbar[: cols - scen]], axis=0)
        dual = dual_s[it]
        lifted = dual + sd * (gbar - earlier)
        bound = row(caps_v.at[2], n_gens)
        return lifted - sd * jnp.minimum(jnp.maximum(lifted / sd, -bound), bound)

    zero_at = n_tiles + n_gens
    arrived(0, idx_v)
    slot = idx_v[0] * width + (idx_v[1] - (r - 1) * lb)
    down = lax.broadcasted_iota(jnp.int32, (n_tiles, n_tiles), 0)
    across = lax.broadcasted_iota(jnp.int32, (n_tiles, n_tiles), 1)
    upright = jnp.sum(jnp.where(down == across, slot, 0), axis=1, keepdims=True)
    places = lax.broadcasted_iota(jnp.int32, (n_tiles, 128), 1)
    ids = lax.broadcasted_iota(jnp.int32, (n_tiles, 128), 0)
    found = jnp.sum(jnp.where(upright == places, ids - zero_at, 0), axis=0, keepdims=True)
    lane = lax.broadcasted_iota(jnp.int32, (1, 128), 1)
    for g in range(n_gens):
        found = jnp.where(lane == gen_bus[g] * width + 3 * lb + g, n_tiles + g - zero_at, found)
    table_v[...] = jnp.clip(zero_at + found, 0, zero_at)
    to_scalar = pltpu.make_async_copy(table_v, table_s, in_sem.at[0])
    to_scalar.start()

    w1 = jnp.full((1, 1), weight[...], f32)
    arrived(1, first_v)
    set_pt(price_v)
    dual_s[0] = ramp_v[...].T
    d_send[0] = dual_s[0][:scen]
    arrived(2, all_tiles)
    to_scalar.wait()
    build(FAR)
    pl.semaphore_wait(barrier, nt - 1 + count[FAR] + count[NEAR])
    if n_stages > 0:
        stage_signal(0)
    dual_copy(0).start()
    for ch in range(0, nch, per_dot):
        far_sums(0, ch)
        send_far(0, ch)
    late_loads()
    build(NEAR)
    pull_near(0)
    build(3)
    pull_gens()
    arrived(0, late_v)
    arrived(1, caps_v)
    gen_s[0] = gen_v[...].T
    gen_pull(0)
    pass_on(0)
    build(2)
    pull_own()
    sd1 = step_scale * w1
    sp1 = step_scale / w1
    for b in range(lb):
        flow_s[0, :, b * blk : (b + 1) * blk] = flow_v[b * blk : (b + 1) * blk, :].T
    arrived(2, fcap_v)
    near_arrived(0)
    if early > 0:
        ahead_start(0)
    primal_acc = jnp.zeros((8, 128), f32)
    for ch in range(nch):
        primal_acc = primal_acc + fold(flow_step(0, ch, sp1, total_at(0, ch)))
        if ch == 0:
            pass_on(1)
    send_near(0)
    for stage in range(2, n_stages - 1):
        pass_on(stage)
    changed, gbar1 = gen_step(0, sp1)
    primal_acc = primal_acc + fold(changed)
    low = lax.broadcasted_iota(jnp.int32, (1, 128), 1) < 64
    primal_row = both_halves(primal_acc)

    def ramp_now():
        prev_copy(0).wait_recv()
        dual_one = ramp_step(0, gbar1, prev_bar(0, sp1), sd1)
        dual_s[1] = dual_one
        change_v[...] = fold((dual_one - dual_s[0]) ** 2)
        dual_copy(0).wait_send()
        d_send[1] = dual_one[:scen]
        dual_copy(1).start()

    def price_now(rows, pushed):
        old = price_v[rows]
        new = old + sd1 * (demand_v[rows] - (acc_v[rows] if pushed is None else acc_v[rows] + pushed))
        price1_v[rows] = new
        change_v[...] += fold((new - old) ** 2)

    def rows_ready():
        ar_s[...] = jnp.where(low, primal_row, both_halves(change_v[...]))

    push(0, sp1, ramp_now, lambda: None, price_now, rows_ready)

    if n_stages > 0:
        stage_wait(n_stages - 1)
    others_t = partners(t, nt) + [(0, t)]
    others_r = partners(r, nr) + [(0, r)]
    for k, to_r in others_r:
        for j, to_t in others_t:
            if j or k:
                pltpu.make_async_remote_copy(
                    src_ref=ar_s,
                    dst_ref=ar_r.at[j * nr + k],
                    send_sem=ar_sem.at[0],
                    recv_sem=ar_sem.at[1],
                    device_id={"tm": to_t, "region": to_r},
                    device_id_type=MESH,
                ).start()
    others = ar_r.at[pl.ds(1, nt * nr - 1)]
    sent(0)
    set_pt(price1_v)
    for ch in range(0, nch, per_dot):
        far_sums(1, ch)
        send_far(1, ch)
    pull_near(1)
    pull_gens()
    prev_copy(0).wait_send()
    gen_pull(1)
    pull_own()
    near_arrived(1)
    if early > 0:
        ahead_start(1)
    pltpu.make_async_copy(others, others, ar_sem.at[1]).wait()
    parts = [ar_s[...]] + [ar_r[at] for at in range(1, nt * nr)]
    while len(parts) > 1:
        parts = [a + b for a, b in zip(parts[::2], parts[1::2])] + parts[len(parts) // 2 * 2 :]
    summed = parts[0]
    primal_mean = jnp.sum(jnp.where(low, summed, 0.0), axis=1, keepdims=True) / count_p
    dual_mean = jnp.sum(jnp.where(low, 0.0, summed), axis=1, keepdims=True) / count_d
    w2 = jnp.sqrt(w1 * jnp.sqrt((dual_mean + tiny) / (primal_mean + tiny)))

    sd2 = step_scale * w2
    sp2 = step_scale / w2
    for ch in range(nch):
        flow_step(1, ch, sp2, total_at(1, ch))
    send_near(1)
    _, gbar2 = gen_step(1, sp2)

    def results():
        prev_copy(1).wait_recv()
        o_ramp[...] = ramp_step(1, gbar2, prev_bar(1, sp2), sd2).T
        for b in range(lb):
            o_flow[b * blk : (b + 1) * blk, :] = flow_s[2, :, b * blk : (b + 1) * blk].T
        o_gen[...] = gen_s[2].T

    def price_but_last():
        acc_v[...] = price1_v[...] + sd2 * (demand_v[...] - acc_v[...])

    def price_out(rows, pushed):
        o_price[rows] = acc_v[rows] if pushed is None else acc_v[rows] - sd2 * pushed

    push(1, sp2, results, price_but_last, price_out, lambda: None)

    dual_copy(1).wait_send()
    prev_copy(1).wait_send()
    sent(1)
    if early > 0:
        @pl.when(has[FAR])
        def _():
            ahead_copy(1).wait_send()

    pltpu.make_async_copy(others, others, ar_sem.at[0]).wait()


def shards(
    gen, flow, price, ramp_dual, demand, incid_tiles, tile_bus, tile_line, gen_tiles, gen_bus,
    gen_cost, gen_cap, ramp_cap, flow_cap, weight,
):
    gb, blk, hours, scen = gen.shape
    lb, bb = flow.shape[0], price.shape[0]
    n_tiles = incid_tiles.shape[0]
    cols = hours * scen
    nt, nr = lax.axis_size("tm"), lax.axis_size("region")
    lines, buses, gens = lb * blk, bb * blk, gb * blk
    width = 3 * lb + gb
    nch = lb
    early = nch // 2
    ahead_rows = max(2 * cols + 8, early * cols)
    cw = lines // nch
    n_stages, reach = 0, 0
    while reach < nr - 1:
        reach += 2**n_stages
        n_stages += 1

    dims = (
        nt, nr, scen,
        float((gen.size + flow.size) * nt * nr), float((price.size + ramp_dual.size) * nt * nr), early,
    )
    any_spec = pl.BlockSpec(memory_space=pl.ANY)
    smem_spec = pl.BlockSpec(memory_space=pltpu.SMEM)
    dma = pltpu.SemaphoreType.DMA
    V = pltpu.VMEM
    scratch = [
        V((n_tiles + gb + 1, blk, blk), bf16),
        V((buses, width * blk), bf16),
        V((buses + gens, cols), f32),
        V((lines + buses + gens, cols), f32),
        V((3, gb, blk), f32),
        V((lb, blk), f32),
        V((cols, buses), bf16),
        V((cols, lines + gens), f32),
        V((buses, cols), f32),
        V((3, cols, lines), f32),
        V((3, cols, gens), f32),
        V((2, cols, gens), f32),
        V((cols, gens), bf16),
        V((2, 2, nch, cols, cw), f32),
        V((2, 2, nch, cols, cw), f32),
        V((2, nch, cols, cw), bf16),
        V((2, 2, nch, cols, cw), bf16),
        V((2, scen, gens), f32),
        V((2, scen, gens), f32),
        V((2, 2, scen, gens), f32),
        V((2, 2, scen, gens), f32),
        V((scen, gens), f32),
        V((2, ahead_rows, cw), f32),
        V((2, ahead_rows, cw), f32),
        V((max(early, 1), cols + 8, cw), f32),
        V((max(early, 1), cols + 8, cw), f32),
        V((1, 128), f32),
        V((nt * nr, 1, 128), f32),
        V((buses, cols), f32),
        V((8, 128), f32),
        V((2, 1, n_tiles), jnp.int32),
        V((1, 128), jnp.int32),
        pltpu.SMEM((1, 128), jnp.int32),
        dma((3,)),
        dma((2,)),
        dma((nch + 2,)),
        dma((2,)),
        dma((nch + 1,)),
        dma((6,)),
        dma((2,)),
        dma((4,)),
        pltpu.SemaphoreType.REGULAR((n_stages,)),
    ]
    vmem_spec = pl.BlockSpec(memory_space=pltpu.VMEM)
    shapes = ((gens, cols), (lines, cols), (buses, cols), (gens, cols))
    outs = pl.pallas_call(
        functools.partial(kernel, dims),
        out_shape=tuple(V(shape, f32) for shape in shapes),
        in_specs=[smem_spec, smem_spec] + [any_spec] * 13,
        out_specs=(vmem_spec,) * 4,
        scratch_shapes=scratch,
        compiler_params=pltpu.CompilerParams(collective_id=0, has_side_effects=True),
    )(
        gen_bus, weight, tile_bus.reshape(1, n_tiles), tile_line.reshape(1, n_tiles), incid_tiles, gen_tiles,
        price.reshape(buses, cols), flow.reshape(lines, cols), gen.reshape(gens, cols),
        ramp_dual.reshape(gens, cols), demand.reshape(buses, cols),
        gen_cost, gen_cap, ramp_cap, flow_cap,
    )
    outs = pl.pallas_call(
        writer,
        out_shape=tuple(jax.ShapeDtypeStruct(shape, f32) for shape in shapes),
        in_specs=[any_spec] * 4,
        out_specs=(any_spec,) * 4,
        scratch_shapes=[dma((4,))],
    )(*(pltpu.with_memory_space_constraint(out, pltpu.VMEM) for out in outs))
    return tuple(
        out.reshape(like.shape) for out, like in zip(outs, (gen, flow, price, ramp_dual))
    )


def solution(mesh):
    field = P("region", None, "tm", None)
    placed = (
        field, field, field, field, field,
        P("region", None, None), P("region"), P("region"), P("region", None, None), P("region"),
        P("region", None), P("region", None), P("region", None), P("region", None), P(),
    )
    return jax.shard_map(
        shards, mesh=mesh, in_specs=placed, out_specs=(field,) * 4, check_vma=False
    )
```
